32 devices in a mesh: kpt: 1, ga: 32 (over z, y, x, core).
Axes of the slice: x: 2, y: 2, z: 4, core: 2. Of those that a mesh axis runs over, the one named last changes fastest.
Arguments:
- orbitals: float32 [2, 1024, 131072], P(None, 'kpt', 'ga'), may hold values from -6 to 6
- coeff_cells: int32 [131072], P('ga'), may hold values from -1 to 2097151, as said below
- potential: float32 [128, 128, 128], P('ga'), may hold values from -6 to 6
Outputs:
- applied: float32 [2, 1, 131072], P(None, 'kpt', 'ga')
- subspace: float32 [1024, 2, 1], P('ga', None, 'kpt')
The draws below stay inside these ranges and needn't reach their ends.
Inputs may be any that keep to these rules, and one draw needn't show every extreme that they name: `coeff_cells`: each block of 4096 entries (one device's) lists whole columns of cells (cells with the same first two coordinates) one after another, each column's cells in rising third coordinate, and then -1 in its remaining slots. The cells listed over all blocks are exactly the cells with f(a)^2 + f(b)^2 + f(c)^2 <= 30^2, each once. The numbers of columns of two blocks differ by one at most.
All inputs are finite; a program needn't handle non-finite values.
Results may differ from the reference program's by a relative error of at most 0.0003.
Values sent between devices are 32-bit elements; how exact they have to be, the bound alone decides.
No kernel may reach another device: no remote copies, remote signals or barrier semaphores. Data moves between devices by JAX's collectives and lax.ppermute only.
A program may use at most 128 MiB of HBM per device.

```python
import math
import jax
import jax.numpy as jnp
from jax import lax

NGRID = 128
RADIUS = 30
NG = 131072
NB_ALL = 1024
BANDS = 1
NG_DEV = 4096
N_GA = 32


def draw_coeff_cells(key, part):
    extent = NGRID
    device_count = N_GA
    columns_all = extent * extent
    indices = jnp.arange(extent, dtype=jnp.int32)
    frequency = jnp.where(indices < extent // 2, indices, indices - extent)
    square = frequency * frequency
    column_square = (square[:, None] + square[None, :]).reshape(columns_all)
    inside = square[None, :] <= (RADIUS * RADIUS - column_square)[:, None]
    inside_count = inside.astype(jnp.int32)
    lengths = jnp.sum(inside_count, axis=1)
    shuffle = jax.random.permutation(key, columns_all).astype(jnp.int32)
    scores = lengths * columns_all + shuffle
    ordering = jnp.argsort(-scores).astype(jnp.int32)
    rank_of = jnp.zeros((columns_all,), jnp.int32).at[ordering].set(jnp.arange(columns_all, dtype=jnp.int32))
    rounds = rank_of // device_count
    position = rank_of % device_count
    owners = jnp.where(rounds % 2 == 0, position, device_count - 1 - position)
    sorted_lengths = lengths[ordering]
    sorted_owner = owners[ordering]
    owner_ids = jnp.arange(device_count, dtype=jnp.int32)
    owner_hits = (sorted_owner[:, None] == owner_ids[None, :]).astype(jnp.int32)
    weighted = owner_hits * sorted_lengths[:, None]
    running = jnp.cumsum(weighted, axis=0) - weighted
    sorted_start = jnp.sum(running * owner_hits, axis=1)
    column_start = jnp.zeros((columns_all,), jnp.int32).at[ordering].set(sorted_start)
    within = jnp.cumsum(inside_count, axis=1) - inside_count
    slot_of = owners[:, None] * NG_DEV + column_start[:, None] + within
    slot_of = jnp.where(inside, slot_of, NG)
    cell_ids = jnp.arange(extent ** 3, dtype=jnp.int32).reshape(columns_all, extent)
    filled = jnp.full((NG + 1,), -1, jnp.int32).at[slot_of.reshape(-1)].set(cell_ids.reshape(-1))
    return filled[:NG]


def raised(values, rng, source, target, shards_of, factor):
    def block_of(dim):
        return (jnp.arange(values.shape[dim]) // (values.shape[dim] // shards_of)).reshape((-1,) + (1,) * (values.ndim - 1 - dim))

    near = jax.random.permutation(rng, shards_of)[block_of(target)]
    other_side = (block_of(target) + shards_of // 2) % shards_of
    return jnp.where((block_of(source) == near) | (block_of(source) == other_side), factor * values, values)


def steps_of(stream_key, dims, shards, least, top_value):
    def one(dim, blocks):
        steps = jax.random.uniform(jax.random.fold_in(jax.random.fold_in(stream_key, 6), dim), (blocks,), jnp.float32, least / len(shards), top_value / len(shards))
        return jnp.repeat(jnp.exp(steps), dims[dim] // blocks).reshape((-1,) + (1,) * (len(dims) - dim - 1))

    level = one(*shards[0])
    for cut in shards[1:]:
        level = level * one(*cut)
    return level


def normal_values(rng, shape, scale, reach, split=(), kind=jnp.bfloat16):
    factor_of = steps_of(rng, shape, split, -0.22, 0.18) if split else 1.0
    array = jax.random.normal(rng, shape, jnp.float32) * scale * factor_of
    return jnp.minimum(jnp.maximum(array, -reach), reach).astype(kind)


def heavy_noise(own_key, shape, scale, most, shards, heavy, kind=jnp.bfloat16):
    result = scale * jax.random.normal(own_key, shape, jnp.float32)
    if shards:
        result = result * steps_of(own_key, shape, shards, -0.22, 0.18)
    return jnp.clip(raised(result, jax.random.fold_in(own_key, 3), *heavy), -most, most).astype(kind)


def setup_inputs(seed: int = 0, part: int = 0) -> dict:
    key_of = jax.random.split(jax.random.key(seed), 4)
    own_keys = jax.random.split(jax.random.fold_in(key_of[3], part), 4)
    orbitals = heavy_noise(own_keys[0], (2, NB_ALL, NG), 1.0, 6.0, ((2, 32),), (2, 1, 32, 2.75), jnp.float32)
    coeff_cells = draw_coeff_cells(jax.random.fold_in(key_of[3], 71), part)
    potential = normal_values(key_of[2], (NGRID, NGRID, NGRID), 1.0, 6.0, ((0, 32),), jnp.float32)
    return dict(orbitals=orbitals, coeff_cells=coeff_cells, potential=potential)


def signed_frequency(values):
    return jnp.where(values < NGRID // 2, values, values - NGRID)

def kinetic_of(grid_cells):
    plane_a = grid_cells // (NGRID * NGRID)
    plane_b = grid_cells // NGRID % NGRID
    plane_c = grid_cells % NGRID
    total = signed_frequency(plane_a) ** 2 + signed_frequency(plane_b) ** 2 + signed_frequency(plane_c) ** 2
    return total.astype(jnp.float32) / (RADIUS * RADIUS)

def reference(orbitals, coeff_cells, potential):
    volume = NGRID ** 3
    is_live = coeff_cells >= 0
    live_mask = is_live.astype(jnp.float32)
    target = jnp.where(is_live, coeff_cells, volume).astype(jnp.int32)
    kinetic = kinetic_of(jnp.where(is_live, coeff_cells, 0).astype(jnp.int32)) * live_mask
    real_part = orbitals[0, :BANDS]
    imag_part = orbitals[1, :BANDS]
    norm_root = math.sqrt(NG)

    def one_band(values):
        coeffs = lax.complex(values[0], values[1])
        spread = jnp.zeros((volume + 1,), coeffs.dtype).at[target].set(coeffs)[:volume]
        spread = spread.reshape(NGRID, NGRID, NGRID)
        real_space = jnp.fft.ifftn(spread) * (volume / norm_root)
        products = jnp.fft.fftn(potential * real_space) * (norm_root / volume)
        extended = jnp.concatenate([products.reshape(volume), jnp.zeros((1,), products.dtype)])
        picked = extended[target]
        return (jnp.real(picked), jnp.imag(picked))
    field_real, field_imag = lax.map(one_band, (real_part, imag_part))
    applied_real = kinetic * real_part + field_real
    applied_imag = kinetic * imag_part + field_imag
    applied = jnp.stack([applied_real, applied_imag])
    numbers = (((1,), (1,)), ((), ()))
    highest = lax.Precision.HIGHEST
    tile_real = lax.dot_general(orbitals[0], applied_real, numbers, precision=highest) + lax.dot_general(orbitals[1], applied_imag, numbers, precision=highest)
    tile_imag = lax.dot_general(orbitals[0], applied_imag, numbers, precision=highest) - lax.dot_general(orbitals[1], applied_real, numbers, precision=highest)
    subspace = jnp.stack([tile_real, tile_imag], axis=1) / NG
    return (applied, subspace)
```

```python
import math

import jax
import jax.numpy as jnp
import numpy as np
from jax import lax
from jax.experimental import pallas as pl
from jax.experimental.pallas import tpu as pltpu
from jax.sharding import PartitionSpec as P

RADIUS = 30
LANES = 128
SUB = 8
HALF = 32
KROWS = 32
F32 = jnp.float32
BF16 = jnp.bfloat16
I32 = jnp.int32

NT = ((1,), (1,))
NN = ((1,), (0,))


def column_total(extent):
    indices = np.arange(extent)
    frequency = np.where(indices < extent // 2, indices, indices - extent)
    return int(np.sum(frequency[:, None] ** 2 + frequency[None, :] ** 2 <= RADIUS * RADIUS))


class Sizes:
    def __init__(self, devices, extent, slots, bands_all):
        self.devices = devices
        self.extent = extent
        self.layers = extent // devices
        self.channels = 2 * self.layers
        self.slot_rows = slots // LANES
        self.slots = slots
        self.sticks = -(-column_total(extent) // devices)
        self.spare = LANES - self.sticks
        self.id_rows = -(-self.sticks // self.spare)
        used = self.channels + self.layers * self.layers
        self.rows = -(-used // SUB) * SUB
        self.bands_all = bands_all
        self.band_rows = bands_all // devices
        assert extent == LANES and self.channels <= SUB
        assert self.id_rows <= self.channels


def parts_of(matrix):
    values = np.asarray(matrix, np.float32)
    high = values.astype(jnp.bfloat16)
    low = (values - high.astype(np.float32)).astype(jnp.bfloat16)
    return np.stack([high, low])


def angle(x, y, extent):
    phase = (x[:, None] * y[None, :]) % extent
    return 2.0 * math.pi * phase.astype(np.float64) / extent


def tables(sz):
    n, d, layers = sz.extent, sz.devices, sz.layers
    cells = np.arange(n)
    dev, part, lay = np.meshgrid(np.arange(d), np.arange(2), np.arange(layers), indexing="ij")
    z_rows = (dev * layers + lay).reshape(-1)
    part_rows = part.reshape(-1)
    t = angle(z_rows, cells, n)
    re, im = np.cos(t), np.sin(t)
    is_im = part_rows[:, None] == 1
    forward_z = np.concatenate([np.where(is_im, im, re), np.where(is_im, re, -im)], 1)
    freq = np.arange(2 * HALF) - HALF
    tb = angle(freq, cells, n)
    cb, sb = np.cos(tb), np.sin(tb)
    eye = np.eye(2)
    cc, ss = np.kron(eye, cb), np.kron(eye, sb)
    forward_b = np.block([[cc, ss], [-ss, cc]])
    cct, sst = cc.T, ss.T
    inverse_b = np.block([[cct, -sst], [sst, cct]])
    a_rows = (np.arange(d)[None, :] * layers + np.arange(layers)[:, None]).reshape(-1)
    lo, k = np.meshgrid(np.arange(2), np.arange(KROWS), indexing="ij")
    a_freq = (2 * k + lo - HALF).reshape(-1)
    ta = angle(a_rows, a_freq, n)
    ca, sa = np.cos(ta), np.sin(ta)
    forward_a = np.block([[ca, -sa], [sa, ca]])
    inverse_a = np.block([[ca.T, sa.T], [-sa.T, ca.T]])
    part2, lay2, dev2 = np.meshgrid(np.arange(2), np.arange(layers), np.arange(d), indexing="ij")
    t2 = angle((dev2 * layers + lay2).reshape(-1), cells, n)
    re2, im2 = np.cos(t2) / n**3, np.sin(t2) / n**3
    im_rows = part2.reshape(-1)[:, None] == 1
    inverse_z = np.concatenate([np.where(im_rows, im2, re2), np.where(im_rows, re2, -im2)], 1)
    return {
        "forward_z": parts_of(forward_z),
        "forward_b": parts_of(forward_b),
        "forward_a": parts_of(forward_a),
        "inverse_a": parts_of(inverse_a),
        "inverse_b": parts_of(inverse_b),
        "inverse_z": parts_of(inverse_z),
    }


def split(x):
    high = x.astype(BF16)
    return high, (x - high.astype(F32)).astype(BF16)


def dot(a, b, dims=NN):
    return lax.dot_general(a, b, (dims, ((), ())), preferred_element_type=F32)


def dot3(a, b, dims=NN):
    return dot(a[0], b[0], dims) + dot(a[0], b[1], dims) + dot(a[1], b[0], dims)


def iota(shape, dim):
    return lax.broadcasted_iota(I32, shape, dim)


def ones_where(mask):
    return jnp.where(mask, 1.0, 0.0).astype(F32)


def pick(values, lanes):
    return jnp.take_along_axis(values, lanes, axis=1, mode="promise_in_bounds")


def signed(x, extent):
    return jnp.where(x < extent // 2, x, x - extent)


def column_facts(meta, sz):
    shape = (LANES, LANES)
    col_a = jnp.broadcast_to(meta[:, 0:1], shape)
    col_b = jnp.broadcast_to(meta[:, 1:2], shape)
    row = jnp.broadcast_to(meta[:, 2:3], shape)
    lane = jnp.broadcast_to(meta[:, 3:4], shape)
    valid = jnp.broadcast_to(meta[:, 4:5], shape) > 0.5
    fa = jnp.where(col_a < sz.extent // 2, col_a, col_a - sz.extent)
    fb = jnp.where(col_b < sz.extent // 2, col_b, col_b - sz.extent)
    fc = signed(iota(shape, 1), sz.extent).astype(F32)
    inside = valid & (fc * fc <= RADIUS * RADIUS - fa * fa - fb * fb)
    return row, lane, inside


def spread_kernel(sz, cells_ref, orbitals_ref, potential_ref, table_ref,
                  send_ref, window_ref, meta_ref,
                  block, pot, table, turned, sems):
    loads = [
        pltpu.make_async_copy(orbitals_ref.at[:, pl.ds(0, SUB), :], block, sems.at[0]),
        pltpu.make_async_copy(table_ref, table, sems.at[1]),
        pltpu.make_async_copy(potential_ref, pot, sems.at[2]),
    ]
    for load in loads:
        load.start()
    rows = sz.slot_rows
    shape = (rows, LANES)
    cells = cells_ref[...]
    live = cells >= 0
    column = lax.shift_right_arithmetic(cells, int(math.log2(sz.extent)))
    rolled = pltpu.roll(column, 1, 1)
    above = pltpu.roll(rolled, 1, 0)
    lane = iota(shape, 1)
    row = iota(shape, 0)
    before = jnp.where(lane == 0, jnp.where(row == 0, -1, above), rolled)
    starts = live & (column != before)
    flags = ones_where(starts).astype(BF16)
    square = (LANES, LANES)
    upto = ones_where(iota(square, 0) <= iota(square, 1)).astype(BF16)
    all_ones = jnp.ones(square, BF16)
    within = dot(flags, upto)
    totals = dot(flags, all_ones)
    lower = ones_where(iota((rows, rows), 1) < iota((rows, rows), 0)).astype(BF16)
    rank = (within + dot(lower, totals.astype(BF16))).astype(I32) - 1
    rank = jnp.where(starts, rank, -1)
    col_a = lax.shift_right_arithmetic(column, int(math.log2(sz.extent)))
    col_b = column & (sz.extent - 1)
    sub = iota((SUB, LANES), 0)
    lane8 = iota((SUB, LANES), 1)
    place = iota(square, 0)
    hots, facts = [], []
    for r in range(rows):
        hots.append(ones_where(place == rank[r : r + 1, :]).astype(BF16))
        fact = jnp.where(sub == 0, col_a[r : r + 1, :], col_b[r : r + 1, :])
        fact = jnp.where(sub == 2, r, fact)
        fact = jnp.where(sub == 3, lane8, fact)
        fact = jnp.where(sub == 4, 1, fact)
        facts.append(fact.astype(F32).astype(BF16))
    meta_t = dot(jnp.concatenate(facts, 1), jnp.concatenate(hots, 1), NT)
    meta_ref[...] = meta_t
    meta = jnp.transpose(jnp.concatenate([meta_t, jnp.zeros((LANES - SUB, LANES), F32)], 0))
    first_row, first_lane, inside = column_facts(meta, sz)
    hot = ones_where(inside).astype(BF16)
    before_in = ones_where(iota(square, 0) < iota(square, 1)).astype(BF16)
    slot = (first_lane + dot(hot, before_in)).astype(I32)
    second = slot >= LANES
    slot_lane = slot & (LANES - 1)

    loads[0].wait()
    for r in range(rows):
        window_ref[r : r + 1, :] = block[0, 0:1, r * LANES : (r + 1) * LANES]
        window_ref[rows + r : rows + r + 1, :] = block[1, 0:1, r * LANES : (r + 1) * LANES]
    window = jnp.concatenate([window_ref[0:rows, :], window_ref[rows : 2 * rows, :]], 1)
    high, low = split(window)
    row_of = first_row.astype(I32)[:, 0:rows]
    which = iota((LANES, rows), 1)
    near = ones_where(which == row_of).astype(BF16)
    far = ones_where(which == row_of + 1).astype(BF16)
    near_w = dot(near, high) + dot(near, low)
    far_w = dot(far, high) + dot(far, low)
    sticks = []
    for part in range(2):
        cut = slice(part * LANES, (part + 1) * LANES)
        value = jnp.where(second, pick(far_w[:, cut], slot_lane), pick(near_w[:, cut], slot_lane))
        sticks.append(jnp.where(inside, value, 0.0))
    sticks = jnp.concatenate(sticks, 1)
    loads[1].wait()
    depth = dot3((table[0], table[1]), split(sticks), NT)

    ids = jnp.where(
        meta_t[4:5, :] > 0.5, meta_t[0:1, :] * sz.extent + meta_t[1:2, :], -1.0
    )
    ids = jnp.broadcast_to(ids, (SUB, LANES))
    carried = jnp.zeros((SUB, LANES), F32)
    for i in range(sz.id_rows):
        shifted = pltpu.roll(ids, (sz.sticks - i * sz.spare) % LANES, 1)
        carried = jnp.where(sub == i, shifted, carried)
    is_stick = lane8 < sz.sticks
    channels, layers, devices = sz.channels, sz.layers, sz.devices
    for d in range(devices):
        values = depth[d * channels : (d + 1) * channels, :]
        send_ref[d * sz.rows : d * sz.rows + channels, :] = jnp.where(
            is_stick[0:channels], values, carried[0:channels]
        )
    loads[2].wait()
    for al in range(layers):
        turned[...] = jnp.transpose(pot[al])
        for p in range(layers):
            at = channels + al * layers + p
            send_ref[pl.ds(at, devices, stride=sz.rows), :] = turned[
                pl.ds(p, devices, stride=layers), :
            ]
    for at in range(channels + layers * layers, sz.rows):
        send_ref[pl.ds(at, devices, stride=sz.rows), :] = jnp.zeros((devices, LANES), F32)


def plane_kernel(sz, recv_ref, fb_ref, fa_ref, ia_ref, ib_ref,
                 out_ref,
                 fb, fa, ia, ib, found, planes, back, at_k, at_lane, sems):
    copies = [
        pltpu.make_async_copy(src, dst, sems.at[i])
        for i, (src, dst) in enumerate([(fb_ref, fb), (fa_ref, fa), (ia_ref, ia), (ib_ref, ib)])
    ]
    for c in copies:
        c.start()
    devices, layers, channels = sz.devices, sz.layers, sz.channels
    lane = iota((devices, LANES), 1)
    ids = jnp.full((devices, LANES), -1.0, F32)
    for i in range(sz.id_rows):
        rows = recv_ref[pl.ds(i, devices, stride=sz.rows), :]
        shifted = pltpu.roll(rows, (i * sz.spare - sz.sticks) % LANES, 1)
        mine = (lane >= i * sz.spare) & (lane < min((i + 1) * sz.spare, sz.sticks))
        ids = jnp.where(mine, shifted, ids)
    ids = ids.astype(I32)
    col_a = lax.shift_right_arithmetic(ids, int(math.log2(sz.extent)))
    col_b = ids & (sz.extent - 1)
    sa = (col_a + HALF) & (sz.extent - 1)
    sb = (col_b + HALF) & (sz.extent - 1)
    kv = jnp.where(ids >= 0, lax.shift_right_arithmetic(sa, 1), -1)
    lv = (sa & 1) * (2 * HALF) + sb
    lv = jnp.where(ids >= 0, lv, 0)
    at_k[...] = kv
    at_lane[...] = lv
    ks = iota((KROWS, LANES), 0)
    cell = iota((LANES, LANES), 0)
    place = iota((KROWS, LANES), 1)
    left, right = [], []
    for e in range(devices):
        here = ks == kv[e : e + 1, :]
        left.append(
            jnp.concatenate([jnp.where(here, e + 1, 0), jnp.where(here, place, 0)], 0)
            .astype(F32)
            .astype(BF16)
        )
        right.append(ones_where(cell == lv[e : e + 1, :]).astype(BF16))
    found[...] = dot(jnp.concatenate(left, 1), jnp.concatenate(right, 1), NT).astype(I32)

    def to_planes(k, carry):
        owner = jnp.broadcast_to(found[pl.ds(k, 1), :], (SUB, LANES)) - 1
        source = jnp.broadcast_to(found[pl.ds(k + KROWS, 1), :], (SUB, LANES))
        value = jnp.zeros((SUB, LANES), F32)
        for e in range(devices):
            value = jnp.where(
                owner == e, pick(recv_ref[e * sz.rows : e * sz.rows + SUB, :], source), value
            )
        planes[pl.ds(pl.multiple_of(k * SUB, SUB), SUB), :] = value
        return carry

    lax.fori_loop(0, KROWS, to_planes, 0)

    def plane_part(part, p):
        return planes[pl.ds(part * layers + p, KROWS, stride=SUB), :]

    grid = jnp.concatenate(
        [
            jnp.concatenate([plane_part(part, p) for p in range(layers)], 0)
            for part in range(2)
        ],
        1,
    )
    copies[0].wait()
    grid = dot3(split(grid), (fb[0], fb[1]))
    grid = jnp.concatenate(
        [
            jnp.concatenate(
                [
                    grid[p * KROWS : (p + 1) * KROWS, q * LANES : (q + 1) * LANES]
                    for q in range(4)
                ],
                0,
            )
            for p in range(layers)
        ],
        1,
    )
    copies[1].wait()
    grid = dot3((fa[0], fa[1]), split(grid))
    potential = jnp.concatenate(
        [
            jnp.concatenate(
                [
                    recv_ref[pl.ds(channels + al * layers + p, devices, stride=sz.rows), :]
                    for al in range(layers)
                ],
                0,
            )
            for p in range(layers)
        ],
        1,
    )
    half = sz.extent
    field = jnp.concatenate([grid[0:half] * potential, grid[half:] * potential], 0)
    copies[2].wait()
    grid = dot3((ia[0], ia[1]), split(field))
    grid = jnp.concatenate(
        [
            jnp.concatenate(
                [
                    grid[q * KROWS : (q + 1) * KROWS, p * LANES : (p + 1) * LANES]
                    for q in range(4)
                ],
                1,
            )
            for p in range(layers)
        ],
        0,
    )
    copies[3].wait()
    grid = dot3(split(grid), (ib[0], ib[1]))
    for part in range(2):
        for p in range(layers):
            back[pl.ds(part * layers + p, KROWS, stride=SUB), :] = grid[
                p * KROWS : (p + 1) * KROWS, part * LANES : (part + 1) * LANES
            ]

    def to_columns(e, carry):
        k_row = jnp.broadcast_to(at_k[pl.ds(e, 1), :], (SUB, LANES))
        lanes = jnp.broadcast_to(at_lane[pl.ds(e, 1), :], (SUB, LANES))
        value = jnp.zeros((SUB, LANES), F32)
        for k in range(KROWS):
            value = jnp.where(k_row == k, pick(back[k * SUB : (k + 1) * SUB, :], lanes), value)
        out_ref[pl.ds(pl.multiple_of(e * SUB, SUB), SUB), :] = value
        return carry

    lax.fori_loop(0, devices, to_columns, 0)


def final_kernel(sz, chunk, back_ref, cells_ref, window_ref, meta_ref, table_ref, orbitals_ref,
                 applied_ref, tile_ref,
                 bands, acc, sems):
    chunks = sz.bands_all // chunk

    def load(i):
        return pltpu.make_async_copy(
            orbitals_ref.at[:, pl.ds(i * chunk, chunk), :],
            bands.at[:, pl.ds(i * chunk, chunk), :],
            sems.at[i],
        )

    for i in range(chunks):
        load(i).start()
    devices, layers, rows = sz.devices, sz.layers, sz.slot_rows
    square = (LANES, LANES)
    values = jnp.concatenate(
        [
            back_ref[pl.ds(part * layers + p, devices, stride=SUB), :]
            for part in range(2)
            for p in range(layers)
        ],
        0,
    )
    values = jnp.transpose(values)
    sticks = dot3(split(values), (table_ref[0], table_ref[1]))
    meta_t = meta_ref[...]
    meta = jnp.transpose(jnp.concatenate([meta_t, jnp.zeros((LANES - SUB, LANES), F32)], 0))
    first_row, first_lane, inside = column_facts(meta, sz)
    length = dot(ones_where(inside).astype(BF16), jnp.ones(square, BF16)).astype(I32)
    shift = iota(square, 1) - first_lane.astype(I32)
    top = lax.shift_right_arithmetic(length - 1, 1)
    placed = []
    for turn in range(2):
        p = shift + turn * LANES
        held = (p >= 0) & (p < length)
        depth = jnp.where(p <= top, p, p + sz.extent - length) & (sz.extent - 1)
        placed.append(
            jnp.concatenate(
                [
                    jnp.where(held, pick(sticks[:, q * LANES : (q + 1) * LANES], depth), 0.0)
                    for q in range(2)
                ],
                1,
            )
        )
    placed = split(jnp.concatenate(placed, 0))
    row_t = jnp.broadcast_to(meta_t[2:3, :].astype(I32), (rows, LANES))
    which = iota((rows, LANES), 0)
    hot = jnp.concatenate(
        [ones_where(which == row_t), ones_where(which == row_t + 1)], 1
    ).astype(BF16)
    local = dot(hot, placed[0]) + dot(hot, placed[1])
    cells = cells_ref[...]
    live = cells >= 0
    bits = int(math.log2(sz.extent))
    mask = sz.extent - 1
    fa = signed(lax.shift_right_arithmetic(cells, 2 * bits) & mask, sz.extent)
    fb = signed(lax.shift_right_arithmetic(cells, bits) & mask, sz.extent)
    fc = signed(cells & mask, sz.extent)
    kinetic = (fa * fa + fb * fb + fc * fc).astype(F32) / (RADIUS * RADIUS)
    for part in range(2):
        own = window_ref[part * rows : (part + 1) * rows, :]
        full = kinetic * own + local[:, part * LANES : (part + 1) * LANES]
        applied_ref[part * rows : (part + 1) * rows, :] = jnp.where(live, full, 0.0)

    step_rows = min(64, chunk)
    steps = chunk // step_rows

    def product(i, carry):
        @pl.when(i % steps == 0)
        def _():
            load(i // steps).wait()

        start = pl.multiple_of(i * step_rows, step_rows)
        real = jnp.zeros((step_rows, LANES), F32)
        imag = jnp.zeros((step_rows, LANES), F32)
        for r in range(rows):
            a_re = applied_ref[r : r + 1, :]
            a_im = applied_ref[rows + r : rows + r + 1, :]
            o_re = bands[0, pl.ds(start, step_rows), r * LANES : (r + 1) * LANES]
            o_im = bands[1, pl.ds(start, step_rows), r * LANES : (r + 1) * LANES]
            real = real + (o_re * a_re + o_im * a_im)
            imag = imag + (o_re * a_im - o_im * a_re)
        acc[0, pl.ds(start, step_rows), :] = real
        acc[1, pl.ds(start, step_rows), :] = imag
        return carry

    lax.fori_loop(0, sz.bands_all // step_rows, product, 0)
    blocks = sz.bands_all // LANES
    block_row = iota((blocks, LANES), 0)
    sums = []
    for part in range(2):
        total = jnp.zeros((blocks, LANES), F32)
        for i in range(blocks):
            hot_row = ones_where(block_row == i).astype(BF16)
            high, low = split(acc[part, i * LANES : (i + 1) * LANES, :])
            total = total + (dot(hot_row, high, NT) + dot(hot_row, low, NT))
        sums.append(total * (1.0 / (sz.slots * sz.devices)))
    width = sz.band_rows
    per_row = LANES // width
    lane = iota((blocks, LANES), 1)
    for q in range(per_row):
        real = pltpu.roll(sums[0], (-q * width) % LANES, 1)
        imag = pltpu.roll(sums[1], (width - q * width) % LANES, 1)
        tile_ref[pl.ds(q, blocks, stride=per_row), :] = jnp.where(lane < width, real, imag)


def sum_kernel(sz, tile_ref, out_ref):
    width = sz.band_rows
    total = jnp.sum(tile_ref[...], axis=0, keepdims=True)
    shape = (width, LANES)
    total = jnp.broadcast_to(total, shape)
    lane = iota(shape, 1)
    row = iota(shape, 0)
    real = jnp.sum(jnp.where(lane == row, total, 0.0), axis=1, keepdims=True)
    imag = jnp.sum(jnp.where(lane == row + width, total, 0.0), axis=1, keepdims=True)
    out_ref[...] = jnp.concatenate([real, imag], 1)


def full_spec():
    return pl.BlockSpec(memory_space=pltpu.VMEM)


def any_spec():
    return pl.BlockSpec(memory_space=pl.ANY)


def run_spread(sz, cells, orbitals, potential, table, **kw):
    return pl.pallas_call(
        lambda *refs: spread_kernel(sz, *refs),
        out_shape=(
            jax.ShapeDtypeStruct((sz.devices * sz.rows, LANES), F32),
            jax.ShapeDtypeStruct((2 * sz.slot_rows, LANES), F32),
            jax.ShapeDtypeStruct((SUB, LANES), F32),
        ),
        in_specs=[full_spec(), any_spec(), any_spec(), any_spec()],
        out_specs=(full_spec(), full_spec(), full_spec()),
        scratch_shapes=[
            pltpu.VMEM((2, SUB, sz.slots), F32),
            pltpu.VMEM((sz.layers, LANES, LANES), F32),
            pltpu.VMEM(table.shape, BF16),
            pltpu.VMEM((LANES, LANES), F32),
            pltpu.SemaphoreType.DMA((3,)),
        ],
        name="spread",
        **kw,
    )(cells, orbitals, potential, table)


def run_planes(sz, recv, tabs, **kw):
    mats = [tabs[n] for n in ("forward_b", "forward_a", "inverse_a", "inverse_b")]
    return pl.pallas_call(
        lambda *refs: plane_kernel(sz, *refs),
        out_shape=jax.ShapeDtypeStruct((sz.devices * SUB, LANES), F32),
        in_specs=[full_spec()] + [any_spec()] * 4,
        out_specs=full_spec(),
        scratch_shapes=[pltpu.VMEM(m.shape, BF16) for m in mats]
        + [
            pltpu.VMEM((2 * KROWS, LANES), I32),
            pltpu.VMEM((KROWS * SUB, LANES), F32),
            pltpu.VMEM((KROWS * SUB, LANES), F32),
            pltpu.VMEM((sz.devices, LANES), I32),
            pltpu.VMEM((sz.devices, LANES), I32),
            pltpu.SemaphoreType.DMA((4,)),
        ],
        name="planes",
        **kw,
    )(recv, *mats)


def run_final(sz, back, cells, window, meta, table, orbitals, **kw):
    chunk = 64
    return pl.pallas_call(
        lambda *refs: final_kernel(sz, chunk, *refs),
        out_shape=(
            jax.ShapeDtypeStruct((2 * sz.slot_rows, LANES), F32),
            jax.ShapeDtypeStruct((sz.devices, LANES), F32),
        ),
        in_specs=[full_spec()] * 5 + [any_spec()],
        out_specs=(full_spec(), full_spec()),
        scratch_shapes=[
            pltpu.VMEM((2, sz.bands_all, sz.slots), F32),
            pltpu.VMEM((2, sz.bands_all, LANES), F32),
            pltpu.SemaphoreType.DMA((sz.bands_all // chunk,)),
        ],
        name="final",
        **kw,
    )(back, cells, window, meta, table, orbitals)


def run_sum(sz, tile, **kw):
    return pl.pallas_call(
        lambda *refs: sum_kernel(sz, *refs),
        out_shape=jax.ShapeDtypeStruct((sz.band_rows, 2), F32),
        in_specs=[full_spec()],
        out_specs=full_spec(),
        name="add",
        **kw,
    )(tile)


def exchange(x):
    return lax.all_to_all(x, "ga", split_axis=0, concat_axis=0, tiled=True)


def local(orbitals, coeff_cells, potential):
    devices = lax.axis_size("ga")
    sz = Sizes(devices, potential.shape[1], coeff_cells.shape[0], orbitals.shape[1])
    tabs = {name: jnp.asarray(value) for name, value in tables(sz).items()}
    cells = coeff_cells.reshape(sz.slot_rows, LANES)
    send, window, meta = run_spread(sz, cells, orbitals, potential, tabs["forward_z"])
    back = exchange(run_planes(sz, exchange(send), tabs))
    applied, tile = run_final(sz, back, cells, window, meta, tabs["inverse_z"], orbitals)
    subspace = run_sum(sz, exchange(tile))
    return (
        applied.reshape(2, 1, sz.slots),
        subspace.reshape(sz.band_rows, 2, 1),
    )


def solution(mesh):
    in_specs = (P(None, "kpt", "ga"), P("ga"), P("ga", None, None))
    out_specs = (P(None, "kpt", "ga"), P("ga", None, "kpt"))
    return jax.shard_map(local, mesh=mesh, in_specs=in_specs, out_specs=out_specs, check_vma=False)
```

```python
import math

import jax
import jax.numpy as jnp
import numpy as np
from jax import lax
from jax.experimental import pallas as pl
from jax.experimental.pallas import tpu as pltpu
from jax.sharding import PartitionSpec as P

RADIUS = 30
LANES = 128
SUB = 8
HALF = 32
KROWS = 32
CELLS = 4 * 2 * HALF
GROUPS = KROWS // 2
F32 = jnp.float32
BF16 = jnp.bfloat16
I32 = jnp.int32

NT = ((1,), (1,))
NN = ((1,), (0,))


def column_total(extent):
    indices = np.arange(extent)
    frequency = np.where(indices < extent // 2, indices, indices - extent)
    return int(np.sum(frequency[:, None] ** 2 + frequency[None, :] ** 2 <= RADIUS * RADIUS))


class Sizes:
    def __init__(self, devices, extent, slots, bands_all):
        self.devices = devices
        self.extent = extent
        self.layers = extent // devices
        self.channels = 2 * self.layers
        self.slot_rows = slots // LANES
        self.slots = slots
        self.sticks = -(-column_total(extent) // devices)
        self.spare = LANES - self.sticks
        self.id_rows = -(-self.sticks // self.spare)
        used = self.channels + self.layers * self.layers
        self.rows = -(-used // SUB) * SUB
        self.bands_all = bands_all
        self.band_rows = bands_all // devices
        assert extent == LANES and self.channels <= SUB
        assert self.id_rows <= self.channels


def parts_of(matrix):
    values = np.asarray(matrix, np.float32)
    high = values.astype(jnp.bfloat16)
    low = (values - high.astype(np.float32)).astype(jnp.bfloat16)
    return np.stack([high, low])


def angle(x, y, extent):
    phase = (x[:, None] * y[None, :]) % extent
    return 2.0 * math.pi * phase.astype(np.float64) / extent


def tables(sz):
    n, d, layers = sz.extent, sz.devices, sz.layers
    cells = np.arange(n)
    dev, part, lay = np.meshgrid(np.arange(d), np.arange(2), np.arange(layers), indexing="ij")
    z_rows = (dev * layers + lay).reshape(-1)
    part_rows = part.reshape(-1)
    t = angle(z_rows, cells, n)
    re, im = np.cos(t), np.sin(t)
    is_im = part_rows[:, None] == 1
    forward_z = np.concatenate([np.where(is_im, im, re), np.where(is_im, re, -im)], 1)
    freq = np.arange(2 * HALF) - HALF
    tb = angle(freq, cells, n)
    cb, sb = np.cos(tb), np.sin(tb)
    eye = np.eye(2)
    cc, ss = np.kron(eye, cb), np.kron(eye, sb)
    forward_b = np.block([[cc, ss], [-ss, cc]])
    cct, sst = cc.T, ss.T
    inverse_b = np.block([[cct, -sst], [sst, cct]])
    a_rows = (np.arange(d)[None, :] * layers + np.arange(layers)[:, None]).reshape(-1)
    lo, k = np.meshgrid(np.arange(2), np.arange(KROWS), indexing="ij")
    a_freq = (4 * (k % GROUPS) + 2 * (k // GROUPS) + lo - HALF).reshape(-1)
    ta = angle(a_rows, a_freq, n)
    ca, sa = np.cos(ta), np.sin(ta)
    forward_a = np.block([[ca, -sa], [sa, ca]])
    inverse_a = np.block([[ca.T, sa.T], [-sa.T, ca.T]])
    part2, lay2, dev2 = np.meshgrid(np.arange(2), np.arange(layers), np.arange(d), indexing="ij")
    t2 = angle((dev2 * layers + lay2).reshape(-1), cells, n)
    re2, im2 = np.cos(t2) / n**3, np.sin(t2) / n**3
    im_rows = part2.reshape(-1)[:, None] == 1
    inverse_z = np.concatenate([np.where(im_rows, im2, re2), np.where(im_rows, re2, -im2)], 1)
    return {
        "forward_z": parts_of(forward_z),
        "forward_b": parts_of(forward_b),
        "forward_a": parts_of(forward_a),
        "inverse_a": parts_of(inverse_a),
        "inverse_b": parts_of(inverse_b),
        "inverse_z": parts_of(inverse_z),
    }


def split(x):
    high = x.astype(BF16)
    return high, (x - high.astype(F32)).astype(BF16)


def dot(a, b, dims=NN):
    return lax.dot_general(a, b, (dims, ((), ())), preferred_element_type=F32)


def dot3(a, b, dims=NN):
    return dot(a[0], b[0], dims) + dot(a[0], b[1], dims) + dot(a[1], b[0], dims)


def iota(shape, dim):
    return lax.broadcasted_iota(I32, shape, dim)


def ones_where(mask):
    return jnp.where(mask, 1.0, 0.0).astype(F32)


def pick(values, lanes):
    return jnp.take_along_axis(values, lanes, axis=1, mode="promise_in_bounds")


def signed(x, extent):
    return jnp.where(x < extent // 2, x, x - extent)


def column_facts(meta, sz):
    shape = (LANES, LANES)
    col_a = jnp.broadcast_to(meta[:, 0:1], shape)
    col_b = jnp.broadcast_to(meta[:, 1:2], shape)
    row = jnp.broadcast_to(meta[:, 2:3], shape)
    lane = jnp.broadcast_to(meta[:, 3:4], shape)
    valid = jnp.broadcast_to(meta[:, 4:5], shape) > 0.5
    fa = jnp.where(col_a < sz.extent // 2, col_a, col_a - sz.extent)
    fb = jnp.where(col_b < sz.extent // 2, col_b, col_b - sz.extent)
    fc = signed(iota(shape, 1), sz.extent).astype(F32)
    inside = valid & (fc * fc <= RADIUS * RADIUS - fa * fa - fb * fb)
    return row, lane, inside


def spread_kernel(sz, cells_ref, orbitals_ref, potential_ref, table_ref,
                  send_ref, window_ref, meta_ref,
                  block, pot, table, turned, sems):
    loads = [
        pltpu.make_async_copy(orbitals_ref.at[:, pl.ds(0, SUB), :], block, sems.at[0]),
        pltpu.make_async_copy(table_ref, table, sems.at[1]),
        pltpu.make_async_copy(potential_ref, pot, sems.at[2]),
    ]
    for load in loads:
        load.start()
    rows = sz.slot_rows
    shape = (rows, LANES)
    cells = cells_ref[...]
    live = cells >= 0
    column = lax.shift_right_arithmetic(cells, int(math.log2(sz.extent)))
    rolled = pltpu.roll(column, 1, 1)
    above = pltpu.roll(rolled, 1, 0)
    lane = iota(shape, 1)
    row = iota(shape, 0)
    before = jnp.where(lane == 0, jnp.where(row == 0, -1, above), rolled)
    starts = live & (column != before)
    flags = ones_where(starts).astype(BF16)
    square = (LANES, LANES)
    upto = ones_where(iota(square, 0) <= iota(square, 1)).astype(BF16)
    all_ones = jnp.ones(square, BF16)
    within = dot(flags, upto)
    totals = dot(flags, all_ones)
    lower = ones_where(iota((rows, rows), 1) < iota((rows, rows), 0)).astype(BF16)
    rank = (within + dot(lower, totals.astype(BF16))).astype(I32) - 1
    rank = jnp.where(starts, rank, -1)
    col_a = lax.shift_right_arithmetic(column, int(math.log2(sz.extent)))
    col_b = column & (sz.extent - 1)
    sub = iota((SUB, LANES), 0)
    lane8 = iota((SUB, LANES), 1)
    place = iota(square, 0)
    hots, facts = [], []
    for r in range(rows):
        hots.append(ones_where(place == rank[r : r + 1, :]).astype(BF16))
        fact = jnp.where(sub == 0, col_a[r : r + 1, :], col_b[r : r + 1, :])
        fact = jnp.where(sub == 2, r, fact)
        fact = jnp.where(sub == 3, lane8, fact)
        fact = jnp.where(sub == 4, 1, fact)
        facts.append(fact.astype(F32).astype(BF16))
    meta_t = dot(jnp.concatenate(facts, 1), jnp.concatenate(hots, 1), NT)
    meta_ref[...] = meta_t
    meta = jnp.transpose(jnp.concatenate([meta_t, jnp.zeros((LANES - SUB, LANES), F32)], 0))
    first_row, first_lane, inside = column_facts(meta, sz)
    hot = ones_where(inside).astype(BF16)
    before_in = ones_where(iota(square, 0) < iota(square, 1)).astype(BF16)
    slot = (first_lane + dot(hot, before_in)).astype(I32)
    second = slot >= LANES
    slot_lane = slot & (LANES - 1)

    loads[0].wait()
    for r in range(rows):
        window_ref[r : r + 1, :] = block[0, 0:1, r * LANES : (r + 1) * LANES]
        window_ref[rows + r : rows + r + 1, :] = block[1, 0:1, r * LANES : (r + 1) * LANES]
    window = jnp.concatenate([window_ref[0:rows, :], window_ref[rows : 2 * rows, :]], 1)
    high, low = split(window)
    row_of = first_row.astype(I32)[:, 0:rows]
    which = iota((LANES, rows), 1)
    near = ones_where(which == row_of).astype(BF16)
    far = ones_where(which == row_of + 1).astype(BF16)
    near_w = dot(near, high) + dot(near, low)
    far_w = dot(far, high) + dot(far, low)
    sticks = []
    for part in range(2):
        cut = slice(part * LANES, (part + 1) * LANES)
        value = jnp.where(second, pick(far_w[:, cut], slot_lane), pick(near_w[:, cut], slot_lane))
        sticks.append(jnp.where(inside, value, 0.0))
    sticks = jnp.concatenate(sticks, 1)
    loads[1].wait()
    depth = dot3((table[0], table[1]), split(sticks), NT)

    ids = jnp.where(
        meta_t[4:5, :] > 0.5, meta_t[0:1, :] * sz.extent + meta_t[1:2, :], -1.0
    )
    ids = jnp.broadcast_to(ids, (SUB, LANES))
    carried = jnp.zeros((SUB, LANES), F32)
    for i in range(sz.id_rows):
        shifted = pltpu.roll(ids, (sz.sticks - i * sz.spare) % LANES, 1)
        carried = jnp.where(sub == i, shifted, carried)
    is_stick = lane8 < sz.sticks
    channels, layers, devices = sz.channels, sz.layers, sz.devices
    for d in range(devices):
        values = depth[d * channels : (d + 1) * channels, :]
        send_ref[d * sz.rows : d * sz.rows + channels, :] = jnp.where(
            is_stick[0:channels], values, carried[0:channels]
        )
    loads[2].wait()
    for al in range(layers):
        turned[...] = jnp.transpose(pot[al])
        for p in range(layers):
            at = channels + al * layers + p
            send_ref[pl.ds(at, devices, stride=sz.rows), :] = turned[
                pl.ds(p, devices, stride=layers), :
            ]
    for at in range(channels + layers * layers, sz.rows):
        send_ref[pl.ds(at, devices, stride=sz.rows), :] = jnp.zeros((devices, LANES), F32)


def plane_kernel(sz, recv_ref, fb_ref, fa_ref, ia_ref, ib_ref,
                 out_ref,
                 fb, fa, ia, ib, hot_ref, planes, back, group_ref, sems):
    copies = [
        pltpu.make_async_copy(src, dst, sems.at[i])
        for i, (src, dst) in enumerate([(fb_ref, fb), (fa_ref, fa), (ia_ref, ia), (ib_ref, ib)])
    ]
    for c in copies:
        c.start()
    devices, layers, channels = sz.devices, sz.layers, sz.channels
    lane = iota((devices, LANES), 1)
    ids = jnp.full((devices, LANES), -1.0, F32)
    for i in range(sz.id_rows):
        rows = recv_ref[pl.ds(i, devices, stride=sz.rows), :]
        shifted = pltpu.roll(rows, (i * sz.spare - sz.sticks) % LANES, 1)
        mine = (lane >= i * sz.spare) & (lane < min((i + 1) * sz.spare, sz.sticks))
        ids = jnp.where(mine, shifted, ids)
    ids = ids.astype(I32)
    col_a = lax.shift_right_arithmetic(ids, int(math.log2(sz.extent)))
    col_b = ids & (sz.extent - 1)
    sa = (col_a + HALF) & (sz.extent - 1)
    sb = (col_b + HALF) & (sz.extent - 1)
    group = jnp.where(ids >= 0, lax.shift_right_arithmetic(sa, 2), -1)
    cell = (sa & 3) * (2 * HALF) + sb
    group_ref[...] = group
    cell_of = iota((CELLS, LANES), 0)
    left_high, left_low = [], []
    for e in range(devices):
        high, low = split(recv_ref[e * sz.rows : e * sz.rows + SUB, :])
        high, low = high.astype(F32), low.astype(F32)
        here = [jnp.broadcast_to(group[e : e + 1, :], (SUB, LANES)) == g for g in range(GROUPS)]
        for values, side in ((high, left_high), (low, left_low)):
            side.append(
                jnp.concatenate([jnp.where(h, values, 0.0) for h in here], 0).astype(BF16)
            )
        hot_ref[:, e * LANES : (e + 1) * LANES] = ones_where(cell_of == cell[e : e + 1, :]).astype(
            BF16
        )
    left = jnp.concatenate(
        [jnp.concatenate(left_high, 1), jnp.concatenate(left_low, 1)], 0
    )
    spread = dot(left, hot_ref[...], NT)
    size = GROUPS * SUB
    spread = spread[:size] + spread[size:]
    for half in range(2):
        planes[half * size : (half + 1) * size, :] = spread[:, half * LANES : (half + 1) * LANES]

    def plane_part(part, p):
        return planes[pl.ds(part * layers + p, KROWS, stride=SUB), :]

    grid = jnp.concatenate(
        [
            jnp.concatenate([plane_part(part, p) for p in range(layers)], 0)
            for part in range(2)
        ],
        1,
    )
    copies[0].wait()
    grid = dot3(split(grid), (fb[0], fb[1]))
    grid = jnp.concatenate(
        [
            jnp.concatenate(
                [
                    grid[p * KROWS : (p + 1) * KROWS, q * LANES : (q + 1) * LANES]
                    for q in range(4)
                ],
                0,
            )
            for p in range(layers)
        ],
        1,
    )
    copies[1].wait()
    grid = dot3((fa[0], fa[1]), split(grid))
    potential = jnp.concatenate(
        [
            jnp.concatenate(
                [
                    recv_ref[pl.ds(channels + al * layers + p, devices, stride=sz.rows), :]
                    for al in range(layers)
                ],
                0,
            )
            for p in range(layers)
        ],
        1,
    )
    half = sz.extent
    field = jnp.concatenate([grid[0:half] * potential, grid[half:] * potential], 0)
    copies[2].wait()
    grid = dot3((ia[0], ia[1]), split(field))
    grid = jnp.concatenate(
        [
            jnp.concatenate(
                [
                    grid[q * KROWS : (q + 1) * KROWS, p * LANES : (p + 1) * LANES]
                    for q in range(4)
                ],
                1,
            )
            for p in range(layers)
        ],
        0,
    )
    copies[3].wait()
    grid = dot3(split(grid), (ib[0], ib[1]))
    for part in range(2):
        for p in range(layers):
            back[pl.ds(part * layers + p, KROWS, stride=SUB), :] = grid[
                p * KROWS : (p + 1) * KROWS, part * LANES : (part + 1) * LANES
            ]

    values = jnp.concatenate([back[:size, :], back[size:, :]], 1)
    values = jnp.concatenate(split(values), 0)
    for e in range(devices):
        found = dot(values, hot_ref[:, e * LANES : (e + 1) * LANES])
        found = found[:size] + found[size:]
        own = jnp.broadcast_to(group_ref[e : e + 1, :], (SUB, LANES))
        total = jnp.zeros((SUB, LANES), F32)
        for g in range(GROUPS):
            total = total + jnp.where(own == g, found[g * SUB : (g + 1) * SUB, :], 0.0)
        out_ref[e * SUB : (e + 1) * SUB, :] = total


def final_kernel(sz, chunk, back_ref, cells_ref, window_ref, meta_ref, table_ref, orbitals_ref,
                 applied_ref, tile_ref,
                 bands, acc, sems):
    chunks = sz.bands_all // chunk

    def load(i):
        return pltpu.make_async_copy(
            orbitals_ref.at[:, pl.ds(i * chunk, chunk), :],
            bands.at[:, pl.ds(i * chunk, chunk), :],
            sems.at[i],
        )

    for i in range(chunks):
        load(i).start()
    devices, layers, rows = sz.devices, sz.layers, sz.slot_rows
    square = (LANES, LANES)
    values = jnp.concatenate(
        [
            back_ref[pl.ds(part * layers + p, devices, stride=SUB), :]
            for part in range(2)
            for p in range(layers)
        ],
        0,
    )
    values = jnp.transpose(values)
    sticks = dot3(split(values), (table_ref[0], table_ref[1]))
    meta_t = meta_ref[...]
    meta = jnp.transpose(jnp.concatenate([meta_t, jnp.zeros((LANES - SUB, LANES), F32)], 0))
    first_row, first_lane, inside = column_facts(meta, sz)
    length = dot(ones_where(inside).astype(BF16), jnp.ones(square, BF16)).astype(I32)
    shift = iota(square, 1) - first_lane.astype(I32)
    top = lax.shift_right_arithmetic(length - 1, 1)
    placed = []
    for turn in range(2):
        p = shift + turn * LANES
        held = (p >= 0) & (p < length)
        depth = jnp.where(p <= top, p, p + sz.extent - length) & (sz.extent - 1)
        placed.append(
            jnp.concatenate(
                [
                    jnp.where(held, pick(sticks[:, q * LANES : (q + 1) * LANES], depth), 0.0)
                    for q in range(2)
                ],
                1,
            )
        )
    placed = split(jnp.concatenate(placed, 0))
    row_t = jnp.broadcast_to(meta_t[2:3, :].astype(I32), (rows, LANES))
    which = iota((rows, LANES), 0)
    hot = jnp.concatenate(
        [ones_where(which == row_t), ones_where(which == row_t + 1)], 1
    ).astype(BF16)
    local = dot(hot, placed[0]) + dot(hot, placed[1])
    cells = cells_ref[...]
    live = cells >= 0
    bits = int(math.log2(sz.extent))
    mask = sz.extent - 1
    fa = signed(lax.shift_right_arithmetic(cells, 2 * bits) & mask, sz.extent)
    fb = signed(lax.shift_right_arithmetic(cells, bits) & mask, sz.extent)
    fc = signed(cells & mask, sz.extent)
    kinetic = (fa * fa + fb * fb + fc * fc).astype(F32) / (RADIUS * RADIUS)
    for part in range(2):
        own = window_ref[part * rows : (part + 1) * rows, :]
        full = kinetic * own + local[:, part * LANES : (part + 1) * LANES]
        applied_ref[part * rows : (part + 1) * rows, :] = jnp.where(live, full, 0.0)

    step_rows = min(64, chunk)
    steps = chunk // step_rows

    def product(i, carry):
        @pl.when(i % steps == 0)
        def _():
            load(i // steps).wait()

        start = pl.multiple_of(i * step_rows, step_rows)
        real = jnp.zeros((step_rows, LANES), F32)
        imag = jnp.zeros((step_rows, LANES), F32)
        for r in range(rows):
            a_re = applied_ref[r : r + 1, :]
            a_im = applied_ref[rows + r : rows + r + 1, :]
            o_re = bands[0, pl.ds(start, step_rows), r * LANES : (r + 1) * LANES]
            o_im = bands[1, pl.ds(start, step_rows), r * LANES : (r + 1) * LANES]
            real = real + (o_re * a_re + o_im * a_im)
            imag = imag + (o_re * a_im - o_im * a_re)
        acc[0, pl.ds(start, step_rows), :] = real
        acc[1, pl.ds(start, step_rows), :] = imag
        return carry

    lax.fori_loop(0, sz.bands_all // step_rows, product, 0)
    blocks = sz.bands_all // LANES
    block_row = iota((blocks, LANES), 0)
    sums = []
    for part in range(2):
        total = jnp.zeros((blocks, LANES), F32)
        for i in range(blocks):
            hot_row = ones_where(block_row == i).astype(BF16)
            high, low = split(acc[part, i * LANES : (i + 1) * LANES, :])
            total = total + (dot(hot_row, high, NT) + dot(hot_row, low, NT))
        sums.append(total * (1.0 / (sz.slots * sz.devices)))
    width = sz.band_rows
    per_row = LANES // width
    lane = iota((blocks, LANES), 1)
    for q in range(per_row):
        real = pltpu.roll(sums[0], (-q * width) % LANES, 1)
        imag = pltpu.roll(sums[1], (width - q * width) % LANES, 1)
        tile_ref[pl.ds(q, blocks, stride=per_row), :] = jnp.where(lane < width, real, imag)


def sum_kernel(sz, tile_ref, out_ref):
    width = sz.band_rows
    total = jnp.sum(tile_ref[...], axis=0, keepdims=True)
    for part in range(2):
        out_ref[part, :, :] = total[:, part * width : (part + 1) * width]


def full_spec():
    return pl.BlockSpec(memory_space=pltpu.VMEM)


def hbm_spec():
    return pl.BlockSpec(memory_space=pltpu.HBM)


def any_spec():
    return pl.BlockSpec(memory_space=pl.ANY)


def vmem(mib):
    return pltpu.CompilerParams(vmem_limit_bytes=mib << 20)


def run_spread(sz, cells, orbitals, potential, table, **kw):
    return pl.pallas_call(
        lambda *refs: spread_kernel(sz, *refs),
        out_shape=(
            jax.ShapeDtypeStruct((sz.devices * sz.rows, LANES), F32),
            jax.ShapeDtypeStruct((2 * sz.slot_rows, LANES), F32),
            jax.ShapeDtypeStruct((SUB, LANES), F32),
        ),
        in_specs=[full_spec(), hbm_spec(), hbm_spec(), any_spec()],
        out_specs=(full_spec(), full_spec(), full_spec()),
        scratch_shapes=[
            pltpu.VMEM((2, SUB, sz.slots), F32),
            pltpu.VMEM((sz.layers, LANES, LANES), F32),
            pltpu.VMEM(table.shape, BF16),
            pltpu.VMEM((LANES, LANES), F32),
            pltpu.SemaphoreType.DMA((3,)),
        ],
        name="spread",
        compiler_params=vmem(8),
        **kw,
    )(cells, orbitals, potential, table)


def run_planes(sz, recv, tabs, **kw):
    mats = [tabs[n] for n in ("forward_b", "forward_a", "inverse_a", "inverse_b")]
    return pl.pallas_call(
        lambda *refs: plane_kernel(sz, *refs),
        out_shape=jax.ShapeDtypeStruct((sz.devices * SUB, LANES), F32),
        in_specs=[full_spec()] + [any_spec()] * 4,
        out_specs=full_spec(),
        scratch_shapes=[pltpu.VMEM(m.shape, BF16) for m in mats]
        + [
            pltpu.VMEM((CELLS, sz.devices * LANES), BF16),
            pltpu.VMEM((KROWS * SUB, LANES), F32),
            pltpu.VMEM((KROWS * SUB, LANES), F32),
            pltpu.VMEM((sz.devices, LANES), I32),
            pltpu.SemaphoreType.DMA((4,)),
        ],
        name="planes",
        compiler_params=vmem(16),
        **kw,
    )(recv, *mats)


def run_final(sz, back, cells, window, meta, table, orbitals, **kw):
    chunk = 64
    return pl.pallas_call(
        lambda *refs: final_kernel(sz, chunk, *refs),
        out_shape=(
            jax.ShapeDtypeStruct((2 * sz.slot_rows, LANES), F32),
            jax.ShapeDtypeStruct((sz.devices, LANES), F32),
        ),
        in_specs=[full_spec()] * 5 + [any_spec()],
        out_specs=(full_spec(), full_spec()),
        scratch_shapes=[
            pltpu.VMEM((2, sz.bands_all, sz.slots), F32),
            pltpu.VMEM((2, sz.bands_all, LANES), F32),
            pltpu.SemaphoreType.DMA((sz.bands_all // chunk,)),
        ],
        name="final",
        compiler_params=vmem(40),
        **kw,
    )(back, cells, window, meta, table, orbitals)


def run_sum(sz, tile, **kw):
    return pl.pallas_call(
        lambda *refs: sum_kernel(sz, *refs),
        out_shape=jax.ShapeDtypeStruct((2, 1, sz.band_rows), F32),
        in_specs=[full_spec()],
        out_specs=full_spec(),
        name="add",
        compiler_params=vmem(2),
        **kw,
    )(tile)


def exchange(x):
    return lax.all_to_all(x, "ga", split_axis=0, concat_axis=0, tiled=True)


def local(orbitals, coeff_cells, potential):
    devices = lax.axis_size("ga")
    sz = Sizes(devices, potential.shape[1], coeff_cells.shape[0], orbitals.shape[1])
    tabs = {name: jnp.asarray(value) for name, value in tables(sz).items()}
    cells = coeff_cells.reshape(sz.slot_rows, LANES)
    send, window, meta = run_spread(
        sz,
        cells,
        pltpu.with_memory_space_constraint(orbitals, pltpu.HBM),
        pltpu.with_memory_space_constraint(potential, pltpu.HBM),
        tabs["forward_z"],
    )
    back = exchange(run_planes(sz, exchange(send), tabs))
    applied, tile = run_final(sz, back, cells, window, meta, tabs["inverse_z"], orbitals)
    subspace = run_sum(sz, exchange(tile))
    return (
        applied.reshape(2, 1, sz.slots),
        jnp.transpose(subspace, (2, 0, 1)),
    )


def solution(mesh):
    in_specs = (P(None, "kpt", "ga"), P("ga"), P("ga", None, None))
    out_specs = (P(None, "kpt", "ga"), P("ga", None, "kpt"))
    return jax.shard_map(local, mesh=mesh, in_specs=in_specs, out_specs=out_specs, check_vma=False)
```

```python
import math

import jax
import jax.numpy as jnp
import numpy as np
from jax import lax
from jax.experimental import pallas as pl
from jax.experimental.pallas import tpu as pltpu
from jax.sharding import PartitionSpec as P

RADIUS = 30
LANES = 128
SUB = 8
HALF = 32
KROWS = 32
CELLS = 4 * 2 * HALF
GROUPS = KROWS // 2
CHUNK = 64
EARLY = 192
MIDDLE = 384
F32 = jnp.float32
BF16 = jnp.bfloat16
I32 = jnp.int32

NT = ((1,), (1,))
NN = ((1,), (0,))


def column_total(extent):
    indices = np.arange(extent)
    frequency = np.where(indices < extent // 2, indices, indices - extent)
    return int(np.sum(frequency[:, None] ** 2 + frequency[None, :] ** 2 <= RADIUS * RADIUS))


class Sizes:
    def __init__(self, devices, extent, slots, bands_all):
        self.devices = devices
        self.extent = extent
        self.layers = extent // devices
        self.channels = 2 * self.layers
        self.slot_rows = slots // LANES
        self.slots = slots
        self.sticks = -(-column_total(extent) // devices)
        self.spare = LANES - self.sticks
        self.id_rows = -(-self.sticks // self.spare)
        used = self.channels + self.layers * self.layers
        self.rows = -(-used // SUB) * SUB
        self.bands_all = bands_all
        self.band_rows = bands_all // devices
        assert extent == LANES and self.channels <= SUB
        assert self.id_rows <= self.channels


def parts_of(matrix):
    values = np.asarray(matrix, np.float32)
    high = values.astype(jnp.bfloat16)
    low = (values - high.astype(np.float32)).astype(jnp.bfloat16)
    return np.stack([high, low])


def angle(x, y, extent):
    phase = (x[:, None] * y[None, :]) % extent
    return 2.0 * math.pi * phase.astype(np.float64) / extent


def tables(sz):
    n, d, layers = sz.extent, sz.devices, sz.layers
    cells = np.arange(n)
    dev, part, lay = np.meshgrid(np.arange(d), np.arange(2), np.arange(layers), indexing="ij")
    z_rows = (dev * layers + lay).reshape(-1)
    part_rows = part.reshape(-1)
    t = angle(z_rows, cells, n)
    re, im = np.cos(t), np.sin(t)
    is_im = part_rows[:, None] == 1
    forward_z = np.concatenate([np.where(is_im, im, re), np.where(is_im, re, -im)], 1)
    freq = np.arange(2 * HALF) - HALF
    tb = angle(freq, cells, n)
    cb, sb = np.cos(tb), np.sin(tb)
    eye = np.eye(2)
    cc, ss = np.kron(eye, cb), np.kron(eye, sb)
    forward_b = np.block([[cc, ss], [-ss, cc]])
    cct, sst = cc.T, ss.T
    inverse_b = np.block([[cct, -sst], [sst, cct]])
    a_rows = (np.arange(d)[None, :] * layers + np.arange(layers)[:, None]).reshape(-1)
    lo, k = np.meshgrid(np.arange(2), np.arange(KROWS), indexing="ij")
    a_freq = (4 * (k % GROUPS) + 2 * (k // GROUPS) + lo - HALF).reshape(-1)
    ta = angle(a_rows, a_freq, n)
    ca, sa = np.cos(ta), np.sin(ta)
    forward_a = np.block([[ca, -sa], [sa, ca]])
    inverse_a = np.block([[ca.T, sa.T], [-sa.T, ca.T]])
    part2, lay2, dev2 = np.meshgrid(np.arange(2), np.arange(layers), np.arange(d), indexing="ij")
    t2 = angle((dev2 * layers + lay2).reshape(-1), cells, n)
    re2, im2 = np.cos(t2) / n**3, np.sin(t2) / n**3
    im_rows = part2.reshape(-1)[:, None] == 1
    inverse_z = np.concatenate([np.where(im_rows, im2, re2), np.where(im_rows, re2, -im2)], 1)
    return {
        "forward_z": parts_of(forward_z),
        "forward_b": parts_of(forward_b),
        "forward_a": parts_of(forward_a),
        "inverse_a": parts_of(inverse_a),
        "inverse_b": parts_of(inverse_b),
        "inverse_z": parts_of(inverse_z),
    }


def split(x):
    high = x.astype(BF16)
    return high, (x - high.astype(F32)).astype(BF16)


def dot(a, b, dims=NN):
    return lax.dot_general(a, b, (dims, ((), ())), preferred_element_type=F32)


def dot3(a, b, dims=NN):
    return dot(a[0], b[0], dims) + dot(a[0], b[1], dims) + dot(a[1], b[0], dims)


def iota(shape, dim):
    return lax.broadcasted_iota(I32, shape, dim)


def ones_where(mask):
    return jnp.where(mask, 1.0, 0.0).astype(F32)


def pick(values, lanes):
    return jnp.take_along_axis(values, lanes, axis=1, mode="promise_in_bounds")


def signed(x, extent):
    return jnp.where(x < extent // 2, x, x - extent)


def column_facts(meta, sz):
    shape = (LANES, LANES)
    col_a = jnp.broadcast_to(meta[:, 0:1], shape)
    col_b = jnp.broadcast_to(meta[:, 1:2], shape)
    row = jnp.broadcast_to(meta[:, 2:3], shape)
    lane = jnp.broadcast_to(meta[:, 3:4], shape)
    valid = jnp.broadcast_to(meta[:, 4:5], shape) > 0.5
    fa = jnp.where(col_a < sz.extent // 2, col_a, col_a - sz.extent)
    fb = jnp.where(col_b < sz.extent // 2, col_b, col_b - sz.extent)
    fc = signed(iota(shape, 1), sz.extent).astype(F32)
    inside = valid & (fc * fc <= RADIUS * RADIUS - fa * fa - fb * fb)
    return row, lane, inside


class BandLoads:
    def __init__(self, source, target, sems, first, count):
        self.copies = [
            pltpu.make_async_copy(
                source.at[:, pl.ds(first + at, CHUNK), :],
                target.at[:, pl.ds(at, CHUNK), :],
                sems.at[at // CHUNK],
            )
            for at in range(0, count, CHUNK)
        ]

    def start(self):
        for copy in self.copies:
            copy.start()

    def wait(self):
        for copy in self.copies:
            copy.wait()


def spread_kernel(sz, cells_ref, orbitals_ref, potential_ref, table_ref,
                  send_ref, window_ref, meta_ref, early_ref,
                  cells_in, block, pot, table, turned, sems, band_sems):
    loads = [
        pltpu.make_async_copy(orbitals_ref.at[:, pl.ds(0, SUB), :], block, sems.at[0]),
        pltpu.make_async_copy(table_ref, table, sems.at[1]),
        pltpu.make_async_copy(potential_ref, pot, sems.at[2]),
    ]
    cell_load = pltpu.make_async_copy(cells_ref, cells_in, sems.at[3])
    cell_load.start()
    for load in loads:
        load.start()
    bands = BandLoads(orbitals_ref, early_ref, band_sems, 0, EARLY)
    bands.start()
    cell_load.wait()
    rows = sz.slot_rows
    shape = (rows, LANES)
    cells = cells_in[...]
    live = cells >= 0
    column = lax.shift_right_arithmetic(cells, int(math.log2(sz.extent)))
    rolled = pltpu.roll(column, 1, 1)
    above = pltpu.roll(rolled, 1, 0)
    lane = iota(shape, 1)
    row = iota(shape, 0)
    before = jnp.where(lane == 0, jnp.where(row == 0, -1, above), rolled)
    starts = live & (column != before)
    flags = ones_where(starts).astype(BF16)
    square = (LANES, LANES)
    upto = ones_where(iota(square, 0) <= iota(square, 1)).astype(BF16)
    all_ones = jnp.ones(square, BF16)
    within = dot(flags, upto)
    totals = dot(flags, all_ones)
    lower = ones_where(iota((rows, rows), 1) < iota((rows, rows), 0)).astype(BF16)
    rank = (within + dot(lower, totals.astype(BF16))).astype(I32) - 1
    rank = jnp.where(starts, rank, -1)
    col_a = lax.shift_right_arithmetic(column, int(math.log2(sz.extent)))
    col_b = column & (sz.extent - 1)
    sub = iota((SUB, LANES), 0)
    lane8 = iota((SUB, LANES), 1)
    place = iota(square, 0)
    hots, facts = [], []
    for r in range(rows):
        hots.append(ones_where(place == rank[r : r + 1, :]).astype(BF16))
        fact = jnp.where(sub == 0, col_a[r : r + 1, :], col_b[r : r + 1, :])
        fact = jnp.where(sub == 2, r, fact)
        fact = jnp.where(sub == 3, lane8, fact)
        fact = jnp.where(sub == 4, 1, fact)
        facts.append(fact.astype(F32).astype(BF16))
    meta_t = dot(jnp.concatenate(facts, 1), jnp.concatenate(hots, 1), NT)
    meta_ref[...] = meta_t
    meta = jnp.transpose(jnp.concatenate([meta_t, jnp.zeros((LANES - SUB, LANES), F32)], 0))
    first_row, first_lane, inside = column_facts(meta, sz)
    hot = ones_where(inside).astype(BF16)
    before_in = ones_where(iota(square, 0) < iota(square, 1)).astype(BF16)
    slot = (first_lane + dot(hot, before_in)).astype(I32)
    second = slot >= LANES
    slot_lane = slot & (LANES - 1)

    loads[0].wait()
    for r in range(rows):
        window_ref[r : r + 1, :] = block[0, 0:1, r * LANES : (r + 1) * LANES]
        window_ref[rows + r : rows + r + 1, :] = block[1, 0:1, r * LANES : (r + 1) * LANES]
    window = jnp.concatenate([window_ref[0:rows, :], window_ref[rows : 2 * rows, :]], 1)
    high, low = split(window)
    row_of = first_row.astype(I32)[:, 0:rows]
    which = iota((LANES, rows), 1)
    near = ones_where(which == row_of).astype(BF16)
    far = ones_where(which == row_of + 1).astype(BF16)
    near_w = dot(near, high) + dot(near, low)
    far_w = dot(far, high) + dot(far, low)
    sticks = []
    for part in range(2):
        cut = slice(part * LANES, (part + 1) * LANES)
        value = jnp.where(second, pick(far_w[:, cut], slot_lane), pick(near_w[:, cut], slot_lane))
        sticks.append(jnp.where(inside, value, 0.0))
    sticks = jnp.concatenate(sticks, 1)
    loads[1].wait()
    depth = dot3((table[0], table[1]), split(sticks), NT)

    ids = jnp.where(
        meta_t[4:5, :] > 0.5, meta_t[0:1, :] * sz.extent + meta_t[1:2, :], -1.0
    )
    ids = jnp.broadcast_to(ids, (SUB, LANES))
    carried = jnp.zeros((SUB, LANES), F32)
    for i in range(sz.id_rows):
        shifted = pltpu.roll(ids, (sz.sticks - i * sz.spare) % LANES, 1)
        carried = jnp.where(sub == i, shifted, carried)
    is_stick = lane8 < sz.sticks
    channels, layers, devices = sz.channels, sz.layers, sz.devices
    for d in range(devices):
        values = depth[d * channels : (d + 1) * channels, :]
        send_ref[d * sz.rows : d * sz.rows + channels, :] = jnp.where(
            is_stick[0:channels], values, carried[0:channels]
        )
    loads[2].wait()
    for al in range(layers):
        turned[...] = jnp.transpose(pot[al])
        for p in range(layers):
            at = channels + al * layers + p
            send_ref[pl.ds(at, devices, stride=sz.rows), :] = turned[
                pl.ds(p, devices, stride=layers), :
            ]
    for at in range(channels + layers * layers, sz.rows):
        send_ref[pl.ds(at, devices, stride=sz.rows), :] = jnp.zeros((devices, LANES), F32)
    bands.wait()


def plane_kernel(sz, recv_ref, fb_ref, fa_ref, ia_ref, ib_ref, orbitals_ref,
                 out_ref, middle_ref,
                 fb, fa, ia, ib, hot_ref, planes, back, group_ref, sems, band_sems):
    bands = BandLoads(orbitals_ref, middle_ref, band_sems, EARLY, MIDDLE)
    bands.start()
    copies = [
        pltpu.make_async_copy(src, dst, sems.at[i])
        for i, (src, dst) in enumerate([(fb_ref, fb), (fa_ref, fa), (ia_ref, ia), (ib_ref, ib)])
    ]
    for c in copies:
        c.start()
    devices, layers, channels = sz.devices, sz.layers, sz.channels
    lane = iota((devices, LANES), 1)
    ids = jnp.full((devices, LANES), -1.0, F32)
    for i in range(sz.id_rows):
        rows = recv_ref[pl.ds(i, devices, stride=sz.rows), :]
        shifted = pltpu.roll(rows, (i * sz.spare - sz.sticks) % LANES, 1)
        mine = (lane >= i * sz.spare) & (lane < min((i + 1) * sz.spare, sz.sticks))
        ids = jnp.where(mine, shifted, ids)
    ids = ids.astype(I32)
    col_a = lax.shift_right_arithmetic(ids, int(math.log2(sz.extent)))
    col_b = ids & (sz.extent - 1)
    sa = (col_a + HALF) & (sz.extent - 1)
    sb = (col_b + HALF) & (sz.extent - 1)
    group = jnp.where(ids >= 0, lax.shift_right_arithmetic(sa, 2), -1)
    cell = (sa & 3) * (2 * HALF) + sb
    group_ref[...] = group
    cell_of = iota((CELLS, LANES), 0)
    left_high, left_low = [], []
    for e in range(devices):
        high, low = split(recv_ref[e * sz.rows : e * sz.rows + SUB, :])
        high, low = high.astype(F32), low.astype(F32)
        here = [jnp.broadcast_to(group[e : e + 1, :], (SUB, LANES)) == g for g in range(GROUPS)]
        for values, side in ((high, left_high), (low, left_low)):
            side.append(
                jnp.concatenate([jnp.where(h, values, 0.0) for h in here], 0).astype(BF16)
            )
        hot_ref[:, e * LANES : (e + 1) * LANES] = ones_where(cell_of == cell[e : e + 1, :]).astype(
            BF16
        )
    left = jnp.concatenate(
        [jnp.concatenate(left_high, 1), jnp.concatenate(left_low, 1)], 0
    )
    spread = dot(left, hot_ref[...], NT)
    size = GROUPS * SUB
    spread = spread[:size] + spread[size:]
    for half in range(2):
        planes[half * size : (half + 1) * size, :] = spread[:, half * LANES : (half + 1) * LANES]

    def plane_part(part, p):
        return planes[pl.ds(part * layers + p, KROWS, stride=SUB), :]

    grid = jnp.concatenate(
        [
            jnp.concatenate([plane_part(part, p) for p in range(layers)], 0)
            for part in range(2)
        ],
        1,
    )
    copies[0].wait()
    grid = dot3(split(grid), (fb[0], fb[1]))
    grid = jnp.concatenate(
        [
            jnp.concatenate(
                [
                    grid[p * KROWS : (p + 1) * KROWS, q * LANES : (q + 1) * LANES]
                    for q in range(4)
                ],
                0,
            )
            for p in range(layers)
        ],
        1,
    )
    copies[1].wait()
    grid = dot3((fa[0], fa[1]), split(grid))
    potential = jnp.concatenate(
        [
            jnp.concatenate(
                [
                    recv_ref[pl.ds(channels + al * layers + p, devices, stride=sz.rows), :]
                    for al in range(layers)
                ],
                0,
            )
            for p in range(layers)
        ],
        1,
    )
    half = sz.extent
    field = jnp.concatenate([grid[0:half] * potential, grid[half:] * potential], 0)
    copies[2].wait()
    grid = dot3((ia[0], ia[1]), split(field))
    grid = jnp.concatenate(
        [
            jnp.concatenate(
                [
                    grid[q * KROWS : (q + 1) * KROWS, p * LANES : (p + 1) * LANES]
                    for q in range(4)
                ],
                1,
            )
            for p in range(layers)
        ],
        0,
    )
    copies[3].wait()
    grid = dot3(split(grid), (ib[0], ib[1]))
    for part in range(2):
        for p in range(layers):
            back[pl.ds(part * layers + p, KROWS, stride=SUB), :] = grid[
                p * KROWS : (p + 1) * KROWS, part * LANES : (part + 1) * LANES
            ]

    values = jnp.concatenate([back[:size, :], back[size:, :]], 1)
    values = jnp.concatenate(split(values), 0)
    for e in range(devices):
        found = dot(values, hot_ref[:, e * LANES : (e + 1) * LANES])
        found = found[:size] + found[size:]
        own = jnp.broadcast_to(group_ref[e : e + 1, :], (SUB, LANES))
        total = jnp.zeros((SUB, LANES), F32)
        for g in range(GROUPS):
            total = total + jnp.where(own == g, found[g * SUB : (g + 1) * SUB, :], 0.0)
        out_ref[e * SUB : (e + 1) * SUB, :] = total
    bands.wait()


def final_kernel(sz, back_ref, cells_ref, window_ref, meta_ref, table_ref, early_ref, middle_ref,
                 orbitals_ref,
                 applied_ref, tile_ref,
                 late_ref, acc, band_sems):
    done = EARLY + MIDDLE
    bands = BandLoads(orbitals_ref, late_ref, band_sems, done, sz.bands_all - done)
    bands.start()
    devices, layers, rows = sz.devices, sz.layers, sz.slot_rows
    square = (LANES, LANES)
    values = jnp.concatenate(
        [
            back_ref[pl.ds(part * layers + p, devices, stride=SUB), :]
            for part in range(2)
            for p in range(layers)
        ],
        0,
    )
    values = jnp.transpose(values)
    sticks = dot3(split(values), (table_ref[0], table_ref[1]))
    meta_t = meta_ref[...]
    meta = jnp.transpose(jnp.concatenate([meta_t, jnp.zeros((LANES - SUB, LANES), F32)], 0))
    first_row, first_lane, inside = column_facts(meta, sz)
    length = dot(ones_where(inside).astype(BF16), jnp.ones(square, BF16)).astype(I32)
    shift = iota(square, 1) - first_lane.astype(I32)
    top = lax.shift_right_arithmetic(length - 1, 1)
    placed = []
    for turn in range(2):
        p = shift + turn * LANES
        held = (p >= 0) & (p < length)
        depth = jnp.where(p <= top, p, p + sz.extent - length) & (sz.extent - 1)
        placed.append(
            jnp.concatenate(
                [
                    jnp.where(held, pick(sticks[:, q * LANES : (q + 1) * LANES], depth), 0.0)
                    for q in range(2)
                ],
                1,
            )
        )
    placed = split(jnp.concatenate(placed, 0))
    row_t = jnp.broadcast_to(meta_t[2:3, :].astype(I32), (rows, LANES))
    which = iota((rows, LANES), 0)
    hot = jnp.concatenate(
        [ones_where(which == row_t), ones_where(which == row_t + 1)], 1
    ).astype(BF16)
    local = dot(hot, placed[0]) + dot(hot, placed[1])
    cells = cells_ref[...]
    live = cells >= 0
    bits = int(math.log2(sz.extent))
    mask = sz.extent - 1
    fa = signed(lax.shift_right_arithmetic(cells, 2 * bits) & mask, sz.extent)
    fb = signed(lax.shift_right_arithmetic(cells, bits) & mask, sz.extent)
    fc = signed(cells & mask, sz.extent)
    kinetic = (fa * fa + fb * fb + fc * fc).astype(F32) / (RADIUS * RADIUS)
    for part in range(2):
        own = window_ref[part * rows : (part + 1) * rows, :]
        full = kinetic * own + local[:, part * LANES : (part + 1) * LANES]
        applied_ref[part * rows : (part + 1) * rows, :] = jnp.where(live, full, 0.0)

    def product_of(source, first):
        def product(i, carry):
            start = pl.multiple_of(i * CHUNK, CHUNK)
            real = jnp.zeros((CHUNK, LANES), F32)
            imag = jnp.zeros((CHUNK, LANES), F32)
            for r in range(rows):
                a_re = applied_ref[r : r + 1, :]
                a_im = applied_ref[rows + r : rows + r + 1, :]
                o_re = source[0, pl.ds(start, CHUNK), r * LANES : (r + 1) * LANES]
                o_im = source[1, pl.ds(start, CHUNK), r * LANES : (r + 1) * LANES]
                real = real + (o_re * a_re + o_im * a_im)
                imag = imag + (o_re * a_im - o_im * a_re)
            acc[0, pl.ds(first + start, CHUNK), :] = real
            acc[1, pl.ds(first + start, CHUNK), :] = imag
            return carry

        lax.fori_loop(0, source.shape[1] // CHUNK, product, 0)

    product_of(early_ref, 0)
    product_of(middle_ref, EARLY)
    bands.wait()
    product_of(late_ref, done)
    blocks = sz.bands_all // LANES
    block_row = iota((blocks, LANES), 0)
    sums = []
    for part in range(2):
        total = jnp.zeros((blocks, LANES), F32)
        for i in range(blocks):
            hot_row = ones_where(block_row == i).astype(BF16)
            high, low = split(acc[part, i * LANES : (i + 1) * LANES, :])
            total = total + (dot(hot_row, high, NT) + dot(hot_row, low, NT))
        sums.append(total * (1.0 / (sz.slots * sz.devices)))
    width = sz.band_rows
    per_row = LANES // width
    lane = iota((blocks, LANES), 1)
    for q in range(per_row):
        real = pltpu.roll(sums[0], (-q * width) % LANES, 1)
        imag = pltpu.roll(sums[1], (width - q * width) % LANES, 1)
        tile_ref[pl.ds(q, blocks, stride=per_row), :] = jnp.where(lane < width, real, imag)


def sum_kernel(sz, tile_ref, out_ref):
    width = sz.band_rows
    total = jnp.sum(tile_ref[...], axis=0, keepdims=True)
    for part in range(2):
        out_ref[part, :, :] = total[:, part * width : (part + 1) * width]


def full_spec():
    return pl.BlockSpec(memory_space=pltpu.VMEM)


def any_spec():
    return pl.BlockSpec(memory_space=pl.ANY)


def vmem(mib):
    return pltpu.CompilerParams(vmem_limit_bytes=mib << 20)


def run_spread(sz, cells, orbitals, potential, table, **kw):
    return pl.pallas_call(
        lambda *refs: spread_kernel(sz, *refs),
        out_shape=(
            jax.ShapeDtypeStruct((sz.devices * sz.rows, LANES), F32),
            jax.ShapeDtypeStruct((2 * sz.slot_rows, LANES), F32),
            jax.ShapeDtypeStruct((SUB, LANES), F32),
            pltpu.VMEM((2, EARLY, sz.slots), F32),
        ),
        in_specs=[any_spec()] * 4,
        out_specs=(full_spec(),) * 4,
        scratch_shapes=[
            pltpu.VMEM((sz.slot_rows, LANES), I32),
            pltpu.VMEM((2, SUB, sz.slots), F32),
            pltpu.VMEM((sz.layers, LANES, LANES), F32),
            pltpu.VMEM(table.shape, BF16),
            pltpu.VMEM((LANES, LANES), F32),
            pltpu.SemaphoreType.DMA((4,)),
            pltpu.SemaphoreType.DMA((EARLY // CHUNK,)),
        ],
        name="spread",
        compiler_params=vmem(8),
        **kw,
    )(cells, orbitals, potential, table)


def run_planes(sz, recv, tabs, orbitals, **kw):
    mats = [tabs[n] for n in ("forward_b", "forward_a", "inverse_a", "inverse_b")]
    return pl.pallas_call(
        lambda *refs: plane_kernel(sz, *refs),
        out_shape=(
            jax.ShapeDtypeStruct((sz.devices * SUB, LANES), F32),
            pltpu.VMEM((2, MIDDLE, sz.slots), F32),
        ),
        in_specs=[full_spec()] + [any_spec()] * 5,
        out_specs=(full_spec(), full_spec()),
        scratch_shapes=[pltpu.VMEM(m.shape, BF16) for m in mats]
        + [
            pltpu.VMEM((CELLS, sz.devices * LANES), BF16),
            pltpu.VMEM((KROWS * SUB, LANES), F32),
            pltpu.VMEM((KROWS * SUB, LANES), F32),
            pltpu.VMEM((sz.devices, LANES), I32),
            pltpu.SemaphoreType.DMA((4,)),
            pltpu.SemaphoreType.DMA((MIDDLE // CHUNK,)),
        ],
        name="planes",
        compiler_params=vmem(16),
        **kw,
    )(recv, *mats, orbitals)


def run_final(sz, back, cells, window, meta, table, early, middle, orbitals, **kw):
    late = sz.bands_all - EARLY - MIDDLE
    return pl.pallas_call(
        lambda *refs: final_kernel(sz, *refs),
        out_shape=(
            jax.ShapeDtypeStruct((2 * sz.slot_rows, LANES), F32),
            jax.ShapeDtypeStruct((sz.devices, LANES), F32),
        ),
        in_specs=[full_spec()] * 7 + [any_spec()],
        out_specs=(full_spec(), full_spec()),
        scratch_shapes=[
            pltpu.VMEM((2, late, sz.slots), F32),
            pltpu.VMEM((2, sz.bands_all, LANES), F32),
            pltpu.SemaphoreType.DMA((late // CHUNK,)),
        ],
        name="final",
        compiler_params=vmem(20),
        **kw,
    )(back, cells, window, meta, table, early, middle, orbitals)


def run_sum(sz, tile, **kw):
    return pl.pallas_call(
        lambda *refs: sum_kernel(sz, *refs),
        out_shape=jax.ShapeDtypeStruct((2, 1, sz.band_rows), F32),
        in_specs=[full_spec()],
        out_specs=full_spec(),
        name="add",
        compiler_params=vmem(2),
        **kw,
    )(tile)


def exchange(x):
    return lax.all_to_all(x, "ga", split_axis=0, concat_axis=0, tiled=True)


def local(orbitals, coeff_cells, potential):
    devices = lax.axis_size("ga")
    sz = Sizes(devices, potential.shape[1], coeff_cells.shape[0], orbitals.shape[1])
    tabs = {name: jnp.asarray(value) for name, value in tables(sz).items()}
    cells = coeff_cells.reshape(sz.slot_rows, LANES)
    stay = lambda x: pltpu.with_memory_space_constraint(x, pltpu.HBM)
    orbitals = stay(orbitals)
    send, window, meta, early = run_spread(
        sz, stay(cells), orbitals, stay(potential), stay(tabs["forward_z"])
    )
    back, middle = run_planes(sz, exchange(send), tabs, orbitals)
    applied, tile = run_final(
        sz, exchange(back), cells, window, meta, tabs["inverse_z"], early, middle, orbitals
    )
    subspace = run_sum(sz, exchange(tile))
    return (
        applied.reshape(2, 1, sz.slots),
        jnp.transpose(subspace, (2, 0, 1)),
    )


def solution(mesh):
    in_specs = (P(None, "kpt", "ga"), P("ga"), P("ga", None, None))
    out_specs = (P(None, "kpt", "ga"), P("ga", None, "kpt"))
    return jax.shard_map(local, mesh=mesh, in_specs=in_specs, out_specs=out_specs, check_vma=False)
```

```python
import math

import jax
import jax.numpy as jnp
import numpy as np
from jax import lax
from jax.experimental import pallas as pl
from jax.experimental.pallas import tpu as pltpu
from jax.sharding import PartitionSpec as P

RADIUS = 30
LANES = 128
SUB = 8
HALF = 32
KROWS = 32
CELLS = 4 * 2 * HALF
GROUPS = KROWS // 2
CHUNK = 64
EARLY = 128
MIDDLE = 384
F32 = jnp.float32
BF16 = jnp.bfloat16
I32 = jnp.int32

NT = ((1,), (1,))
NN = ((1,), (0,))


def column_total(extent):
    indices = np.arange(extent)
    frequency = np.where(indices < extent // 2, indices, indices - extent)
    return int(np.sum(frequency[:, None] ** 2 + frequency[None, :] ** 2 <= RADIUS * RADIUS))


class Sizes:
    def __init__(self, devices, extent, slots, bands_all):
        self.devices = devices
        self.extent = extent
        self.layers = extent // devices
        self.channels = 2 * self.layers
        self.slot_rows = slots // LANES
        self.slots = slots
        self.sticks = -(-column_total(extent) // devices)
        self.spare = LANES - self.sticks
        self.id_rows = -(-self.sticks // self.spare)
        used = self.channels + self.layers * self.layers
        self.rows = -(-used // SUB) * SUB
        self.bands_all = bands_all
        self.band_rows = bands_all // devices
        assert extent == LANES and self.channels <= SUB
        assert self.id_rows <= self.channels


def parts_of(matrix):
    values = np.asarray(matrix, np.float32)
    high = values.astype(jnp.bfloat16)
    low = (values - high.astype(np.float32)).astype(jnp.bfloat16)
    return np.stack([high, low])


def angle(x, y, extent):
    phase = (x[:, None] * y[None, :]) % extent
    return 2.0 * math.pi * phase.astype(np.float64) / extent


def tables(sz):
    n, d, layers = sz.extent, sz.devices, sz.layers
    cells = np.arange(n)
    dev, part, lay = np.meshgrid(np.arange(d), np.arange(2), np.arange(layers), indexing="ij")
    z_rows = (dev * layers + lay).reshape(-1)
    part_rows = part.reshape(-1)
    t = angle(z_rows, cells, n)
    re, im = np.cos(t), np.sin(t)
    is_im = part_rows[:, None] == 1
    forward_z = np.concatenate([np.where(is_im, im, re), np.where(is_im, re, -im)], 1)
    freq = np.arange(2 * HALF) - HALF
    tb = angle(freq, cells, n)
    cb, sb = np.cos(tb), np.sin(tb)
    eye = np.eye(2)
    cc, ss = np.kron(eye, cb), np.kron(eye, sb)
    forward_b = np.block([[cc, ss], [-ss, cc]])
    cct, sst = cc.T, ss.T
    inverse_b = np.block([[cct, -sst], [sst, cct]])
    a_rows = (np.arange(d)[None, :] * layers + np.arange(layers)[:, None]).reshape(-1)
    lo, k = np.meshgrid(np.arange(2), np.arange(KROWS), indexing="ij")
    a_freq = (4 * (k % GROUPS) + 2 * (k // GROUPS) + lo - HALF).reshape(-1)
    ta = angle(a_rows, a_freq, n)
    ca, sa = np.cos(ta), np.sin(ta)
    forward_a = np.block([[ca, -sa], [sa, ca]])
    inverse_a = np.block([[ca.T, sa.T], [-sa.T, ca.T]])
    part2, lay2, dev2 = np.meshgrid(np.arange(2), np.arange(layers), np.arange(d), indexing="ij")
    t2 = angle((dev2 * layers + lay2).reshape(-1), cells, n)
    re2, im2 = np.cos(t2) / n**3, np.sin(t2) / n**3
    im_rows = part2.reshape(-1)[:, None] == 1
    inverse_z = np.concatenate([np.where(im_rows, im2, re2), np.where(im_rows, re2, -im2)], 1)
    return {
        "forward_z": parts_of(forward_z),
        "forward_b": parts_of(forward_b),
        "forward_a": parts_of(forward_a),
        "inverse_a": parts_of(inverse_a),
        "inverse_b": parts_of(inverse_b),
        "inverse_z": parts_of(inverse_z),
    }


def split(x):
    high = x.astype(BF16)
    return high, (x - high.astype(F32)).astype(BF16)


def dot(a, b, dims=NN):
    return lax.dot_general(a, b, (dims, ((), ())), preferred_element_type=F32)


def dot3(a, b, dims=NN):
    return dot(a[0], b[0], dims) + dot(a[0], b[1], dims) + dot(a[1], b[0], dims)


def iota(shape, dim):
    return lax.broadcasted_iota(I32, shape, dim)


def ones_where(mask):
    return jnp.where(mask, 1.0, 0.0).astype(F32)


def pick(values, lanes):
    return jnp.take_along_axis(values, lanes, axis=1, mode="promise_in_bounds")


def signed(x, extent):
    return jnp.where(x < extent // 2, x, x - extent)


def column_facts(meta, sz):
    shape = (LANES, LANES)
    col_a = jnp.broadcast_to(meta[:, 0:1], shape)
    col_b = jnp.broadcast_to(meta[:, 1:2], shape)
    row = jnp.broadcast_to(meta[:, 2:3], shape)
    lane = jnp.broadcast_to(meta[:, 3:4], shape)
    valid = jnp.broadcast_to(meta[:, 4:5], shape) > 0.5
    fa = jnp.where(col_a < sz.extent // 2, col_a, col_a - sz.extent)
    fb = jnp.where(col_b < sz.extent // 2, col_b, col_b - sz.extent)
    fc = signed(iota(shape, 1), sz.extent).astype(F32)
    inside = valid & (fc * fc <= RADIUS * RADIUS - fa * fa - fb * fb)
    return row, lane, inside


class BandLoads:
    def __init__(self, source, target, sems, first, count):
        self.refs = (source, target, sems, first)
        self.count = count // CHUNK

    def copy(self, i):
        source, target, sems, first = self.refs
        return pltpu.make_async_copy(
            source.at[:, pl.ds(first + i * CHUNK, CHUNK), :],
            target.at[:, pl.ds(i * CHUNK, CHUNK), :],
            sems.at[i],
        )

    def start(self):
        for i in range(self.count):
            self.copy(i).start()

    def wait_one(self, i):
        self.copy(i).wait()

    def wait(self):
        for i in range(self.count):
            self.copy(i).wait()


def spread_kernel(sz, cells_ref, orbitals_ref, potential_ref, table_ref,
                  send_ref, window_ref, meta_ref, early_ref,
                  cells_in, block, pot, table, turned, sems, band_sems):
    loads = [
        pltpu.make_async_copy(orbitals_ref.at[:, pl.ds(0, SUB), :], block, sems.at[0]),
        pltpu.make_async_copy(table_ref, table, sems.at[1]),
        pltpu.make_async_copy(potential_ref, pot, sems.at[2]),
    ]
    cell_load = pltpu.make_async_copy(cells_ref, cells_in, sems.at[3])
    cell_load.start()
    for load in loads:
        load.start()
    bands = BandLoads(orbitals_ref, early_ref, band_sems, 0, EARLY)
    bands.start()
    cell_load.wait()
    rows = sz.slot_rows
    shape = (rows, LANES)
    cells = cells_in[...]
    live = cells >= 0
    column = lax.shift_right_arithmetic(cells, int(math.log2(sz.extent)))
    rolled = pltpu.roll(column, 1, 1)
    above = pltpu.roll(rolled, 1, 0)
    lane = iota(shape, 1)
    row = iota(shape, 0)
    before = jnp.where(lane == 0, jnp.where(row == 0, -1, above), rolled)
    starts = live & (column != before)
    flags = ones_where(starts).astype(BF16)
    square = (LANES, LANES)
    upto = ones_where(iota(square, 0) <= iota(square, 1)).astype(BF16)
    all_ones = jnp.ones(square, BF16)
    within = dot(flags, upto)
    totals = dot(flags, all_ones)
    lower = ones_where(iota((rows, rows), 1) < iota((rows, rows), 0)).astype(BF16)
    rank = (within + dot(lower, totals.astype(BF16))).astype(I32) - 1
    rank = jnp.where(starts, rank, -1)
    col_a = lax.shift_right_arithmetic(column, int(math.log2(sz.extent)))
    col_b = column & (sz.extent - 1)
    sub = iota((SUB, LANES), 0)
    lane8 = iota((SUB, LANES), 1)
    place = iota(square, 0)
    hots, facts = [], []
    for r in range(rows):
        hots.append(ones_where(place == rank[r : r + 1, :]).astype(BF16))
        fact = jnp.where(sub == 0, col_a[r : r + 1, :], col_b[r : r + 1, :])
        fact = jnp.where(sub == 2, r, fact)
        fact = jnp.where(sub == 3, lane8, fact)
        fact = jnp.where(sub == 4, 1, fact)
        facts.append(fact.astype(F32).astype(BF16))
    meta_t = dot(jnp.concatenate(facts, 1), jnp.concatenate(hots, 1), NT)
    meta_ref[...] = meta_t
    meta = jnp.transpose(jnp.concatenate([meta_t, jnp.zeros((LANES - SUB, LANES), F32)], 0))
    first_row, first_lane, inside = column_facts(meta, sz)
    hot = ones_where(inside).astype(BF16)
    before_in = ones_where(iota(square, 0) < iota(square, 1)).astype(BF16)
    slot = (first_lane + dot(hot, before_in)).astype(I32)
    second = slot >= LANES
    slot_lane = slot & (LANES - 1)

    loads[0].wait()
    for r in range(rows):
        window_ref[r : r + 1, :] = block[0, 0:1, r * LANES : (r + 1) * LANES]
        window_ref[rows + r : rows + r + 1, :] = block[1, 0:1, r * LANES : (r + 1) * LANES]
    window = jnp.concatenate([window_ref[0:rows, :], window_ref[rows : 2 * rows, :]], 1)
    high, low = split(window)
    row_of = first_row.astype(I32)[:, 0:rows]
    which = iota((LANES, rows), 1)
    near = ones_where(which == row_of).astype(BF16)
    far = ones_where(which == row_of + 1).astype(BF16)
    near_w = dot(near, high) + dot(near, low)
    far_w = dot(far, high) + dot(far, low)
    sticks = []
    for part in range(2):
        cut = slice(part * LANES, (part + 1) * LANES)
        value = jnp.where(second, pick(far_w[:, cut], slot_lane), pick(near_w[:, cut], slot_lane))
        sticks.append(jnp.where(inside, value, 0.0))
    sticks = jnp.concatenate(sticks, 1)
    loads[1].wait()
    depth = dot3((table[0], table[1]), split(sticks), NT)

    ids = jnp.where(
        meta_t[4:5, :] > 0.5, meta_t[0:1, :] * sz.extent + meta_t[1:2, :], -1.0
    )
    ids = jnp.broadcast_to(ids, (SUB, LANES))
    carried = jnp.zeros((SUB, LANES), F32)
    for i in range(sz.id_rows):
        shifted = pltpu.roll(ids, (sz.sticks - i * sz.spare) % LANES, 1)
        carried = jnp.where(sub == i, shifted, carried)
    is_stick = lane8 < sz.sticks
    channels, layers, devices = sz.channels, sz.layers, sz.devices
    for d in range(devices):
        values = depth[d * channels : (d + 1) * channels, :]
        send_ref[d * sz.rows : d * sz.rows + channels, :] = jnp.where(
            is_stick[0:channels], values, carried[0:channels]
        )
    loads[2].wait()
    for al in range(layers):
        turned[...] = jnp.transpose(pot[al])
        for p in range(layers):
            at = channels + al * layers + p
            send_ref[pl.ds(at, devices, stride=sz.rows), :] = turned[
                pl.ds(p, devices, stride=layers), :
            ]
    for at in range(channels + layers * layers, sz.rows):
        send_ref[pl.ds(at, devices, stride=sz.rows), :] = jnp.zeros((devices, LANES), F32)
    bands.wait()


def plane_kernel(sz, recv_ref, fb_ref, fa_ref, ia_ref, ib_ref, orbitals_ref,
                 out_ref, middle_ref,
                 fb, fa, ia, ib, hot_ref, planes, back, group_ref, sems, band_sems):
    bands = BandLoads(orbitals_ref, middle_ref, band_sems, EARLY, MIDDLE)
    bands.start()
    copies = [
        pltpu.make_async_copy(src, dst, sems.at[i])
        for i, (src, dst) in enumerate([(fb_ref, fb), (fa_ref, fa), (ia_ref, ia), (ib_ref, ib)])
    ]
    for c in copies:
        c.start()
    devices, layers, channels = sz.devices, sz.layers, sz.channels
    lane = iota((devices, LANES), 1)
    ids = jnp.full((devices, LANES), -1.0, F32)
    for i in range(sz.id_rows):
        rows = recv_ref[pl.ds(i, devices, stride=sz.rows), :]
        shifted = pltpu.roll(rows, (i * sz.spare - sz.sticks) % LANES, 1)
        mine = (lane >= i * sz.spare) & (lane < min((i + 1) * sz.spare, sz.sticks))
        ids = jnp.where(mine, shifted, ids)
    ids = ids.astype(I32)
    col_a = lax.shift_right_arithmetic(ids, int(math.log2(sz.extent)))
    col_b = ids & (sz.extent - 1)
    sa = (col_a + HALF) & (sz.extent - 1)
    sb = (col_b + HALF) & (sz.extent - 1)
    group = jnp.where(ids >= 0, lax.shift_right_arithmetic(sa, 2), -1)
    cell = (sa & 3) * (2 * HALF) + sb
    group_ref[...] = group
    cell_of = iota((CELLS, LANES), 0)
    left_high, left_low = [], []
    for e in range(devices):
        high, low = split(recv_ref[e * sz.rows : e * sz.rows + SUB, :])
        high, low = high.astype(F32), low.astype(F32)
        here = [jnp.broadcast_to(group[e : e + 1, :], (SUB, LANES)) == g for g in range(GROUPS)]
        for values, side in ((high, left_high), (low, left_low)):
            side.append(
                jnp.concatenate([jnp.where(h, values, 0.0) for h in here], 0).astype(BF16)
            )
        hot_ref[:, e * LANES : (e + 1) * LANES] = ones_where(cell_of == cell[e : e + 1, :]).astype(
            BF16
        )
    left = jnp.concatenate(
        [jnp.concatenate(left_high, 1), jnp.concatenate(left_low, 1)], 0
    )
    spread = dot(left, hot_ref[...], NT)
    size = GROUPS * SUB
    spread = spread[:size] + spread[size:]
    for half in range(2):
        planes[half * size : (half + 1) * size, :] = spread[:, half * LANES : (half + 1) * LANES]

    def plane_part(part, p):
        return planes[pl.ds(part * layers + p, KROWS, stride=SUB), :]

    grid = jnp.concatenate(
        [
            jnp.concatenate([plane_part(part, p) for p in range(layers)], 0)
            for part in range(2)
        ],
        1,
    )
    copies[0].wait()
    grid = dot3(split(grid), (fb[0], fb[1]))
    grid = jnp.concatenate(
        [
            jnp.concatenate(
                [
                    grid[p * KROWS : (p + 1) * KROWS, q * LANES : (q + 1) * LANES]
                    for q in range(4)
                ],
                0,
            )
            for p in range(layers)
        ],
        1,
    )
    copies[1].wait()
    grid = dot3((fa[0], fa[1]), split(grid))
    potential = jnp.concatenate(
        [
            jnp.concatenate(
                [
                    recv_ref[pl.ds(channels + al * layers + p, devices, stride=sz.rows), :]
                    for al in range(layers)
                ],
                0,
            )
            for p in range(layers)
        ],
        1,
    )
    half = sz.extent
    field = jnp.concatenate([grid[0:half] * potential, grid[half:] * potential], 0)
    copies[2].wait()
    grid = dot3((ia[0], ia[1]), split(field))
    grid = jnp.concatenate(
        [
            jnp.concatenate(
                [
                    grid[q * KROWS : (q + 1) * KROWS, p * LANES : (p + 1) * LANES]
                    for q in range(4)
                ],
                1,
            )
            for p in range(layers)
        ],
        0,
    )
    copies[3].wait()
    grid = dot3(split(grid), (ib[0], ib[1]))
    for part in range(2):
        for p in range(layers):
            back[pl.ds(part * layers + p, KROWS, stride=SUB), :] = grid[
                p * KROWS : (p + 1) * KROWS, part * LANES : (part + 1) * LANES
            ]

    values = jnp.concatenate([back[:size, :], back[size:, :]], 1)
    values = jnp.concatenate(split(values), 0)
    for e in range(devices):
        found = dot(values, hot_ref[:, e * LANES : (e + 1) * LANES])
        found = found[:size] + found[size:]
        own = jnp.broadcast_to(group_ref[e : e + 1, :], (SUB, LANES))
        total = jnp.zeros((SUB, LANES), F32)
        for g in range(GROUPS):
            total = total + jnp.where(own == g, found[g * SUB : (g + 1) * SUB, :], 0.0)
        out_ref[e * SUB : (e + 1) * SUB, :] = total
    bands.wait()


def final_kernel(sz, back_ref, cells_ref, window_ref, meta_ref, table_ref, early_ref, middle_ref,
                 orbitals_ref,
                 applied_out, tile_ref,
                 applied_ref, factors, late_ref, acc, band_sems, out_sem):
    done = EARLY + MIDDLE
    bands = BandLoads(orbitals_ref, late_ref, band_sems, done, sz.bands_all - done)
    bands.start()
    devices, layers, rows = sz.devices, sz.layers, sz.slot_rows
    square = (LANES, LANES)
    values = jnp.concatenate(
        [
            back_ref[pl.ds(part * layers + p, devices, stride=SUB), :]
            for part in range(2)
            for p in range(layers)
        ],
        0,
    )
    values = jnp.transpose(values)
    sticks = dot3(split(values), (table_ref[0], table_ref[1]))
    meta_t = meta_ref[...]
    meta = jnp.transpose(jnp.concatenate([meta_t, jnp.zeros((LANES - SUB, LANES), F32)], 0))
    first_row, first_lane, inside = column_facts(meta, sz)
    length = dot(ones_where(inside).astype(BF16), jnp.ones(square, BF16)).astype(I32)
    shift = iota(square, 1) - first_lane.astype(I32)
    top = lax.shift_right_arithmetic(length - 1, 1)
    placed = []
    for turn in range(2):
        p = shift + turn * LANES
        held = (p >= 0) & (p < length)
        depth = jnp.where(p <= top, p, p + sz.extent - length) & (sz.extent - 1)
        placed.append(
            jnp.concatenate(
                [
                    jnp.where(held, pick(sticks[:, q * LANES : (q + 1) * LANES], depth), 0.0)
                    for q in range(2)
                ],
                1,
            )
        )
    placed = split(jnp.concatenate(placed, 0))
    row_t = jnp.broadcast_to(meta_t[2:3, :].astype(I32), (rows, LANES))
    which = iota((rows, LANES), 0)
    hot = jnp.concatenate(
        [ones_where(which == row_t), ones_where(which == row_t + 1)], 1
    ).astype(BF16)
    local = dot(hot, placed[0]) + dot(hot, placed[1])
    cells = cells_ref[...]
    live = cells >= 0
    bits = int(math.log2(sz.extent))
    mask = sz.extent - 1
    fa = signed(lax.shift_right_arithmetic(cells, 2 * bits) & mask, sz.extent)
    fb = signed(lax.shift_right_arithmetic(cells, bits) & mask, sz.extent)
    fc = signed(cells & mask, sz.extent)
    kinetic = (fa * fa + fb * fb + fc * fc).astype(F32) / (RADIUS * RADIUS)
    for part in range(2):
        own = window_ref[part * rows : (part + 1) * rows, :]
        full = kinetic * own + local[:, part * LANES : (part + 1) * LANES]
        applied_ref[part * rows : (part + 1) * rows, :] = jnp.where(live, full, 0.0)
    store = pltpu.make_async_copy(applied_ref, applied_out, out_sem)
    store.start()
    a_re = applied_ref[0:rows, :]
    a_im = applied_ref[rows : 2 * rows, :]
    factors[0] = a_im
    factors[1] = a_re - a_im
    factors[2] = a_re + a_im

    def product_of(source, first, wait=None):
        def product(i, carry):
            if wait is not None:
                wait(i)
            start = pl.multiple_of(i * CHUNK, CHUNK)
            sums = [jnp.zeros((CHUNK, LANES), F32) for _ in range(3)]
            for r in range(rows):
                x = source[0, pl.ds(start, CHUNK), r * LANES : (r + 1) * LANES]
                y = source[1, pl.ds(start, CHUNK), r * LANES : (r + 1) * LANES]
                for q, value in enumerate((x + y, x, y)):
                    sums[q] = sums[q] + value * factors[q, r : r + 1, :]
            acc[0, pl.ds(first + start, CHUNK), :] = sums[0] + sums[1]
            acc[1, pl.ds(first + start, CHUNK), :] = sums[0] - sums[2]
            return carry

        lax.fori_loop(0, source.shape[1] // CHUNK, product, 0)

    product_of(early_ref, 0)
    product_of(middle_ref, EARLY)
    product_of(late_ref, done, bands.wait_one)
    blocks = sz.bands_all // LANES
    block_row = iota((blocks, LANES), 0)
    sums = []
    for part in range(2):
        total = jnp.zeros((blocks, LANES), F32)
        for i in range(blocks):
            hot_row = ones_where(block_row == i).astype(BF16)
            high, low = split(acc[part, i * LANES : (i + 1) * LANES, :])
            total = total + (dot(hot_row, high, NT) + dot(hot_row, low, NT))
        sums.append(total * (1.0 / (sz.slots * sz.devices)))
    width = sz.band_rows
    per_row = LANES // width
    lane = iota((blocks, LANES), 1)
    for q in range(per_row):
        real = pltpu.roll(sums[0], (-q * width) % LANES, 1)
        imag = pltpu.roll(sums[1], (width - q * width) % LANES, 1)
        tile_ref[pl.ds(q, blocks, stride=per_row), :] = jnp.where(lane < width, real, imag)
    store.wait()


def sum_kernel(sz, tile_ref, out_ref):
    width = sz.band_rows
    total = jnp.sum(tile_ref[...], axis=0, keepdims=True)
    for part in range(2):
        out_ref[part, :, :] = total[:, part * width : (part + 1) * width]


def full_spec():
    return pl.BlockSpec(memory_space=pltpu.VMEM)


def any_spec():
    return pl.BlockSpec(memory_space=pl.ANY)


def vmem(mib):
    return pltpu.CompilerParams(vmem_limit_bytes=mib << 20)


def run_spread(sz, cells, orbitals, potential, table, **kw):
    return pl.pallas_call(
        lambda *refs: spread_kernel(sz, *refs),
        out_shape=(
            jax.ShapeDtypeStruct((sz.devices * sz.rows, LANES), F32),
            jax.ShapeDtypeStruct((2 * sz.slot_rows, LANES), F32),
            jax.ShapeDtypeStruct((SUB, LANES), F32),
            pltpu.VMEM((2, EARLY, sz.slots), F32),
        ),
        in_specs=[any_spec()] * 4,
        out_specs=(full_spec(),) * 4,
        scratch_shapes=[
            pltpu.VMEM((sz.slot_rows, LANES), I32),
            pltpu.VMEM((2, SUB, sz.slots), F32),
            pltpu.VMEM((sz.layers, LANES, LANES), F32),
            pltpu.VMEM(table.shape, BF16),
            pltpu.VMEM((LANES, LANES), F32),
            pltpu.SemaphoreType.DMA((4,)),
            pltpu.SemaphoreType.DMA((EARLY // CHUNK,)),
        ],
        name="spread",
        compiler_params=vmem(8),
        **kw,
    )(cells, orbitals, potential, table)


def run_planes(sz, recv, tabs, orbitals, **kw):
    mats = [tabs[n] for n in ("forward_b", "forward_a", "inverse_a", "inverse_b")]
    return pl.pallas_call(
        lambda *refs: plane_kernel(sz, *refs),
        out_shape=(
            jax.ShapeDtypeStruct((sz.devices * SUB, LANES), F32),
            pltpu.VMEM((2, MIDDLE, sz.slots), F32),
        ),
        in_specs=[full_spec()] + [any_spec()] * 5,
        out_specs=(full_spec(), full_spec()),
        scratch_shapes=[pltpu.VMEM(m.shape, BF16) for m in mats]
        + [
            pltpu.VMEM((CELLS, sz.devices * LANES), BF16),
            pltpu.VMEM((KROWS * SUB, LANES), F32),
            pltpu.VMEM((KROWS * SUB, LANES), F32),
            pltpu.VMEM((sz.devices, LANES), I32),
            pltpu.SemaphoreType.DMA((4,)),
            pltpu.SemaphoreType.DMA((MIDDLE // CHUNK,)),
        ],
        name="planes",
        compiler_params=vmem(16),
        **kw,
    )(recv, *mats, orbitals)


def run_final(sz, back, cells, window, meta, table, early, middle, orbitals, **kw):
    late = sz.bands_all - EARLY - MIDDLE
    return pl.pallas_call(
        lambda *refs: final_kernel(sz, *refs),
        out_shape=(
            jax.ShapeDtypeStruct((2 * sz.slot_rows, LANES), F32),
            jax.ShapeDtypeStruct((sz.devices, LANES), F32),
        ),
        in_specs=[full_spec()] * 7 + [any_spec()],
        out_specs=(any_spec(), full_spec()),
        scratch_shapes=[
            pltpu.VMEM((2 * sz.slot_rows, LANES), F32),
            pltpu.VMEM((3, sz.slot_rows, LANES), F32),
            pltpu.VMEM((2, late, sz.slots), F32),
            pltpu.VMEM((2, sz.bands_all, LANES), F32),
            pltpu.SemaphoreType.DMA((late // CHUNK,)),
            pltpu.SemaphoreType.DMA,
        ],
        name="final",
        compiler_params=vmem(20),
        **kw,
    )(back, cells, window, meta, table, early, middle, orbitals)


def run_sum(sz, tile, **kw):
    return pl.pallas_call(
        lambda *refs: sum_kernel(sz, *refs),
        out_shape=jax.ShapeDtypeStruct((2, 1, sz.band_rows), F32),
        in_specs=[full_spec()],
        out_specs=full_spec(),
        name="add",
        compiler_params=vmem(2),
        **kw,
    )(tile)


def exchange(x):
    return lax.all_to_all(x, "ga", split_axis=0, concat_axis=0, tiled=True)


def local(orbitals, coeff_cells, potential):
    devices = lax.axis_size("ga")
    sz = Sizes(devices, potential.shape[1], coeff_cells.shape[0], orbitals.shape[1])
    tabs = {name: jnp.asarray(value) for name, value in tables(sz).items()}
    cells = coeff_cells.reshape(sz.slot_rows, LANES)
    stay = lambda x: pltpu.with_memory_space_constraint(x, pltpu.HBM)
    orbitals = stay(orbitals)
    send, window, meta, early = run_spread(
        sz, stay(cells), orbitals, stay(potential), stay(tabs["forward_z"])
    )
    back, middle = run_planes(sz, exchange(send), tabs, orbitals)
    applied, tile = run_final(
        sz, exchange(back), cells, window, meta, tabs["inverse_z"], early, middle, orbitals
    )
    subspace = run_sum(sz, exchange(tile))
    return (
        applied.reshape(2, 1, sz.slots),
        jnp.transpose(subspace, (2, 0, 1)),
    )


def solution(mesh):
    in_specs = (P(None, "kpt", "ga"), P("ga"), P("ga", None, None))
    out_specs = (P(None, "kpt", "ga"), P("ga", None, "kpt"))
    return jax.shard_map(local, mesh=mesh, in_specs=in_specs, out_specs=out_specs, check_vma=False)
```

```python
import math

import jax
import jax.numpy as jnp
import numpy as np
from jax import lax
from jax.experimental import pallas as pl
from jax.experimental.pallas import tpu as pltpu
from jax.sharding import PartitionSpec as P

RADIUS = 30
LANES = 128
SUB = 8
HALF = 32
KROWS = 32
CELLS = 4 * 2 * HALF
GROUPS = KROWS // 2
CHUNK = 64
EARLY = 128
MIDDLE = 384
F32 = jnp.float32
BF16 = jnp.bfloat16
I32 = jnp.int32

NT = ((1,), (1,))
NN = ((1,), (0,))


def column_total(extent):
    indices = np.arange(extent)
    frequency = np.where(indices < extent // 2, indices, indices - extent)
    return int(np.sum(frequency[:, None] ** 2 + frequency[None, :] ** 2 <= RADIUS * RADIUS))


def packing(items, width):
    spare = LANES - width
    base = next(b for b in range(1, items + 1) if (items - b) * width <= b * spare)
    pieces = []
    row, at = 0, width
    for item in range(base, items):
        done = 0
        while done < width:
            if at == LANES:
                row, at = row + 1, width
            length = min(width - done, LANES - at)
            pieces.append((item, done, row, at, length))
            done, at = done + length, at + length
    return base, pieces


def pack_row(row, load, pieces):
    value = load(row)
    lane = lax.broadcasted_iota(I32, value.shape, 1)
    for item, source, target_row, target, length in pieces:
        if target_row == row:
            moved = pltpu.roll(load(item), (target - source) % LANES, 1)
            value = jnp.where((lane >= target) & (lane < target + length), moved, value)
    return value


def unpack_item(item, base, load, pieces):
    if item < base:
        return load(item)
    value = None
    for owner, source, row, at, length in pieces:
        if owner == item:
            moved = pltpu.roll(load(row), (source - at) % LANES, 1)
            lane = lax.broadcasted_iota(I32, moved.shape, 1)
            value = moved if value is None else jnp.where(lane >= source, moved, value)
    return value


class Sizes:
    def __init__(self, devices, extent, slots, bands_all):
        self.devices = devices
        self.extent = extent
        self.layers = extent // devices
        self.channels = 2 * self.layers
        self.slot_rows = slots // LANES
        self.slots = slots
        self.sticks = -(-column_total(extent) // devices)
        self.out_rows, self.out_pieces = packing(self.channels + 1, self.sticks)
        self.back_rows, self.back_pieces = packing(self.channels, self.sticks)
        self.rows = self.out_rows + self.layers * self.layers
        self.bands_all = bands_all
        self.band_rows = bands_all // devices
        assert extent == LANES and self.channels <= SUB


def parts_of(matrix):
    values = np.asarray(matrix, np.float32)
    high = values.astype(jnp.bfloat16)
    low = (values - high.astype(np.float32)).astype(jnp.bfloat16)
    return np.stack([high, low])


def angle(x, y, extent):
    phase = (x[:, None] * y[None, :]) % extent
    return 2.0 * math.pi * phase.astype(np.float64) / extent


def tables(sz):
    n, d, layers = sz.extent, sz.devices, sz.layers
    cells = np.arange(n)
    dev, part, lay = np.meshgrid(np.arange(d), np.arange(2), np.arange(layers), indexing="ij")
    z_rows = (dev * layers + lay).reshape(-1)
    part_rows = part.reshape(-1)
    t = angle(z_rows, cells, n)
    re, im = np.cos(t), np.sin(t)
    is_im = part_rows[:, None] == 1
    forward_z = np.concatenate([np.where(is_im, im, re), np.where(is_im, re, -im)], 1)
    freq = np.arange(2 * HALF) - HALF
    tb = angle(freq, cells, n)
    cb, sb = np.cos(tb), np.sin(tb)
    eye = np.eye(2)
    cc, ss = np.kron(eye, cb), np.kron(eye, sb)
    forward_b = np.block([[cc, ss], [-ss, cc]])
    cct, sst = cc.T, ss.T
    inverse_b = np.block([[cct, -sst], [sst, cct]])
    a_rows = (np.arange(d)[None, :] * layers + np.arange(layers)[:, None]).reshape(-1)
    lo, k = np.meshgrid(np.arange(2), np.arange(KROWS), indexing="ij")
    a_freq = (4 * (k % GROUPS) + 2 * (k // GROUPS) + lo - HALF).reshape(-1)
    ta = angle(a_rows, a_freq, n)
    ca, sa = np.cos(ta), np.sin(ta)
    forward_a = np.block([[ca, -sa], [sa, ca]])
    inverse_a = np.block([[ca.T, sa.T], [-sa.T, ca.T]])
    part2, lay2, dev2 = np.meshgrid(np.arange(2), np.arange(layers), np.arange(d), indexing="ij")
    t2 = angle((dev2 * layers + lay2).reshape(-1), cells, n)
    re2, im2 = np.cos(t2) / n**3, np.sin(t2) / n**3
    im_rows = part2.reshape(-1)[:, None] == 1
    inverse_z = np.concatenate([np.where(im_rows, im2, re2), np.where(im_rows, re2, -im2)], 1)
    return {
        "forward_z": parts_of(forward_z),
        "forward_b": parts_of(forward_b),
        "forward_a": parts_of(forward_a),
        "inverse_a": parts_of(inverse_a),
        "inverse_b": parts_of(inverse_b),
        "inverse_z": parts_of(inverse_z),
    }


def split(x):
    high = x.astype(BF16)
    return high, (x - high.astype(F32)).astype(BF16)


def dot(a, b, dims=NN):
    return lax.dot_general(a, b, (dims, ((), ())), preferred_element_type=F32)


def dot3(a, b, dims=NN):
    return dot(a[0], b[0], dims) + dot(a[0], b[1], dims) + dot(a[1], b[0], dims)


def iota(shape, dim):
    return lax.broadcasted_iota(I32, shape, dim)


def ones_where(mask):
    return jnp.where(mask, 1.0, 0.0).astype(F32)


def pick(values, lanes):
    return jnp.take_along_axis(values, lanes, axis=1, mode="promise_in_bounds")


def signed(x, extent):
    return jnp.where(x < extent // 2, x, x - extent)


def column_facts(meta, sz):
    shape = (LANES, LANES)
    col_a = jnp.broadcast_to(meta[:, 0:1], shape)
    col_b = jnp.broadcast_to(meta[:, 1:2], shape)
    row = jnp.broadcast_to(meta[:, 2:3], shape)
    lane = jnp.broadcast_to(meta[:, 3:4], shape)
    valid = jnp.broadcast_to(meta[:, 4:5], shape) > 0.5
    fa = jnp.where(col_a < sz.extent // 2, col_a, col_a - sz.extent)
    fb = jnp.where(col_b < sz.extent // 2, col_b, col_b - sz.extent)
    fc = signed(iota(shape, 1), sz.extent).astype(F32)
    inside = valid & (fc * fc <= RADIUS * RADIUS - fa * fa - fb * fb)
    return row, lane, inside


class BandLoads:
    def __init__(self, source, target, sems, first, count):
        self.refs = (source, target, sems, first)
        self.count = count // CHUNK

    def copy(self, i):
        source, target, sems, first = self.refs
        return pltpu.make_async_copy(
            source.at[:, pl.ds(first + i * CHUNK, CHUNK), :],
            target.at[:, pl.ds(i * CHUNK, CHUNK), :],
            sems.at[i],
        )

    def start(self):
        for i in range(self.count):
            self.copy(i).start()

    def wait_one(self, i):
        self.copy(i).wait()

    def wait(self):
        for i in range(self.count):
            self.copy(i).wait()


def spread_kernel(sz, cells_ref, orbitals_ref, potential_ref, table_ref,
                  send_ref, window_ref, meta_ref, early_ref,
                  cells_in, block, pot, table, turned, rows_ref, sems, band_sems):
    loads = [
        pltpu.make_async_copy(orbitals_ref.at[:, pl.ds(0, SUB), :], block, sems.at[0]),
        pltpu.make_async_copy(table_ref, table, sems.at[1]),
        pltpu.make_async_copy(potential_ref, pot, sems.at[2]),
    ]
    cell_load = pltpu.make_async_copy(cells_ref, cells_in, sems.at[3])
    cell_load.start()
    for load in loads:
        load.start()
    bands = BandLoads(orbitals_ref, early_ref, band_sems, 0, EARLY)
    bands.start()
    cell_load.wait()
    rows = sz.slot_rows
    shape = (rows, LANES)
    cells = cells_in[...]
    live = cells >= 0
    column = lax.shift_right_arithmetic(cells, int(math.log2(sz.extent)))
    rolled = pltpu.roll(column, 1, 1)
    above = pltpu.roll(rolled, 1, 0)
    lane = iota(shape, 1)
    row = iota(shape, 0)
    before = jnp.where(lane == 0, jnp.where(row == 0, -1, above), rolled)
    starts = live & (column != before)
    flags = ones_where(starts).astype(BF16)
    square = (LANES, LANES)
    upto = ones_where(iota(square, 0) <= iota(square, 1)).astype(BF16)
    all_ones = jnp.ones(square, BF16)
    within = dot(flags, upto)
    totals = dot(flags, all_ones)
    lower = ones_where(iota((rows, rows), 1) < iota((rows, rows), 0)).astype(BF16)
    rank = (within + dot(lower, totals.astype(BF16))).astype(I32) - 1
    rank = jnp.where(starts, rank, -1)
    col_a = lax.shift_right_arithmetic(column, int(math.log2(sz.extent)))
    col_b = column & (sz.extent - 1)
    sub = iota((SUB, LANES), 0)
    lane8 = iota((SUB, LANES), 1)
    place = iota(square, 0)
    hots, facts = [], []
    for r in range(rows):
        hots.append(ones_where(place == rank[r : r + 1, :]).astype(BF16))
        fact = jnp.where(sub == 0, col_a[r : r + 1, :], col_b[r : r + 1, :])
        fact = jnp.where(sub == 2, r, fact)
        fact = jnp.where(sub == 3, lane8, fact)
        fact = jnp.where(sub == 4, 1, fact)
        facts.append(fact.astype(F32).astype(BF16))
    meta_t = dot(jnp.concatenate(facts, 1), jnp.concatenate(hots, 1), NT)
    meta_ref[...] = meta_t
    meta = jnp.transpose(jnp.concatenate([meta_t, jnp.zeros((LANES - SUB, LANES), F32)], 0))
    first_row, first_lane, inside = column_facts(meta, sz)
    hot = ones_where(inside).astype(BF16)
    before_in = ones_where(iota(square, 0) < iota(square, 1)).astype(BF16)
    slot = (first_lane + dot(hot, before_in)).astype(I32)
    second = slot >= LANES
    slot_lane = slot & (LANES - 1)

    loads[0].wait()
    for r in range(rows):
        window_ref[r : r + 1, :] = block[0, 0:1, r * LANES : (r + 1) * LANES]
        window_ref[rows + r : rows + r + 1, :] = block[1, 0:1, r * LANES : (r + 1) * LANES]
    window = jnp.concatenate([window_ref[0:rows, :], window_ref[rows : 2 * rows, :]], 1)
    high, low = split(window)
    row_of = first_row.astype(I32)[:, 0:rows]
    which = iota((LANES, rows), 1)
    near = ones_where(which == row_of).astype(BF16)
    far = ones_where(which == row_of + 1).astype(BF16)
    near_w = dot(near, high) + dot(near, low)
    far_w = dot(far, high) + dot(far, low)
    sticks = []
    for part in range(2):
        cut = slice(part * LANES, (part + 1) * LANES)
        value = jnp.where(second, pick(far_w[:, cut], slot_lane), pick(near_w[:, cut], slot_lane))
        sticks.append(jnp.where(inside, value, 0.0))
    sticks = jnp.concatenate(sticks, 1)
    loads[1].wait()
    depth = dot3((table[0], table[1]), split(sticks), NT)

    channels, layers, devices = sz.channels, sz.layers, sz.devices
    ids = jnp.where(
        meta_t[4:5, :] > 0.5, meta_t[0:1, :] * sz.extent + meta_t[1:2, :], -1.0
    )
    ids = jnp.broadcast_to(ids, (devices, LANES))
    rows_ref[...] = depth

    def item(i):
        return ids if i == channels else rows_ref[pl.ds(i, devices, stride=channels), :]

    for r in range(sz.out_rows):
        send_ref[pl.ds(r, devices, stride=sz.rows), :] = pack_row(r, item, sz.out_pieces)
    loads[2].wait()
    for al in range(layers):
        turned[...] = jnp.transpose(pot[al])
        for p in range(layers):
            at = sz.out_rows + al * layers + p
            send_ref[pl.ds(at, devices, stride=sz.rows), :] = turned[
                pl.ds(p, devices, stride=layers), :
            ]
    bands.wait()


def plane_kernel(sz, recv_ref, fb_ref, fa_ref, ia_ref, ib_ref, orbitals_ref,
                 out_ref, middle_ref,
                 fb, fa, ia, ib, hot_ref, planes, back, group_ref, z_ref, sems, band_sems):
    bands = BandLoads(orbitals_ref, middle_ref, band_sems, EARLY, MIDDLE)
    bands.start()
    copies = [
        pltpu.make_async_copy(src, dst, sems.at[i])
        for i, (src, dst) in enumerate([(fb_ref, fb), (fa_ref, fa), (ia_ref, ia), (ib_ref, ib)])
    ]
    for c in copies:
        c.start()
    devices, layers, channels = sz.devices, sz.layers, sz.channels

    def recv_row(r):
        return recv_ref[pl.ds(r, devices, stride=sz.rows), :]

    def recv_item(i):
        return unpack_item(i, sz.out_rows, recv_row, sz.out_pieces)

    lane = iota((devices, LANES), 1)
    ids = jnp.where(lane < sz.sticks, recv_item(channels), -1.0).astype(I32)
    if channels < SUB:
        z_ref[...] = jnp.zeros(z_ref.shape, F32)
    for i in range(channels):
        z_ref[pl.ds(i, devices, stride=SUB), :] = recv_item(i)
    col_a = lax.shift_right_arithmetic(ids, int(math.log2(sz.extent)))
    col_b = ids & (sz.extent - 1)
    sa = (col_a + HALF) & (sz.extent - 1)
    sb = (col_b + HALF) & (sz.extent - 1)
    group = jnp.where(ids >= 0, lax.shift_right_arithmetic(sa, 2), -1)
    cell = (sa & 3) * (2 * HALF) + sb
    group_ref[...] = group
    two = (2 * SUB, LANES)
    cell_rows = [(iota(two, 0) + i).astype(F32).astype(BF16) for i in range(0, CELLS, 2 * SUB)]
    group_rows = [
        (lax.shift_right_logical(iota(two, 0), 3) + g).astype(F32).astype(BF16)
        for g in range(0, GROUPS, 2)
    ]
    one, zero = jnp.ones(two, BF16), jnp.zeros(two, BF16)
    cell, group_f = cell.astype(F32), group.astype(F32)
    left_high, left_low = [], []
    for e in range(devices):
        own_cell = jnp.broadcast_to(cell[e : e + 1, :], two).astype(BF16)
        own_group = jnp.broadcast_to(group_f[e : e + 1, :], two).astype(BF16)
        values = z_ref[e * SUB : (e + 1) * SUB, :]
        high, low = split(jnp.concatenate([values, values], 0))
        here = [own_group == g for g in group_rows]
        left_high.append(jnp.concatenate([jnp.where(h, high, zero) for h in here], 0))
        left_low.append(jnp.concatenate([jnp.where(h, low, zero) for h in here], 0))
        for i, rows in enumerate(cell_rows):
            hot_ref[2 * SUB * i : 2 * SUB * (i + 1), e * LANES : (e + 1) * LANES] = jnp.where(
                own_cell == rows, one, zero
            )
    left = jnp.concatenate(
        [jnp.concatenate(left_high, 1), jnp.concatenate(left_low, 1)], 0
    )
    spread = dot(left, hot_ref[...], NT)
    size = GROUPS * SUB
    spread = spread[:size] + spread[size:]
    for half in range(2):
        planes[half * size : (half + 1) * size, :] = spread[:, half * LANES : (half + 1) * LANES]

    def plane_part(part, p):
        return planes[pl.ds(part * layers + p, KROWS, stride=SUB), :]

    grid = jnp.concatenate(
        [
            jnp.concatenate([plane_part(part, p) for p in range(layers)], 0)
            for part in range(2)
        ],
        1,
    )
    copies[0].wait()
    grid = dot3(split(grid), (fb[0], fb[1]))
    grid = jnp.concatenate(
        [
            jnp.concatenate(
                [
                    grid[p * KROWS : (p + 1) * KROWS, q * LANES : (q + 1) * LANES]
                    for q in range(4)
                ],
                0,
            )
            for p in range(layers)
        ],
        1,
    )
    copies[1].wait()
    grid = dot3((fa[0], fa[1]), split(grid))
    potential = jnp.concatenate(
        [
            jnp.concatenate(
                [
                    recv_row(sz.out_rows + al * layers + p)
                    for al in range(layers)
                ],
                0,
            )
            for p in range(layers)
        ],
        1,
    )
    half = sz.extent
    field = jnp.concatenate([grid[0:half] * potential, grid[half:] * potential], 0)
    copies[2].wait()
    grid = dot3((ia[0], ia[1]), split(field))
    grid = jnp.concatenate(
        [
            jnp.concatenate(
                [
                    grid[q * KROWS : (q + 1) * KROWS, p * LANES : (p + 1) * LANES]
                    for q in range(4)
                ],
                1,
            )
            for p in range(layers)
        ],
        0,
    )
    copies[3].wait()
    grid = dot3(split(grid), (ib[0], ib[1]))
    for part in range(2):
        for p in range(layers):
            back[pl.ds(part * layers + p, KROWS, stride=SUB), :] = grid[
                p * KROWS : (p + 1) * KROWS, part * LANES : (part + 1) * LANES
            ]

    values = jnp.concatenate([back[:size, :], back[size:, :]], 1)
    values = jnp.concatenate(split(values), 0)
    for e in range(devices):
        found = dot(values, hot_ref[:, e * LANES : (e + 1) * LANES])
        found = found[:size] + found[size:]
        own = jnp.broadcast_to(group_ref[e : e + 1, :], (SUB, LANES))
        total = jnp.zeros((SUB, LANES), F32)
        for g in range(GROUPS):
            total = total + jnp.where(own == g, found[g * SUB : (g + 1) * SUB, :], 0.0)
        z_ref[e * SUB : (e + 1) * SUB, :] = total

    def back_item(i):
        return z_ref[pl.ds(i, devices, stride=SUB), :]

    for r in range(sz.back_rows):
        out_ref[pl.ds(r, devices, stride=sz.back_rows), :] = pack_row(
            r, back_item, sz.back_pieces
        )
    bands.wait()


def final_kernel(sz, back_ref, cells_ref, window_ref, meta_ref, table_ref, early_ref, middle_ref,
                 orbitals_ref,
                 applied_out, tile_ref,
                 applied_ref, factors, late_ref, acc, band_sems, out_sem):
    done = EARLY + MIDDLE
    bands = BandLoads(orbitals_ref, late_ref, band_sems, done, sz.bands_all - done)
    bands.start()
    devices, layers, rows = sz.devices, sz.layers, sz.slot_rows
    square = (LANES, LANES)

    def back_row(r):
        return back_ref[pl.ds(r, devices, stride=sz.back_rows), :]

    values = jnp.concatenate(
        [
            unpack_item(i, sz.back_rows, back_row, sz.back_pieces)
            for i in range(sz.channels)
        ],
        0,
    )
    values = jnp.transpose(values)
    sticks = dot3(split(values), (table_ref[0], table_ref[1]))
    meta_t = meta_ref[...]
    meta = jnp.transpose(jnp.concatenate([meta_t, jnp.zeros((LANES - SUB, LANES), F32)], 0))
    first_row, first_lane, inside = column_facts(meta, sz)
    length = dot(ones_where(inside).astype(BF16), jnp.ones(square, BF16)).astype(I32)
    shift = iota(square, 1) - first_lane.astype(I32)
    top = lax.shift_right_arithmetic(length - 1, 1)
    placed = []
    for turn in range(2):
        p = shift + turn * LANES
        held = (p >= 0) & (p < length)
        depth = jnp.where(p <= top, p, p + sz.extent - length) & (sz.extent - 1)
        placed.append(
            jnp.concatenate(
                [
                    jnp.where(held, pick(sticks[:, q * LANES : (q + 1) * LANES], depth), 0.0)
                    for q in range(2)
                ],
                1,
            )
        )
    placed = split(jnp.concatenate(placed, 0))
    row_t = jnp.broadcast_to(meta_t[2:3, :].astype(I32), (rows, LANES))
    which = iota((rows, LANES), 0)
    hot = jnp.concatenate(
        [ones_where(which == row_t), ones_where(which == row_t + 1)], 1
    ).astype(BF16)
    local = dot(hot, placed[0]) + dot(hot, placed[1])
    cells = cells_ref[...]
    live = cells >= 0
    bits = int(math.log2(sz.extent))
    mask = sz.extent - 1
    fa = signed(lax.shift_right_arithmetic(cells, 2 * bits) & mask, sz.extent)
    fb = signed(lax.shift_right_arithmetic(cells, bits) & mask, sz.extent)
    fc = signed(cells & mask, sz.extent)
    kinetic = (fa * fa + fb * fb + fc * fc).astype(F32) / (RADIUS * RADIUS)
    for part in range(2):
        own = window_ref[part * rows : (part + 1) * rows, :]
        full = kinetic * own + local[:, part * LANES : (part + 1) * LANES]
        applied_ref[part * rows : (part + 1) * rows, :] = jnp.where(live, full, 0.0)
    store = pltpu.make_async_copy(applied_ref, applied_out, out_sem)
    store.start()
    a_re = applied_ref[0:rows, :]
    a_im = applied_ref[rows : 2 * rows, :]
    factors[0] = a_im
    factors[1] = a_re - a_im
    factors[2] = a_re + a_im

    def product_of(source, first, wait=None):
        def product(i, carry):
            if wait is not None:
                wait(i)
            start = pl.multiple_of(i * CHUNK, CHUNK)
            sums = [jnp.zeros((CHUNK, LANES), F32) for _ in range(3)]
            for r in range(rows):
                x = source[0, pl.ds(start, CHUNK), r * LANES : (r + 1) * LANES]
                y = source[1, pl.ds(start, CHUNK), r * LANES : (r + 1) * LANES]
                for q, value in enumerate((x + y, x, y)):
                    sums[q] = sums[q] + value * factors[q, r : r + 1, :]
            acc[0, pl.ds(first + start, CHUNK), :] = sums[0] + sums[1]
            acc[1, pl.ds(first + start, CHUNK), :] = sums[0] - sums[2]
            return carry

        lax.fori_loop(0, source.shape[1] // CHUNK, product, 0)

    product_of(early_ref, 0)
    product_of(middle_ref, EARLY)
    product_of(late_ref, done, bands.wait_one)
    blocks = sz.bands_all // LANES
    block_row = iota((blocks, LANES), 0)
    sums = []
    for part in range(2):
        total = jnp.zeros((blocks, LANES), F32)
        for i in range(blocks):
            hot_row = ones_where(block_row == i).astype(BF16)
            high, low = split(acc[part, i * LANES : (i + 1) * LANES, :])
            total = total + (dot(hot_row, high, NT) + dot(hot_row, low, NT))
        sums.append(total * (1.0 / (sz.slots * sz.devices)))
    width = sz.band_rows
    per_row = LANES // width
    lane = iota((blocks, LANES), 1)
    for q in range(per_row):
        real = pltpu.roll(sums[0], (-q * width) % LANES, 1)
        imag = pltpu.roll(sums[1], (width - q * width) % LANES, 1)
        tile_ref[pl.ds(q, blocks, stride=per_row), :] = jnp.where(lane < width, real, imag)
    store.wait()


def sum_kernel(sz, tile_ref, out_ref):
    width = sz.band_rows
    total = jnp.sum(tile_ref[...], axis=0, keepdims=True)
    for part in range(2):
        out_ref[part, :, :] = total[:, part * width : (part + 1) * width]


def full_spec():
    return pl.BlockSpec(memory_space=pltpu.VMEM)


def any_spec():
    return pl.BlockSpec(memory_space=pl.ANY)


def vmem(mib):
    return pltpu.CompilerParams(vmem_limit_bytes=mib << 20)


def run_spread(sz, cells, orbitals, potential, table, **kw):
    return pl.pallas_call(
        lambda *refs: spread_kernel(sz, *refs),
        out_shape=(
            jax.ShapeDtypeStruct((sz.devices * sz.rows, LANES), F32),
            jax.ShapeDtypeStruct((2 * sz.slot_rows, LANES), F32),
            jax.ShapeDtypeStruct((SUB, LANES), F32),
            pltpu.VMEM((2, EARLY, sz.slots), F32),
        ),
        in_specs=[any_spec()] * 4,
        out_specs=(full_spec(),) * 4,
        scratch_shapes=[
            pltpu.VMEM((sz.slot_rows, LANES), I32),
            pltpu.VMEM((2, SUB, sz.slots), F32),
            pltpu.VMEM((sz.layers, LANES, LANES), F32),
            pltpu.VMEM(table.shape, BF16),
            pltpu.VMEM((LANES, LANES), F32),
            pltpu.VMEM((sz.devices * sz.channels, LANES), F32),
            pltpu.SemaphoreType.DMA((4,)),
            pltpu.SemaphoreType.DMA((EARLY // CHUNK,)),
        ],
        name="spread",
        compiler_params=vmem(8),
        **kw,
    )(cells, orbitals, potential, table)


def run_planes(sz, recv, tabs, orbitals, **kw):
    mats = [tabs[n] for n in ("forward_b", "forward_a", "inverse_a", "inverse_b")]
    return pl.pallas_call(
        lambda *refs: plane_kernel(sz, *refs),
        out_shape=(
            jax.ShapeDtypeStruct((sz.devices * sz.back_rows, LANES), F32),
            pltpu.VMEM((2, MIDDLE, sz.slots), F32),
        ),
        in_specs=[full_spec()] + [any_spec()] * 5,
        out_specs=(full_spec(), full_spec()),
        scratch_shapes=[pltpu.VMEM(m.shape, BF16) for m in mats]
        + [
            pltpu.VMEM((CELLS, sz.devices * LANES), BF16),
            pltpu.VMEM((KROWS * SUB, LANES), F32),
            pltpu.VMEM((KROWS * SUB, LANES), F32),
            pltpu.VMEM((sz.devices, LANES), I32),
            pltpu.VMEM((sz.devices * SUB, LANES), F32),
            pltpu.SemaphoreType.DMA((4,)),
            pltpu.SemaphoreType.DMA((MIDDLE // CHUNK,)),
        ],
        name="planes",
        compiler_params=vmem(16),
        **kw,
    )(recv, *mats, orbitals)


def run_final(sz, back, cells, window, meta, table, early, middle, orbitals, **kw):
    late = sz.bands_all - EARLY - MIDDLE
    return pl.pallas_call(
        lambda *refs: final_kernel(sz, *refs),
        out_shape=(
            jax.ShapeDtypeStruct((2 * sz.slot_rows, LANES), F32),
            jax.ShapeDtypeStruct((sz.devices, LANES), F32),
        ),
        in_specs=[full_spec()] * 7 + [any_spec()],
        out_specs=(any_spec(), full_spec()),
        scratch_shapes=[
            pltpu.VMEM((2 * sz.slot_rows, LANES), F32),
            pltpu.VMEM((3, sz.slot_rows, LANES), F32),
            pltpu.VMEM((2, late, sz.slots), F32),
            pltpu.VMEM((2, sz.bands_all, LANES), F32),
            pltpu.SemaphoreType.DMA((late // CHUNK,)),
            pltpu.SemaphoreType.DMA,
        ],
        name="final",
        compiler_params=vmem(20),
        **kw,
    )(back, cells, window, meta, table, early, middle, orbitals)


def run_sum(sz, tile, **kw):
    return pl.pallas_call(
        lambda *refs: sum_kernel(sz, *refs),
        out_shape=jax.ShapeDtypeStruct((2, 1, sz.band_rows), F32),
        in_specs=[full_spec()],
        out_specs=full_spec(),
        name="add",
        compiler_params=vmem(2),
        **kw,
    )(tile)


def exchange(x):
    rows = x.reshape(x.shape[0], 1, x.shape[1])
    return lax.all_to_all(rows, "ga", split_axis=0, concat_axis=0, tiled=True).reshape(x.shape)


def local(orbitals, coeff_cells, potential):
    devices = lax.axis_size("ga")
    sz = Sizes(devices, potential.shape[1], coeff_cells.shape[0], orbitals.shape[1])
    tabs = {name: jnp.asarray(value) for name, value in tables(sz).items()}
    cells = coeff_cells.reshape(sz.slot_rows, LANES)
    stay = lambda x: pltpu.with_memory_space_constraint(x, pltpu.HBM)
    orbitals = stay(orbitals)
    send, window, meta, early = run_spread(
        sz, stay(cells), orbitals, stay(potential), stay(tabs["forward_z"])
    )
    back, middle = run_planes(sz, exchange(send), tabs, orbitals)
    applied, tile = run_final(
        sz, exchange(back), cells, window, meta, tabs["inverse_z"], early, middle, orbitals
    )
    subspace = run_sum(sz, exchange(tile))
    return (
        applied.reshape(2, 1, sz.slots),
        jnp.transpose(subspace, (2, 0, 1)),
    )


def solution(mesh):
    in_specs = (P(None, "kpt", "ga"), P("ga"), P("ga", None, None))
    out_specs = (P(None, "kpt", "ga"), P("ga", None, "kpt"))
    return jax.shard_map(local, mesh=mesh, in_specs=in_specs, out_specs=out_specs, check_vma=False)
```

```python
import math

import jax
import jax.numpy as jnp
import numpy as np
from jax import lax
from jax.experimental import pallas as pl
from jax.experimental.pallas import tpu as pltpu
from jax.sharding import PartitionSpec as P

RADIUS = 30
LANES = 128
SUB = 8
HALF = 32
KROWS = 32
CELLS = 4 * 2 * HALF
GROUPS = KROWS // 2
CHUNK = 64
EARLY = 128
MIDDLE = 320
F32 = jnp.float32
BF16 = jnp.bfloat16
I32 = jnp.int32

NT = ((1,), (1,))
NN = ((1,), (0,))


def column_total(extent):
    indices = np.arange(extent)
    frequency = np.where(indices < extent // 2, indices, indices - extent)
    return int(np.sum(frequency[:, None] ** 2 + frequency[None, :] ** 2 <= RADIUS * RADIUS))


def packing(items, width):
    spare = LANES - width
    base = next(b for b in range(1, items + 1) if (items - b) * width <= b * spare)
    pieces = []
    row, at = 0, width
    for item in range(base, items):
        done = 0
        while done < width:
            if at == LANES:
                row, at = row + 1, width
            length = min(width - done, LANES - at)
            pieces.append((item, done, row, at, length))
            done, at = done + length, at + length
    return base, pieces


def pack_row(row, load, pieces):
    value = load(row)
    lane = lax.broadcasted_iota(I32, value.shape, 1)
    for item, source, target_row, target, length in pieces:
        if target_row == row:
            moved = pltpu.roll(load(item), (target - source) % LANES, 1)
            value = jnp.where((lane >= target) & (lane < target + length), moved, value)
    return value


def unpack_item(item, base, load, pieces):
    if item < base:
        return load(item)
    value = None
    for owner, source, row, at, length in pieces:
        if owner == item:
            moved = pltpu.roll(load(row), (source - at) % LANES, 1)
            lane = lax.broadcasted_iota(I32, moved.shape, 1)
            value = moved if value is None else jnp.where(lane >= source, moved, value)
    return value


class Sizes:
    def __init__(self, devices, extent, slots, bands_all):
        self.devices = devices
        self.extent = extent
        self.layers = extent // devices
        self.channels = 2 * self.layers
        self.slot_rows = slots // LANES
        self.slots = slots
        self.sticks = -(-column_total(extent) // devices)
        self.out_rows, self.out_pieces = packing(self.channels + 1, self.sticks)
        self.back_rows, self.back_pieces = packing(self.channels, self.sticks)
        self.rows = self.out_rows + self.layers * self.layers
        self.bands_all = bands_all
        self.band_rows = bands_all // devices
        assert extent == LANES and self.channels <= SUB


def parts_of(matrix):
    values = np.asarray(matrix, np.float32)
    high = values.astype(jnp.bfloat16)
    low = (values - high.astype(np.float32)).astype(jnp.bfloat16)
    return np.stack([high, low])


def angle(x, y, extent):
    phase = (x[:, None] * y[None, :]) % extent
    return 2.0 * math.pi * phase.astype(np.float64) / extent


def tables(sz):
    n, d, layers = sz.extent, sz.devices, sz.layers
    cells = np.arange(n)
    dev, part, lay = np.meshgrid(np.arange(d), np.arange(2), np.arange(layers), indexing="ij")
    z_rows = (dev * layers + lay).reshape(-1)
    part_rows = part.reshape(-1)
    t = angle(z_rows, cells, n)
    re, im = np.cos(t), np.sin(t)
    is_im = part_rows[:, None] == 1
    forward_z = np.concatenate([np.where(is_im, im, re), np.where(is_im, re, -im)], 1)
    freq = np.arange(2 * HALF) - HALF
    tb = angle(freq, cells, n)
    cb, sb = np.cos(tb), np.sin(tb)
    eye = np.eye(2)
    cc, ss = np.kron(eye, cb), np.kron(eye, sb)
    forward_b = np.block([[cc, ss], [-ss, cc]])
    cct, sst = cc.T, ss.T
    inverse_b = np.block([[cct, -sst], [sst, cct]])
    a_rows = (np.arange(d)[None, :] * layers + np.arange(layers)[:, None]).reshape(-1)
    lo, k = np.meshgrid(np.arange(2), np.arange(KROWS), indexing="ij")
    a_freq = (4 * (k % GROUPS) + 2 * (k // GROUPS) + lo - HALF).reshape(-1)
    ta = angle(a_rows, a_freq, n)
    ca, sa = np.cos(ta), np.sin(ta)
    forward_a = np.block([[ca, -sa], [sa, ca]])
    inverse_a = np.block([[ca.T, sa.T], [-sa.T, ca.T]])
    part2, lay2, dev2 = np.meshgrid(np.arange(2), np.arange(layers), np.arange(d), indexing="ij")
    t2 = angle((dev2 * layers + lay2).reshape(-1), cells, n)
    re2, im2 = np.cos(t2) / n**3, np.sin(t2) / n**3
    im_rows = part2.reshape(-1)[:, None] == 1
    inverse_z = np.concatenate([np.where(im_rows, im2, re2), np.where(im_rows, re2, -im2)], 1)
    return {
        "forward_z": parts_of(forward_z),
        "forward_b": parts_of(forward_b),
        "forward_a": parts_of(forward_a),
        "inverse_a": parts_of(inverse_a),
        "inverse_b": parts_of(inverse_b),
        "inverse_z": parts_of(inverse_z),
    }


def split(x):
    high = x.astype(BF16)
    return high, (x - high.astype(F32)).astype(BF16)


def dot(a, b, dims=NN):
    return lax.dot_general(a, b, (dims, ((), ())), preferred_element_type=F32)


def dot3(a, b, dims=NN):
    return dot(a[0], b[0], dims) + dot(a[0], b[1], dims) + dot(a[1], b[0], dims)


def iota(shape, dim):
    return lax.broadcasted_iota(I32, shape, dim)


def ones_where(mask):
    return jnp.where(mask, 1.0, 0.0).astype(F32)


def pick(values, lanes):
    return jnp.take_along_axis(values, lanes, axis=1, mode="promise_in_bounds")


def signed(x, extent):
    return jnp.where(x < extent // 2, x, x - extent)


def column_facts(meta, sz):
    shape = (LANES, LANES)
    col_a = jnp.broadcast_to(meta[:, 0:1], shape)
    col_b = jnp.broadcast_to(meta[:, 1:2], shape)
    row = jnp.broadcast_to(meta[:, 2:3], shape)
    lane = jnp.broadcast_to(meta[:, 3:4], shape)
    valid = jnp.broadcast_to(meta[:, 4:5], shape) > 0.5
    fa = jnp.where(col_a < sz.extent // 2, col_a, col_a - sz.extent)
    fb = jnp.where(col_b < sz.extent // 2, col_b, col_b - sz.extent)
    fc = signed(iota(shape, 1), sz.extent).astype(F32)
    inside = valid & (fc * fc <= RADIUS * RADIUS - fa * fa - fb * fb)
    return row, lane, inside


class BandLoads:
    def __init__(self, source, target, sems, first, count):
        self.refs = (source, target, sems, first)
        self.count = count // CHUNK

    def copy(self, i):
        source, target, sems, first = self.refs
        return pltpu.make_async_copy(
            source.at[:, pl.ds(first + i * CHUNK, CHUNK), :],
            target.at[:, pl.ds(i * CHUNK, CHUNK), :],
            sems.at[i],
        )

    def start(self):
        for i in range(self.count):
            self.copy(i).start()

    def wait_one(self, i):
        self.copy(i).wait()

    def wait(self):
        for i in range(self.count):
            self.copy(i).wait()


def spread_kernel(sz, cells_ref, orbitals_ref, potential_ref, table_ref,
                  send_ref, window_ref, meta_ref, early_ref,
                  cells_in, block, pot, table, turned, rows_ref, sems, band_sems):
    loads = [
        pltpu.make_async_copy(cells_ref, cells_in, sems.at[0]),
        pltpu.make_async_copy(orbitals_ref.at[:, pl.ds(0, SUB), :], block, sems.at[1]),
        pltpu.make_async_copy(potential_ref, pot, sems.at[2]),
        pltpu.make_async_copy(table_ref, table, sems.at[3]),
    ]
    for load in loads:
        load.start()
    bands = BandLoads(orbitals_ref, early_ref, band_sems, 0, EARLY)
    bands.start()
    for load in loads:
        load.wait()
    layers, devices = sz.layers, sz.devices
    for al in range(layers):
        turned[al * LANES : (al + 1) * LANES, :] = jnp.transpose(pot[al])
        for p in range(layers):
            at = sz.out_rows + al * layers + p
            send_ref[pl.ds(at, devices, stride=sz.rows), :] = turned[
                pl.ds(al * LANES + p, devices, stride=layers), :
            ]
    rows = sz.slot_rows
    shape = (rows, LANES)
    cells = cells_in[...]
    live = cells >= 0
    column = lax.shift_right_arithmetic(cells, int(math.log2(sz.extent)))
    rolled = pltpu.roll(column, 1, 1)
    above = pltpu.roll(rolled, 1, 0)
    lane = iota(shape, 1)
    row = iota(shape, 0)
    before = jnp.where(lane == 0, jnp.where(row == 0, -1, above), rolled)
    starts = live & (column != before)
    flags = ones_where(starts).astype(BF16)
    square = (LANES, LANES)
    upto = ones_where(iota(square, 0) <= iota(square, 1)).astype(BF16)
    all_ones = jnp.ones(square, BF16)
    within = dot(flags, upto)
    totals = dot(flags, all_ones)
    lower = ones_where(iota((rows, rows), 1) < iota((rows, rows), 0)).astype(BF16)
    rank = (within + dot(lower, totals.astype(BF16))).astype(I32) - 1
    rank = jnp.where(starts, rank, -1)
    col_a = lax.shift_right_arithmetic(column, int(math.log2(sz.extent)))
    col_b = column & (sz.extent - 1)
    sub = iota((SUB, LANES), 0)
    lane8 = iota((SUB, LANES), 1)
    place = iota(square, 0)
    hots, facts = [], []
    for r in range(rows):
        hots.append(ones_where(place == rank[r : r + 1, :]).astype(BF16))
        fact = jnp.where(sub == 0, col_a[r : r + 1, :], col_b[r : r + 1, :])
        fact = jnp.where(sub == 2, r, fact)
        fact = jnp.where(sub == 3, lane8, fact)
        fact = jnp.where(sub == 4, 1, fact)
        facts.append(fact.astype(F32).astype(BF16))
    meta_t = dot(jnp.concatenate(facts, 1), jnp.concatenate(hots, 1), NT)
    meta_ref[...] = meta_t
    meta = jnp.transpose(jnp.concatenate([meta_t, jnp.zeros((LANES - SUB, LANES), F32)], 0))
    first_row, first_lane, inside = column_facts(meta, sz)
    hot = ones_where(inside).astype(BF16)
    before_in = ones_where(iota(square, 0) < iota(square, 1)).astype(BF16)
    slot = (first_lane + dot(hot, before_in)).astype(I32)
    second = slot >= LANES
    slot_lane = slot & (LANES - 1)

    for r in range(rows):
        window_ref[r : r + 1, :] = block[0, 0:1, r * LANES : (r + 1) * LANES]
        window_ref[rows + r : rows + r + 1, :] = block[1, 0:1, r * LANES : (r + 1) * LANES]
    window = jnp.concatenate([window_ref[0:rows, :], window_ref[rows : 2 * rows, :]], 1)
    high, low = split(window)
    row_of = first_row.astype(I32)[:, 0:rows]
    which = iota((LANES, rows), 1)
    near = ones_where(which == row_of).astype(BF16)
    far = ones_where(which == row_of + 1).astype(BF16)
    near_w = dot(near, high) + dot(near, low)
    far_w = dot(far, high) + dot(far, low)
    sticks = []
    for part in range(2):
        cut = slice(part * LANES, (part + 1) * LANES)
        value = jnp.where(second, pick(far_w[:, cut], slot_lane), pick(near_w[:, cut], slot_lane))
        sticks.append(jnp.where(inside, value, 0.0))
    sticks = jnp.concatenate(sticks, 1)
    depth = dot3((table[0], table[1]), split(sticks), NT)

    channels, layers, devices = sz.channels, sz.layers, sz.devices
    ids = jnp.where(
        meta_t[4:5, :] > 0.5, meta_t[0:1, :] * sz.extent + meta_t[1:2, :], -1.0
    )
    ids = jnp.broadcast_to(ids, (devices, LANES))
    rows_ref[...] = depth

    def item(i):
        return ids if i == channels else rows_ref[pl.ds(i, devices, stride=channels), :]

    for r in range(sz.out_rows):
        send_ref[pl.ds(r, devices, stride=sz.rows), :] = pack_row(r, item, sz.out_pieces)
    bands.wait()


def plane_kernel(sz, recv_ref, fb, fa, ia, ib, orbitals_ref,
                 out_ref, middle_ref,
                 hot_ref, planes, back, group_ref, z_ref, band_sems):
    bands = BandLoads(orbitals_ref, middle_ref, band_sems, EARLY, MIDDLE)
    bands.start()
    devices, layers, channels = sz.devices, sz.layers, sz.channels

    def recv_row(r):
        return recv_ref[pl.ds(r, devices, stride=sz.rows), :]

    def recv_item(i):
        return unpack_item(i, sz.out_rows, recv_row, sz.out_pieces)

    lane = iota((devices, LANES), 1)
    ids = jnp.where(lane < sz.sticks, recv_item(channels), -1.0).astype(I32)
    if channels < SUB:
        z_ref[...] = jnp.zeros(z_ref.shape, F32)
    for i in range(channels):
        z_ref[pl.ds(i, devices, stride=SUB), :] = recv_item(i)
    col_a = lax.shift_right_arithmetic(ids, int(math.log2(sz.extent)))
    col_b = ids & (sz.extent - 1)
    sa = (col_a + HALF) & (sz.extent - 1)
    sb = (col_b + HALF) & (sz.extent - 1)
    group = jnp.where(ids >= 0, lax.shift_right_arithmetic(sa, 2), -1)
    cell = (sa & 3) * (2 * HALF) + sb
    group_ref[...] = group
    two = (2 * SUB, LANES)
    cell_rows = [(iota(two, 0) + i).astype(F32).astype(BF16) for i in range(0, CELLS, 2 * SUB)]
    group_rows = [
        (lax.shift_right_logical(iota(two, 0), 3) + g).astype(F32).astype(BF16)
        for g in range(0, GROUPS, 2)
    ]
    one, zero = jnp.ones(two, BF16), jnp.zeros(two, BF16)
    cell, group_f = cell.astype(F32), group.astype(F32)
    left_high, left_low = [], []
    for e in range(devices):
        own_cell = jnp.broadcast_to(cell[e : e + 1, :], two).astype(BF16)
        own_group = jnp.broadcast_to(group_f[e : e + 1, :], two).astype(BF16)
        values = z_ref[e * SUB : (e + 1) * SUB, :]
        high, low = split(jnp.concatenate([values, values], 0))
        here = [own_group == g for g in group_rows]
        left_high.append(jnp.concatenate([jnp.where(h, high, zero) for h in here], 0))
        left_low.append(jnp.concatenate([jnp.where(h, low, zero) for h in here], 0))
        for i, rows in enumerate(cell_rows):
            hot_ref[2 * SUB * i : 2 * SUB * (i + 1), e * LANES : (e + 1) * LANES] = jnp.where(
                own_cell == rows, one, zero
            )
    left = jnp.concatenate(
        [jnp.concatenate(left_high, 1), jnp.concatenate(left_low, 1)], 0
    )
    spread = dot(left, hot_ref[...], NT)
    size = GROUPS * SUB
    spread = spread[:size] + spread[size:]
    for half in range(2):
        planes[half * size : (half + 1) * size, :] = spread[:, half * LANES : (half + 1) * LANES]

    def plane_part(part, p):
        return planes[pl.ds(part * layers + p, KROWS, stride=SUB), :]

    grid = jnp.concatenate(
        [
            jnp.concatenate([plane_part(part, p) for p in range(layers)], 0)
            for part in range(2)
        ],
        1,
    )
    grid = dot3(split(grid), (fb[0], fb[1]))
    grid = jnp.concatenate(
        [
            jnp.concatenate(
                [
                    grid[p * KROWS : (p + 1) * KROWS, q * LANES : (q + 1) * LANES]
                    for q in range(4)
                ],
                0,
            )
            for p in range(layers)
        ],
        1,
    )
    grid = dot3((fa[0], fa[1]), split(grid))
    potential = jnp.concatenate(
        [
            jnp.concatenate(
                [
                    recv_row(sz.out_rows + al * layers + p)
                    for al in range(layers)
                ],
                0,
            )
            for p in range(layers)
        ],
        1,
    )
    half = sz.extent
    field = jnp.concatenate([grid[0:half] * potential, grid[half:] * potential], 0)
    grid = dot3((ia[0], ia[1]), split(field))
    grid = jnp.concatenate(
        [
            jnp.concatenate(
                [
                    grid[q * KROWS : (q + 1) * KROWS, p * LANES : (p + 1) * LANES]
                    for q in range(4)
                ],
                1,
            )
            for p in range(layers)
        ],
        0,
    )
    grid = dot3(split(grid), (ib[0], ib[1]))
    for part in range(2):
        for p in range(layers):
            back[pl.ds(part * layers + p, KROWS, stride=SUB), :] = grid[
                p * KROWS : (p + 1) * KROWS, part * LANES : (part + 1) * LANES
            ]

    values = jnp.concatenate([back[:size, :], back[size:, :]], 1)
    values = jnp.concatenate(split(values), 0)
    for e in range(devices):
        found = dot(values, hot_ref[:, e * LANES : (e + 1) * LANES])
        found = found[:size] + found[size:]
        own = jnp.broadcast_to(group_ref[e : e + 1, :], (SUB, LANES))
        total = jnp.zeros((SUB, LANES), F32)
        for g in range(GROUPS):
            total = total + jnp.where(own == g, found[g * SUB : (g + 1) * SUB, :], 0.0)
        z_ref[e * SUB : (e + 1) * SUB, :] = total

    def back_item(i):
        return z_ref[pl.ds(i, devices, stride=SUB), :]

    for r in range(sz.back_rows):
        out_ref[pl.ds(r, devices, stride=sz.back_rows), :] = pack_row(
            r, back_item, sz.back_pieces
        )
    bands.wait()


def final_kernel(sz, back_ref, cells_ref, window_ref, meta_ref, table_ref, early_ref, middle_ref,
                 orbitals_ref,
                 applied_out, tile_ref,
                 applied_ref, factors, late_ref, acc, band_sems, out_sem):
    done = EARLY + MIDDLE
    bands = BandLoads(orbitals_ref, late_ref, band_sems, done, sz.bands_all - done)
    bands.start()
    devices, layers, rows = sz.devices, sz.layers, sz.slot_rows
    square = (LANES, LANES)

    def back_row(r):
        return back_ref[pl.ds(r, devices, stride=sz.back_rows), :]

    values = jnp.concatenate(
        [
            unpack_item(i, sz.back_rows, back_row, sz.back_pieces)
            for i in range(sz.channels)
        ],
        0,
    )
    values = jnp.transpose(values)
    sticks = dot3(split(values), (table_ref[0], table_ref[1]))
    meta_t = meta_ref[...]
    meta = jnp.transpose(jnp.concatenate([meta_t, jnp.zeros((LANES - SUB, LANES), F32)], 0))
    first_row, first_lane, inside = column_facts(meta, sz)
    length = dot(ones_where(inside).astype(BF16), jnp.ones(square, BF16)).astype(I32)
    shift = iota(square, 1) - first_lane.astype(I32)
    top = lax.shift_right_arithmetic(length - 1, 1)
    placed = []
    for turn in range(2):
        p = shift + turn * LANES
        held = (p >= 0) & (p < length)
        depth = jnp.where(p <= top, p, p + sz.extent - length) & (sz.extent - 1)
        placed.append(
            jnp.concatenate(
                [
                    jnp.where(held, pick(sticks[:, q * LANES : (q + 1) * LANES], depth), 0.0)
                    for q in range(2)
                ],
                1,
            )
        )
    placed = split(jnp.concatenate(placed, 0))
    row_t = jnp.broadcast_to(meta_t[2:3, :].astype(I32), (rows, LANES))
    which = iota((rows, LANES), 0)
    hot = jnp.concatenate(
        [ones_where(which == row_t), ones_where(which == row_t + 1)], 1
    ).astype(BF16)
    local = dot(hot, placed[0]) + dot(hot, placed[1])
    cells = cells_ref[...]
    live = cells >= 0
    bits = int(math.log2(sz.extent))
    mask = sz.extent - 1
    fa = signed(lax.shift_right_arithmetic(cells, 2 * bits) & mask, sz.extent)
    fb = signed(lax.shift_right_arithmetic(cells, bits) & mask, sz.extent)
    fc = signed(cells & mask, sz.extent)
    kinetic = (fa * fa + fb * fb + fc * fc).astype(F32) / (RADIUS * RADIUS)
    for part in range(2):
        own = window_ref[part * rows : (part + 1) * rows, :]
        full = kinetic * own + local[:, part * LANES : (part + 1) * LANES]
        applied_ref[part * rows : (part + 1) * rows, :] = jnp.where(live, full, 0.0)
    store = pltpu.make_async_copy(applied_ref, applied_out, out_sem)
    store.start()
    a_re = applied_ref[0:rows, :]
    a_im = applied_ref[rows : 2 * rows, :]
    factors[0] = a_im
    factors[1] = a_re - a_im
    factors[2] = a_re + a_im

    def product_of(source, first, wait=None):
        def product(i, carry):
            if wait is not None:
                wait(i)
            start = pl.multiple_of(i * CHUNK, CHUNK)
            sums = [jnp.zeros((CHUNK, LANES), F32) for _ in range(3)]
            for r in range(rows):
                x = source[0, pl.ds(start, CHUNK), r * LANES : (r + 1) * LANES]
                y = source[1, pl.ds(start, CHUNK), r * LANES : (r + 1) * LANES]
                for q, value in enumerate((x + y, x, y)):
                    sums[q] = sums[q] + value * factors[q, r : r + 1, :]
            acc[0, pl.ds(first + start, CHUNK), :] = sums[0] + sums[1]
            acc[1, pl.ds(first + start, CHUNK), :] = sums[0] - sums[2]
            return carry

        lax.fori_loop(0, source.shape[1] // CHUNK, product, 0)

    product_of(early_ref, 0)
    product_of(middle_ref, EARLY)
    product_of(late_ref, done, bands.wait_one)
    blocks = sz.bands_all // LANES
    block_row = iota((blocks, LANES), 0)
    sums = []
    for part in range(2):
        total = jnp.zeros((blocks, LANES), F32)
        for i in range(blocks):
            hot_row = ones_where(block_row == i).astype(BF16)
            high, low = split(acc[part, i * LANES : (i + 1) * LANES, :])
            total = total + (dot(hot_row, high, NT) + dot(hot_row, low, NT))
        sums.append(total * (1.0 / (sz.slots * sz.devices)))
    width = sz.band_rows
    per_row = LANES // width
    lane = iota((blocks, LANES), 1)
    for q in range(per_row):
        real = pltpu.roll(sums[0], (-q * width) % LANES, 1)
        imag = pltpu.roll(sums[1], (width - q * width) % LANES, 1)
        tile_ref[pl.ds(q, blocks, stride=per_row), :] = jnp.where(lane < width, real, imag)
    store.wait()


def sum_kernel(sz, tile_ref, out_ref):
    width = sz.band_rows
    total = jnp.sum(tile_ref[...], axis=0, keepdims=True)
    for part in range(2):
        out_ref[part, :, :] = total[:, part * width : (part + 1) * width]


def full_spec():
    return pl.BlockSpec(memory_space=pltpu.VMEM)


def any_spec():
    return pl.BlockSpec(memory_space=pl.ANY)


def vmem(mib):
    return pltpu.CompilerParams(vmem_limit_bytes=mib << 20)


def run_spread(sz, cells, orbitals, potential, table, **kw):
    return pl.pallas_call(
        lambda *refs: spread_kernel(sz, *refs),
        out_shape=(
            jax.ShapeDtypeStruct((sz.devices * sz.rows, LANES), F32),
            jax.ShapeDtypeStruct((2 * sz.slot_rows, LANES), F32),
            jax.ShapeDtypeStruct((SUB, LANES), F32),
            pltpu.VMEM((2, EARLY, sz.slots), F32),
        ),
        in_specs=[any_spec()] * 4,
        out_specs=(full_spec(),) * 4,
        scratch_shapes=[
            pltpu.VMEM((sz.slot_rows, LANES), I32),
            pltpu.VMEM((2, SUB, sz.slots), F32),
            pltpu.VMEM((sz.layers, LANES, LANES), F32),
            pltpu.VMEM(table.shape, BF16),
            pltpu.VMEM((sz.layers * LANES, LANES), F32),
            pltpu.VMEM((sz.devices * sz.channels, LANES), F32),
            pltpu.SemaphoreType.DMA((4,)),
            pltpu.SemaphoreType.DMA((EARLY // CHUNK,)),
        ],
        name="spread",
        compiler_params=vmem(8),
        **kw,
    )(cells, orbitals, potential, table)


def run_planes(sz, recv, tabs, orbitals, **kw):
    mats = [tabs[n] for n in ("forward_b", "forward_a", "inverse_a", "inverse_b")]
    return pl.pallas_call(
        lambda *refs: plane_kernel(sz, *refs),
        out_shape=(
            jax.ShapeDtypeStruct((sz.devices * sz.back_rows, LANES), F32),
            pltpu.VMEM((2, MIDDLE, sz.slots), F32),
        ),
        in_specs=[full_spec()] * 5 + [any_spec()],
        out_specs=(full_spec(), full_spec()),
        scratch_shapes=[
            pltpu.VMEM((CELLS, sz.devices * LANES), BF16),
            pltpu.VMEM((KROWS * SUB, LANES), F32),
            pltpu.VMEM((KROWS * SUB, LANES), F32),
            pltpu.VMEM((sz.devices, LANES), I32),
            pltpu.VMEM((sz.devices * SUB, LANES), F32),
            pltpu.SemaphoreType.DMA((MIDDLE // CHUNK,)),
        ],
        name="planes",
        compiler_params=vmem(16),
        **kw,
    )(recv, *mats, orbitals)


def run_final(sz, back, cells, window, meta, table, early, middle, orbitals, **kw):
    late = sz.bands_all - EARLY - MIDDLE
    return pl.pallas_call(
        lambda *refs: final_kernel(sz, *refs),
        out_shape=(
            jax.ShapeDtypeStruct((2 * sz.slot_rows, LANES), F32),
            jax.ShapeDtypeStruct((sz.devices, LANES), F32),
        ),
        in_specs=[full_spec()] * 7 + [any_spec()],
        out_specs=(any_spec(), full_spec()),
        scratch_shapes=[
            pltpu.VMEM((2 * sz.slot_rows, LANES), F32),
            pltpu.VMEM((3, sz.slot_rows, LANES), F32),
            pltpu.VMEM((2, late, sz.slots), F32),
            pltpu.VMEM((2, sz.bands_all, LANES), F32),
            pltpu.SemaphoreType.DMA((late // CHUNK,)),
            pltpu.SemaphoreType.DMA,
        ],
        name="final",
        compiler_params=vmem(20),
        **kw,
    )(back, cells, window, meta, table, early, middle, orbitals)


def run_sum(sz, tile, **kw):
    return pl.pallas_call(
        lambda *refs: sum_kernel(sz, *refs),
        out_shape=jax.ShapeDtypeStruct((2, 1, sz.band_rows), F32),
        in_specs=[full_spec()],
        out_specs=full_spec(),
        name="add",
        compiler_params=vmem(2),
        **kw,
    )(tile)


def exchange(x):
    rows = x.reshape(x.shape[0], 1, x.shape[1])
    return lax.all_to_all(rows, "ga", split_axis=0, concat_axis=0, tiled=True).reshape(x.shape)


def local(orbitals, coeff_cells, potential):
    devices = lax.axis_size("ga")
    sz = Sizes(devices, potential.shape[1], coeff_cells.shape[0], orbitals.shape[1])
    tabs = {name: jnp.asarray(value) for name, value in tables(sz).items()}
    cells = coeff_cells.reshape(sz.slot_rows, LANES)
    stay = lambda x: pltpu.with_memory_space_constraint(x, pltpu.HBM)
    orbitals = stay(orbitals)
    send, window, meta, early = run_spread(
        sz, stay(cells), orbitals, stay(potential), stay(tabs["forward_z"])
    )
    back, middle = run_planes(sz, exchange(send), tabs, orbitals)
    applied, tile = run_final(
        sz, exchange(back), cells, window, meta, tabs["inverse_z"], early, middle, orbitals
    )
    subspace = run_sum(sz, exchange(tile))
    return (
        applied.reshape(2, 1, sz.slots),
        jnp.transpose(subspace, (2, 0, 1)),
    )


def solution(mesh):
    in_specs = (P(None, "kpt", "ga"), P("ga"), P("ga", None, None))
    out_specs = (P(None, "kpt", "ga"), P("ga", None, "kpt"))
    return jax.shard_map(local, mesh=mesh, in_specs=in_specs, out_specs=out_specs, check_vma=False)
```

```python
import math

import jax
import jax.numpy as jnp
import numpy as np
from jax import lax
from jax.experimental import pallas as pl
from jax.experimental.pallas import tpu as pltpu
from jax.sharding import PartitionSpec as P

RADIUS = 30
LANES = 128
SUB = 8
HALF = 32
KROWS = 32
CELLS = 4 * 2 * HALF
GROUPS = KROWS // 2
CHUNK = 64
EARLY = 128
MIDDLE = 384
F32 = jnp.float32
BF16 = jnp.bfloat16
I32 = jnp.int32

NT = ((1,), (1,))
NN = ((1,), (0,))


def column_total(extent):
    indices = np.arange(extent)
    frequency = np.where(indices < extent // 2, indices, indices - extent)
    return int(np.sum(frequency[:, None] ** 2 + frequency[None, :] ** 2 <= RADIUS * RADIUS))


def packing(items, width):
    spare = LANES - width
    base = next(b for b in range(1, items + 1) if (items - b) * width <= b * spare)
    pieces = []
    row, at = 0, width
    for item in range(base, items):
        done = 0
        while done < width:
            if at == LANES:
                row, at = row + 1, width
            length = min(width - done, LANES - at)
            pieces.append((item, done, row, at, length))
            done, at = done + length, at + length
    return base, pieces


def pack_row(row, load, pieces):
    value = load(row)
    lane = lax.broadcasted_iota(I32, value.shape, 1)
    for item, source, target_row, target, length in pieces:
        if target_row == row:
            moved = pltpu.roll(load(item), (target - source) % LANES, 1)
            value = jnp.where((lane >= target) & (lane < target + length), moved, value)
    return value


def unpack_item(item, base, load, pieces):
    if item < base:
        return load(item)
    value = None
    for owner, source, row, at, length in pieces:
        if owner == item:
            moved = pltpu.roll(load(row), (source - at) % LANES, 1)
            lane = lax.broadcasted_iota(I32, moved.shape, 1)
            value = moved if value is None else jnp.where(lane >= source, moved, value)
    return value


class Sizes:
    def __init__(self, devices, extent, slots, bands_all):
        self.devices = devices
        self.extent = extent
        self.layers = extent // devices
        self.channels = 2 * self.layers
        self.slot_rows = slots // LANES
        self.slots = slots
        self.sticks = -(-column_total(extent) // devices)
        self.out_rows, self.out_pieces = packing(self.channels + 1, self.sticks)
        self.back_rows, self.back_pieces = packing(self.channels, self.sticks)
        self.rows = self.out_rows + self.layers * self.layers
        self.bands_all = bands_all
        self.band_rows = bands_all // devices
        assert extent == LANES and self.channels <= SUB


def parts_of(matrix):
    values = np.asarray(matrix, np.float32)
    high = values.astype(jnp.bfloat16)
    low = (values - high.astype(np.float32)).astype(jnp.bfloat16)
    return np.stack([high, low])


def angle(x, y, extent):
    phase = (x[:, None] * y[None, :]) % extent
    return 2.0 * math.pi * phase.astype(np.float64) / extent


def tables(sz):
    n, d, layers = sz.extent, sz.devices, sz.layers
    cells = np.arange(n)
    dev, part, lay = np.meshgrid(np.arange(d), np.arange(2), np.arange(layers), indexing="ij")
    z_rows = (dev * layers + lay).reshape(-1)
    part_rows = part.reshape(-1)
    t = angle(z_rows, cells, n)
    re, im = np.cos(t), np.sin(t)
    is_im = part_rows[:, None] == 1
    forward_z = np.concatenate([np.where(is_im, im, re), np.where(is_im, re, -im)], 1)
    freq = np.arange(2 * HALF) - HALF
    tb = angle(freq, cells, n)
    cb, sb = np.cos(tb), np.sin(tb)
    eye = np.eye(2)
    cc, ss = np.kron(eye, cb), np.kron(eye, sb)
    forward_b = np.block([[cc, ss], [-ss, cc]])
    cct, sst = cc.T, ss.T
    inverse_b = np.block([[cct, -sst], [sst, cct]])
    a_rows = (np.arange(d)[None, :] * layers + np.arange(layers)[:, None]).reshape(-1)
    lo, k = np.meshgrid(np.arange(2), np.arange(KROWS), indexing="ij")
    a_freq = (4 * (k % GROUPS) + 2 * (k // GROUPS) + lo - HALF).reshape(-1)
    ta = angle(a_rows, a_freq, n)
    ca, sa = np.cos(ta), np.sin(ta)
    forward_a = np.block([[ca, -sa], [sa, ca]])
    inverse_a = np.block([[ca.T, sa.T], [-sa.T, ca.T]])
    part2, lay2, dev2 = np.meshgrid(np.arange(2), np.arange(layers), np.arange(d), indexing="ij")
    t2 = angle((dev2 * layers + lay2).reshape(-1), cells, n)
    re2, im2 = np.cos(t2) / n**3, np.sin(t2) / n**3
    im_rows = part2.reshape(-1)[:, None] == 1
    inverse_z = np.concatenate([np.where(im_rows, im2, re2), np.where(im_rows, re2, -im2)], 1)
    return {
        "forward_z": parts_of(forward_z),
        "forward_b": parts_of(forward_b),
        "forward_a": parts_of(forward_a),
        "inverse_a": parts_of(inverse_a),
        "inverse_b": parts_of(inverse_b),
        "inverse_z": parts_of(inverse_z),
    }


def split(x):
    high = x.astype(BF16)
    return high, (x - high.astype(F32)).astype(BF16)


def dot(a, b, dims=NN):
    return lax.dot_general(a, b, (dims, ((), ())), preferred_element_type=F32)


def dot3(a, b, dims=NN):
    return dot(a[0], b[0], dims) + dot(a[0], b[1], dims) + dot(a[1], b[0], dims)


def iota(shape, dim):
    return lax.broadcasted_iota(I32, shape, dim)


def ones_where(mask):
    return jnp.where(mask, 1.0, 0.0).astype(F32)


def pick(values, lanes):
    return jnp.take_along_axis(values, lanes, axis=1, mode="promise_in_bounds")


def signed(x, extent):
    return jnp.where(x < extent // 2, x, x - extent)


def column_facts(meta, sz):
    shape = (LANES, LANES)
    col_a = jnp.broadcast_to(meta[:, 0:1], shape)
    col_b = jnp.broadcast_to(meta[:, 1:2], shape)
    row = jnp.broadcast_to(meta[:, 2:3], shape)
    lane = jnp.broadcast_to(meta[:, 3:4], shape)
    valid = jnp.broadcast_to(meta[:, 4:5], shape) > 0.5
    fa = jnp.where(col_a < sz.extent // 2, col_a, col_a - sz.extent)
    fb = jnp.where(col_b < sz.extent // 2, col_b, col_b - sz.extent)
    fc = signed(iota(shape, 1), sz.extent).astype(F32)
    inside = valid & (fc * fc <= RADIUS * RADIUS - fa * fa - fb * fb)
    return row, lane, inside


class BandLoads:
    def __init__(self, source, target, sems, first, count):
        self.refs = (source, target, sems, first)
        self.count = count // CHUNK

    def copy(self, i):
        source, target, sems, first = self.refs
        return pltpu.make_async_copy(
            source.at[:, pl.ds(first + i * CHUNK, CHUNK), :],
            target.at[:, pl.ds(i * CHUNK, CHUNK), :],
            sems.at[i],
        )

    def start(self):
        for i in range(self.count):
            self.copy(i).start()

    def wait_one(self, i):
        self.copy(i).wait()

    def wait(self):
        for i in range(self.count):
            self.copy(i).wait()


def spread_kernel(sz, cells_ref, orbitals_ref, potential_ref, table_ref,
                  send_ref, window_ref, depth_ref, slot_hot_ref, kinetic_ref, early_ref,
                  cells_in, block, pot, table, turned, rows_ref, sems, band_sems):
    loads = [
        pltpu.make_async_copy(orbitals_ref.at[:, pl.ds(0, SUB), :], block, sems.at[0]),
        pltpu.make_async_copy(table_ref, table, sems.at[1]),
        pltpu.make_async_copy(potential_ref, pot, sems.at[2]),
    ]
    cell_load = pltpu.make_async_copy(cells_ref, cells_in, sems.at[3])
    cell_load.start()
    for load in loads:
        load.start()
    cell_load.wait()
    bands = BandLoads(orbitals_ref, early_ref, band_sems, 0, EARLY)
    bands.start()
    rows = sz.slot_rows
    shape = (rows, LANES)
    cells = cells_in[...]
    live = cells >= 0
    column = lax.shift_right_arithmetic(cells, int(math.log2(sz.extent)))
    rolled = pltpu.roll(column, 1, 1)
    above = pltpu.roll(rolled, 1, 0)
    lane = iota(shape, 1)
    row = iota(shape, 0)
    before = jnp.where(lane == 0, jnp.where(row == 0, -1, above), rolled)
    starts = live & (column != before)
    flags = ones_where(starts).astype(BF16)
    square = (LANES, LANES)
    upto = ones_where(iota(square, 0) <= iota(square, 1)).astype(BF16)
    all_ones = jnp.ones(square, BF16)
    within = dot(flags, upto)
    totals = dot(flags, all_ones)
    lower = ones_where(iota((rows, rows), 1) < iota((rows, rows), 0)).astype(BF16)
    rank = (within + dot(lower, totals.astype(BF16))).astype(I32) - 1
    rank = jnp.where(starts, rank, -1)
    col_a = lax.shift_right_arithmetic(column, int(math.log2(sz.extent)))
    col_b = column & (sz.extent - 1)
    sub = iota((SUB, LANES), 0)
    lane8 = iota((SUB, LANES), 1)
    place = iota(square, 0)
    hots, facts = [], []
    for r in range(rows):
        hots.append(ones_where(place == rank[r : r + 1, :]).astype(BF16))
        fact = jnp.where(sub == 0, col_a[r : r + 1, :], col_b[r : r + 1, :])
        fact = jnp.where(sub == 2, r, fact)
        fact = jnp.where(sub == 3, lane8, fact)
        fact = jnp.where(sub == 4, 1, fact)
        facts.append(fact.astype(F32).astype(BF16))
    meta_t = dot(jnp.concatenate(facts, 1), jnp.concatenate(hots, 1), NT)
    meta = jnp.transpose(jnp.concatenate([meta_t, jnp.zeros((LANES - SUB, LANES), F32)], 0))
    first_row, first_lane, inside = column_facts(meta, sz)
    hot = ones_where(inside).astype(BF16)
    before_in = ones_where(iota(square, 0) < iota(square, 1)).astype(BF16)
    slot = (first_lane + dot(hot, before_in)).astype(I32)
    second = slot >= LANES
    slot_lane = slot & (LANES - 1)

    loads[0].wait()
    for r in range(rows):
        window_ref[r : r + 1, :] = block[0, 0:1, r * LANES : (r + 1) * LANES]
        window_ref[rows + r : rows + r + 1, :] = block[1, 0:1, r * LANES : (r + 1) * LANES]
    window = jnp.concatenate([window_ref[0:rows, :], window_ref[rows : 2 * rows, :]], 1)
    high, low = split(window)
    row_of = first_row.astype(I32)[:, 0:rows]
    which = iota((LANES, rows), 1)
    near = ones_where(which == row_of).astype(BF16)
    far = ones_where(which == row_of + 1).astype(BF16)
    near_w = dot(near, high) + dot(near, low)
    far_w = dot(far, high) + dot(far, low)
    sticks = []
    for part in range(2):
        cut = slice(part * LANES, (part + 1) * LANES)
        value = jnp.where(second, pick(far_w[:, cut], slot_lane), pick(near_w[:, cut], slot_lane))
        sticks.append(jnp.where(inside, value, 0.0))
    sticks = jnp.concatenate(sticks, 1)
    loads[1].wait()
    depth = dot3((table[0], table[1]), split(sticks), NT)

    channels, layers, devices = sz.channels, sz.layers, sz.devices
    ids = jnp.where(
        meta_t[4:5, :] > 0.5, meta_t[0:1, :] * sz.extent + meta_t[1:2, :], -1.0
    )
    ids = jnp.broadcast_to(ids, (devices, LANES))
    rows_ref[...] = depth

    def item(i):
        return ids if i == channels else rows_ref[pl.ds(i, devices, stride=channels), :]

    for r in range(sz.out_rows):
        send_ref[pl.ds(r, devices, stride=sz.rows), :] = pack_row(r, item, sz.out_pieces)
    loads[2].wait()
    for al in range(layers):
        turned[...] = jnp.transpose(pot[al])
        for p in range(layers):
            at = sz.out_rows + al * layers + p
            send_ref[pl.ds(at, devices, stride=sz.rows), :] = turned[
                pl.ds(p, devices, stride=layers), :
            ]
    length = dot(hot, all_ones).astype(I32)
    shift = iota(square, 1) - first_lane.astype(I32)
    top = lax.shift_right_arithmetic(length - 1, 1)
    for turn in range(2):
        p = shift + turn * LANES
        held = (p >= 0) & (p < length)
        depth_of = jnp.where(p <= top, p, p + sz.extent - length) & (sz.extent - 1)
        depth_ref[turn] = jnp.where(held, depth_of, -1)
    row_t = jnp.broadcast_to(meta_t[2:3, :].astype(I32), shape)
    slot_hot_ref[...] = jnp.concatenate(
        [ones_where(row == row_t), ones_where(row == row_t + 1)], 1
    ).astype(BF16)
    fa = signed(col_a & (sz.extent - 1), sz.extent)
    fb = signed(col_b, sz.extent)
    fc = signed(cells & (sz.extent - 1), sz.extent)
    kinetic = (fa * fa + fb * fb + fc * fc).astype(F32) / (RADIUS * RADIUS)
    kinetic_ref[...] = jnp.where(live, kinetic, -1.0)
    bands.wait()


def plane_kernel(sz, recv_ref, fb_ref, fa_ref, ia_ref, ib_ref, orbitals_ref,
                 out_ref, middle_ref,
                 fb, fa, ia, ib, hot_ref, planes, back, group_ref, z_ref, sems, band_sems):
    bands = BandLoads(orbitals_ref, middle_ref, band_sems, EARLY, MIDDLE)
    bands.start()
    copies = [
        pltpu.make_async_copy(src, dst, sems.at[i])
        for i, (src, dst) in enumerate([(fb_ref, fb), (fa_ref, fa), (ia_ref, ia), (ib_ref, ib)])
    ]
    for c in copies:
        c.start()
    devices, layers, channels = sz.devices, sz.layers, sz.channels

    def recv_row(r):
        return recv_ref[pl.ds(r, devices, stride=sz.rows), :]

    def recv_item(i):
        return unpack_item(i, sz.out_rows, recv_row, sz.out_pieces)

    lane = iota((devices, LANES), 1)
    ids = jnp.where(lane < sz.sticks, recv_item(channels), -1.0).astype(I32)
    if channels < SUB:
        z_ref[...] = jnp.zeros(z_ref.shape, F32)
    for i in range(channels):
        z_ref[pl.ds(i, devices, stride=SUB), :] = recv_item(i)
    col_a = lax.shift_right_arithmetic(ids, int(math.log2(sz.extent)))
    col_b = ids & (sz.extent - 1)
    sa = (col_a + HALF) & (sz.extent - 1)
    sb = (col_b + HALF) & (sz.extent - 1)
    group = jnp.where(ids >= 0, lax.shift_right_arithmetic(sa, 2), -1)
    cell = (sa & 3) * (2 * HALF) + sb
    group_ref[...] = group
    two = (2 * SUB, LANES)
    cell_rows = [(iota(two, 0) + i).astype(F32).astype(BF16) for i in range(0, CELLS, 2 * SUB)]
    group_rows = [
        (lax.shift_right_logical(iota(two, 0), 3) + g).astype(F32).astype(BF16)
        for g in range(0, GROUPS, 2)
    ]
    one, zero = jnp.ones(two, BF16), jnp.zeros(two, BF16)
    cell, group_f = cell.astype(F32), group.astype(F32)
    left_high, left_low = [], []
    for e in range(devices):
        own_cell = jnp.broadcast_to(cell[e : e + 1, :], two).astype(BF16)
        own_group = jnp.broadcast_to(group_f[e : e + 1, :], two).astype(BF16)
        values = z_ref[e * SUB : (e + 1) * SUB, :]
        high, low = split(jnp.concatenate([values, values], 0))
        here = [own_group == g for g in group_rows]
        left_high.append(jnp.concatenate([jnp.where(h, high, zero) for h in here], 0))
        left_low.append(jnp.concatenate([jnp.where(h, low, zero) for h in here], 0))
        for i, rows in enumerate(cell_rows):
            hot_ref[2 * SUB * i : 2 * SUB * (i + 1), e * LANES : (e + 1) * LANES] = jnp.where(
                own_cell == rows, one, zero
            )
    left = jnp.concatenate(
        [jnp.concatenate(left_high, 1), jnp.concatenate(left_low, 1)], 0
    )
    spread = dot(left, hot_ref[...], NT)
    size = GROUPS * SUB
    spread = spread[:size] + spread[size:]
    for half in range(2):
        planes[half * size : (half + 1) * size, :] = spread[:, half * LANES : (half + 1) * LANES]

    def plane_part(part, p):
        return planes[pl.ds(part * layers + p, KROWS, stride=SUB), :]

    grid = jnp.concatenate(
        [
            jnp.concatenate([plane_part(part, p) for p in range(layers)], 0)
            for part in range(2)
        ],
        1,
    )
    copies[0].wait()
    grid = dot3(split(grid), (fb[0], fb[1]))
    grid = jnp.concatenate(
        [
            jnp.concatenate(
                [
                    grid[p * KROWS : (p + 1) * KROWS, q * LANES : (q + 1) * LANES]
                    for q in range(4)
                ],
                0,
            )
            for p in range(layers)
        ],
        1,
    )
    copies[1].wait()
    grid = dot3((fa[0], fa[1]), split(grid))
    potential = jnp.concatenate(
        [
            jnp.concatenate(
                [
                    recv_row(sz.out_rows + al * layers + p)
                    for al in range(layers)
                ],
                0,
            )
            for p in range(layers)
        ],
        1,
    )
    half = sz.extent
    field = jnp.concatenate([grid[0:half] * potential, grid[half:] * potential], 0)
    copies[2].wait()
    grid = dot3((ia[0], ia[1]), split(field))
    grid = jnp.concatenate(
        [
            jnp.concatenate(
                [
                    grid[q * KROWS : (q + 1) * KROWS, p * LANES : (p + 1) * LANES]
                    for q in range(4)
                ],
                1,
            )
            for p in range(layers)
        ],
        0,
    )
    copies[3].wait()
    grid = dot3(split(grid), (ib[0], ib[1]))
    for part in range(2):
        for p in range(layers):
            back[pl.ds(part * layers + p, KROWS, stride=SUB), :] = grid[
                p * KROWS : (p + 1) * KROWS, part * LANES : (part + 1) * LANES
            ]

    values = jnp.concatenate([back[:size, :], back[size:, :]], 1)
    values = jnp.concatenate(split(values), 0)
    for e in range(devices):
        found = dot(values, hot_ref[:, e * LANES : (e + 1) * LANES])
        found = found[:size] + found[size:]
        own = jnp.broadcast_to(group_ref[e : e + 1, :], (SUB, LANES))
        total = jnp.zeros((SUB, LANES), F32)
        for g in range(GROUPS):
            total = total + jnp.where(own == g, found[g * SUB : (g + 1) * SUB, :], 0.0)
        z_ref[e * SUB : (e + 1) * SUB, :] = total

    def back_item(i):
        return z_ref[pl.ds(i, devices, stride=SUB), :]

    for r in range(sz.back_rows):
        out_ref[pl.ds(r, devices, stride=sz.back_rows), :] = pack_row(
            r, back_item, sz.back_pieces
        )
    bands.wait()


def final_kernel(sz, back_ref, window_ref, table_ref, depth_ref, hot_ref, kinetic_ref,
                 early_ref, middle_ref,
                 orbitals_ref,
                 applied_out, tile_ref,
                 applied_ref, factors, late_ref, acc, band_sems, out_sem):
    done = EARLY + MIDDLE
    bands = BandLoads(orbitals_ref, late_ref, band_sems, done, sz.bands_all - done)
    bands.start()
    devices, layers, rows = sz.devices, sz.layers, sz.slot_rows
    square = (LANES, LANES)

    def back_row(r):
        return back_ref[pl.ds(r, devices, stride=sz.back_rows), :]

    values = jnp.concatenate(
        [
            unpack_item(i, sz.back_rows, back_row, sz.back_pieces)
            for i in range(sz.channels)
        ],
        0,
    )
    values = jnp.transpose(values)
    sticks = dot3(split(values), (table_ref[0], table_ref[1]))
    placed = []
    for turn in range(2):
        depth = depth_ref[turn]
        held = depth >= 0
        depth = depth & (sz.extent - 1)
        placed.append(
            jnp.concatenate(
                [
                    jnp.where(held, pick(sticks[:, q * LANES : (q + 1) * LANES], depth), 0.0)
                    for q in range(2)
                ],
                1,
            )
        )
    placed = split(jnp.concatenate(placed, 0))
    hot = hot_ref[...]
    local = dot(hot, placed[0]) + dot(hot, placed[1])
    kinetic = kinetic_ref[...]
    for part in range(2):
        own = window_ref[part * rows : (part + 1) * rows, :]
        full = kinetic * own + local[:, part * LANES : (part + 1) * LANES]
        applied_ref[part * rows : (part + 1) * rows, :] = jnp.where(kinetic >= 0.0, full, 0.0)
    store = pltpu.make_async_copy(applied_ref, applied_out, out_sem)
    store.start()
    a_re = applied_ref[0:rows, :]
    a_im = applied_ref[rows : 2 * rows, :]
    factors[0] = a_im
    factors[1] = a_re - a_im
    factors[2] = a_re + a_im

    def product_of(source, first, wait=None):
        def product(i, carry):
            if wait is not None:
                wait(i)
            start = pl.multiple_of(i * CHUNK, CHUNK)
            sums = [jnp.zeros((CHUNK, LANES), F32) for _ in range(3)]
            for r in range(rows):
                x = source[0, pl.ds(start, CHUNK), r * LANES : (r + 1) * LANES]
                y = source[1, pl.ds(start, CHUNK), r * LANES : (r + 1) * LANES]
                for q, value in enumerate((x + y, x, y)):
                    sums[q] = sums[q] + value * factors[q, r : r + 1, :]
            acc[0, pl.ds(first + start, CHUNK), :] = sums[0] + sums[1]
            acc[1, pl.ds(first + start, CHUNK), :] = sums[0] - sums[2]
            return carry

        lax.fori_loop(0, source.shape[1] // CHUNK, product, 0)

    product_of(early_ref, 0)
    product_of(middle_ref, EARLY)
    product_of(late_ref, done, bands.wait_one)
    blocks = sz.bands_all // LANES
    block_row = iota((blocks, LANES), 0)
    sums = []
    for part in range(2):
        total = jnp.zeros((blocks, LANES), F32)
        for i in range(blocks):
            hot_row = ones_where(block_row == i).astype(BF16)
            high, low = split(acc[part, i * LANES : (i + 1) * LANES, :])
            total = total + (dot(hot_row, high, NT) + dot(hot_row, low, NT))
        sums.append(total * (1.0 / (sz.slots * sz.devices)))
    width = sz.band_rows
    per_row = LANES // width
    lane = iota((blocks, LANES), 1)
    for q in range(per_row):
        real = pltpu.roll(sums[0], (-q * width) % LANES, 1)
        imag = pltpu.roll(sums[1], (width - q * width) % LANES, 1)
        tile_ref[pl.ds(q, blocks, stride=per_row), :] = jnp.where(lane < width, real, imag)
    store.wait()


def sum_kernel(sz, tile_ref, out_ref):
    width = sz.band_rows
    total = jnp.sum(tile_ref[...], axis=0, keepdims=True)
    for part in range(2):
        out_ref[part, :, :] = total[:, part * width : (part + 1) * width]


def full_spec():
    return pl.BlockSpec(memory_space=pltpu.VMEM)


def any_spec():
    return pl.BlockSpec(memory_space=pl.ANY)


def vmem(mib):
    return pltpu.CompilerParams(vmem_limit_bytes=mib << 20)


def run_spread(sz, cells, orbitals, potential, table, **kw):
    return pl.pallas_call(
        lambda *refs: spread_kernel(sz, *refs),
        out_shape=(
            jax.ShapeDtypeStruct((sz.devices * sz.rows, LANES), F32),
            jax.ShapeDtypeStruct((2 * sz.slot_rows, LANES), F32),
            jax.ShapeDtypeStruct((2, LANES, LANES), I32),
            jax.ShapeDtypeStruct((sz.slot_rows, 2 * LANES), BF16),
            jax.ShapeDtypeStruct((sz.slot_rows, LANES), F32),
            pltpu.VMEM((2, EARLY, sz.slots), F32),
        ),
        in_specs=[any_spec()] * 4,
        out_specs=(full_spec(),) * 6,
        scratch_shapes=[
            pltpu.VMEM((sz.slot_rows, LANES), I32),
            pltpu.VMEM((2, SUB, sz.slots), F32),
            pltpu.VMEM((sz.layers, LANES, LANES), F32),
            pltpu.VMEM(table.shape, BF16),
            pltpu.VMEM((LANES, LANES), F32),
            pltpu.VMEM((sz.devices * sz.channels, LANES), F32),
            pltpu.SemaphoreType.DMA((4,)),
            pltpu.SemaphoreType.DMA((EARLY // CHUNK,)),
        ],
        name="spread",
        compiler_params=vmem(8),
        **kw,
    )(cells, orbitals, potential, table)


def run_planes(sz, recv, tabs, orbitals, **kw):
    mats = [tabs[n] for n in ("forward_b", "forward_a", "inverse_a", "inverse_b")]
    return pl.pallas_call(
        lambda *refs: plane_kernel(sz, *refs),
        out_shape=(
            jax.ShapeDtypeStruct((sz.devices * sz.back_rows, LANES), F32),
            pltpu.VMEM((2, MIDDLE, sz.slots), F32),
        ),
        in_specs=[full_spec()] + [any_spec()] * 5,
        out_specs=(full_spec(), full_spec()),
        scratch_shapes=[pltpu.VMEM(m.shape, BF16) for m in mats]
        + [
            pltpu.VMEM((CELLS, sz.devices * LANES), BF16),
            pltpu.VMEM((KROWS * SUB, LANES), F32),
            pltpu.VMEM((KROWS * SUB, LANES), F32),
            pltpu.VMEM((sz.devices, LANES), I32),
            pltpu.VMEM((sz.devices * SUB, LANES), F32),
            pltpu.SemaphoreType.DMA((4,)),
            pltpu.SemaphoreType.DMA((MIDDLE // CHUNK,)),
        ],
        name="planes",
        compiler_params=vmem(16),
        **kw,
    )(recv, *mats, orbitals)


def run_final(sz, back, window, table, depth, hot, kinetic, early, middle, orbitals, **kw):
    late = sz.bands_all - EARLY - MIDDLE
    return pl.pallas_call(
        lambda *refs: final_kernel(sz, *refs),
        out_shape=(
            jax.ShapeDtypeStruct((2 * sz.slot_rows, LANES), F32),
            jax.ShapeDtypeStruct((sz.devices, LANES), F32),
        ),
        in_specs=[full_spec()] * 8 + [any_spec()],
        out_specs=(any_spec(), full_spec()),
        scratch_shapes=[
            pltpu.VMEM((2 * sz.slot_rows, LANES), F32),
            pltpu.VMEM((3, sz.slot_rows, LANES), F32),
            pltpu.VMEM((2, late, sz.slots), F32),
            pltpu.VMEM((2, sz.bands_all, LANES), F32),
            pltpu.SemaphoreType.DMA((late // CHUNK,)),
            pltpu.SemaphoreType.DMA,
        ],
        name="final",
        compiler_params=vmem(20),
        **kw,
    )(back, window, table, depth, hot, kinetic, early, middle, orbitals)


def run_sum(sz, tile, **kw):
    return pl.pallas_call(
        lambda *refs: sum_kernel(sz, *refs),
        out_shape=jax.ShapeDtypeStruct((2, 1, sz.band_rows), F32),
        in_specs=[full_spec()],
        out_specs=full_spec(),
        name="add",
        compiler_params=vmem(2),
        **kw,
    )(tile)


def exchange(x):
    rows = x.reshape(x.shape[0], 1, x.shape[1])
    return lax.all_to_all(rows, "ga", split_axis=0, concat_axis=0, tiled=True).reshape(x.shape)


def local(orbitals, coeff_cells, potential):
    devices = lax.axis_size("ga")
    sz = Sizes(devices, potential.shape[1], coeff_cells.shape[0], orbitals.shape[1])
    tabs = {name: jnp.asarray(value) for name, value in tables(sz).items()}
    cells = coeff_cells.reshape(sz.slot_rows, LANES)
    stay = lambda x: pltpu.with_memory_space_constraint(x, pltpu.HBM)
    orbitals = stay(orbitals)
    send, window, depth, hot, kinetic, early = run_spread(
        sz, stay(cells), orbitals, stay(potential), stay(tabs["forward_z"])
    )
    back, middle = run_planes(sz, exchange(send), tabs, orbitals)
    applied, tile = run_final(
        sz, exchange(back), window, tabs["inverse_z"], depth, hot, kinetic, early, middle, orbitals
    )
    subspace = run_sum(sz, exchange(tile))
    return (
        applied.reshape(2, 1, sz.slots),
        jnp.transpose(subspace, (2, 0, 1)),
    )


def solution(mesh):
    in_specs = (P(None, "kpt", "ga"), P("ga"), P("ga", None, None))
    out_specs = (P(None, "kpt", "ga"), P("ga", None, "kpt"))
    return jax.shard_map(local, mesh=mesh, in_specs=in_specs, out_specs=out_specs, check_vma=False)
```

```python
import math

import jax
import jax.numpy as jnp
import numpy as np
from jax import lax
from jax.experimental import pallas as pl
from jax.experimental.pallas import tpu as pltpu
from jax.sharding import PartitionSpec as P

RADIUS = 30
LANES = 128
SUB = 8
HALF = 32
KROWS = 32
CELLS = 4 * 2 * HALF
GROUPS = KROWS // 2
CHUNK = 64
EARLY = 192
MIDDLE = 448
F32 = jnp.float32
BF16 = jnp.bfloat16
I32 = jnp.int32

NT = ((1,), (1,))
NN = ((1,), (0,))


def column_total(extent):
    indices = np.arange(extent)
    frequency = np.where(indices < extent // 2, indices, indices - extent)
    return int(np.sum(frequency[:, None] ** 2 + frequency[None, :] ** 2 <= RADIUS * RADIUS))


def packing(items, width):
    spare = LANES - width
    base = next(b for b in range(1, items + 1) if (items - b) * width <= b * spare)
    pieces = []
    row, at = 0, width
    for item in range(base, items):
        done = 0
        while done < width:
            if at == LANES:
                row, at = row + 1, width
            length = min(width - done, LANES - at)
            pieces.append((item, done, row, at, length))
            done, at = done + length, at + length
    return base, pieces


def pack_row(row, load, pieces):
    value = load(row)
    lane = lax.broadcasted_iota(I32, value.shape, 1)
    for item, source, target_row, target, length in pieces:
        if target_row == row:
            moved = pltpu.roll(load(item), (target - source) % LANES, 1)
            value = jnp.where((lane >= target) & (lane < target + length), moved, value)
    return value


def unpack_item(item, base, load, pieces):
    if item < base:
        return load(item)
    value = None
    for owner, source, row, at, length in pieces:
        if owner == item:
            moved = pltpu.roll(load(row), (source - at) % LANES, 1)
            lane = lax.broadcasted_iota(I32, moved.shape, 1)
            value = moved if value is None else jnp.where(lane >= source, moved, value)
    return value


class Sizes:
    def __init__(self, devices, extent, slots, bands_all):
        self.devices = devices
        self.extent = extent
        self.layers = extent // devices
        self.channels = 2 * self.layers
        self.slot_rows = slots // LANES
        self.slots = slots
        self.sticks = -(-column_total(extent) // devices)
        self.out_rows, self.out_pieces = packing(self.channels + 1, self.sticks)
        self.back_rows, self.back_pieces = packing(self.channels, self.sticks)
        self.rows = self.out_rows + self.layers * self.layers
        self.bands_all = bands_all
        self.band_rows = bands_all // devices
        assert extent == LANES and self.channels <= SUB


def parts_of(matrix):
    values = np.asarray(matrix, np.float32)
    high = values.astype(jnp.bfloat16)
    low = (values - high.astype(np.float32)).astype(jnp.bfloat16)
    return np.stack([high, low])


def angle(x, y, extent):
    phase = (x[:, None] * y[None, :]) % extent
    return 2.0 * math.pi * phase.astype(np.float64) / extent


def tables(sz):
    n, d, layers = sz.extent, sz.devices, sz.layers
    cells = np.arange(n)
    dev, part, lay = np.meshgrid(np.arange(d), np.arange(2), np.arange(layers), indexing="ij")
    z_rows = (dev * layers + lay).reshape(-1)
    part_rows = part.reshape(-1)
    t = angle(z_rows, cells, n)
    re, im = np.cos(t), np.sin(t)
    is_im = part_rows[:, None] == 1
    forward_z = np.concatenate([np.where(is_im, im, re), np.where(is_im, re, -im)], 1)
    freq = np.arange(2 * HALF) - HALF
    tb = angle(freq, cells, n)
    cb, sb = np.cos(tb), np.sin(tb)
    eye = np.eye(2)
    cc, ss = np.kron(eye, cb), np.kron(eye, sb)
    forward_b = np.block([[cc, ss], [-ss, cc]])
    cct, sst = cc.T, ss.T
    inverse_b = np.block([[cct, -sst], [sst, cct]])
    a_rows = (np.arange(d)[None, :] * layers + np.arange(layers)[:, None]).reshape(-1)
    lo, k = np.meshgrid(np.arange(2), np.arange(KROWS), indexing="ij")
    a_freq = (4 * (k % GROUPS) + 2 * (k // GROUPS) + lo - HALF).reshape(-1)
    ta = angle(a_rows, a_freq, n)
    ca, sa = np.cos(ta), np.sin(ta)
    forward_a = np.block([[ca, -sa], [sa, ca]])
    inverse_a = np.block([[ca.T, sa.T], [-sa.T, ca.T]])
    part2, lay2, dev2 = np.meshgrid(np.arange(2), np.arange(layers), np.arange(d), indexing="ij")
    t2 = angle((dev2 * layers + lay2).reshape(-1), cells, n)
    re2, im2 = np.cos(t2) / n**3, np.sin(t2) / n**3
    im_rows = part2.reshape(-1)[:, None] == 1
    inverse_z = np.concatenate([np.where(im_rows, im2, re2), np.where(im_rows, re2, -im2)], 1)
    return {
        "forward_z": parts_of(forward_z),
        "forward_b": parts_of(forward_b),
        "forward_a": parts_of(forward_a),
        "inverse_a": parts_of(inverse_a),
        "inverse_b": parts_of(inverse_b),
        "inverse_z": parts_of(inverse_z),
    }


def split(x):
    high = x.astype(BF16)
    return high, (x - high.astype(F32)).astype(BF16)


def dot(a, b, dims=NN):
    return lax.dot_general(a, b, (dims, ((), ())), preferred_element_type=F32)


def dot3(a, b, dims=NN):
    return dot(a[0], b[0], dims) + dot(a[0], b[1], dims) + dot(a[1], b[0], dims)


def iota(shape, dim):
    return lax.broadcasted_iota(I32, shape, dim)


def ones_where(mask):
    return jnp.where(mask, 1.0, 0.0).astype(F32)


def pick(values, lanes):
    return jnp.take_along_axis(values, lanes, axis=1, mode="promise_in_bounds")


def signed(x, extent):
    return jnp.where(x < extent // 2, x, x - extent)


def column_facts(meta, sz):
    shape = (LANES, LANES)
    col_a = jnp.broadcast_to(meta[:, 0:1], shape)
    col_b = jnp.broadcast_to(meta[:, 1:2], shape)
    row = jnp.broadcast_to(meta[:, 2:3], shape)
    lane = jnp.broadcast_to(meta[:, 3:4], shape)
    valid = jnp.broadcast_to(meta[:, 4:5], shape) > 0.5
    fa = jnp.where(col_a < sz.extent // 2, col_a, col_a - sz.extent)
    fb = jnp.where(col_b < sz.extent // 2, col_b, col_b - sz.extent)
    fc = signed(iota(shape, 1), sz.extent).astype(F32)
    inside = valid & (fc * fc <= RADIUS * RADIUS - fa * fa - fb * fb)
    return row, lane, inside


class BandLoads:
    def __init__(self, source, target, sems, first, count):
        self.refs = (source, target, sems, first)
        self.count = count // CHUNK

    def copy(self, i):
        source, target, sems, first = self.refs
        return pltpu.make_async_copy(
            source.at[:, pl.ds(first + i * CHUNK, CHUNK), :],
            target.at[:, pl.ds(i * CHUNK, CHUNK), :],
            sems.at[i],
        )

    def start(self):
        for i in range(self.count):
            self.copy(i).start()

    def wait_one(self, i):
        self.copy(i).wait()

    def wait(self):
        for i in range(self.count):
            self.copy(i).wait()


def spread_kernel(sz, cells_ref, orbitals_ref, potential_ref, table_ref,
                  send_ref, window_ref, depth_ref, slot_hot_ref, kinetic_ref, early_ref,
                  cells_in, block, pot, table, turned, rows_ref, sems, band_sems):
    loads = [
        pltpu.make_async_copy(orbitals_ref.at[:, pl.ds(0, SUB), :], block, sems.at[0]),
        pltpu.make_async_copy(table_ref, table, sems.at[1]),
        pltpu.make_async_copy(potential_ref, pot, sems.at[2]),
    ]
    cell_load = pltpu.make_async_copy(cells_ref, cells_in, sems.at[3])
    cell_load.start()
    for load in loads:
        load.start()
    cell_load.wait()
    bands = BandLoads(orbitals_ref, early_ref, band_sems, 0, EARLY)
    bands.start()
    rows = sz.slot_rows
    shape = (rows, LANES)
    cells = cells_in[...]
    live = cells >= 0
    column = lax.shift_right_arithmetic(cells, int(math.log2(sz.extent)))
    rolled = pltpu.roll(column, 1, 1)
    above = pltpu.roll(rolled, 1, 0)
    lane = iota(shape, 1)
    row = iota(shape, 0)
    before = jnp.where(lane == 0, jnp.where(row == 0, -1, above), rolled)
    starts = live & (column != before)
    flags = ones_where(starts).astype(BF16)
    square = (LANES, LANES)
    upto = ones_where(iota(square, 0) <= iota(square, 1)).astype(BF16)
    all_ones = jnp.ones(square, BF16)
    within = dot(flags, upto)
    totals = dot(flags, all_ones)
    lower = ones_where(iota((rows, rows), 1) < iota((rows, rows), 0)).astype(BF16)
    rank = (within + dot(lower, totals.astype(BF16))).astype(I32) - 1
    rank = jnp.where(starts, rank, -1)
    col_a = lax.shift_right_arithmetic(column, int(math.log2(sz.extent)))
    col_b = column & (sz.extent - 1)
    sub = iota((SUB, LANES), 0)
    lane8 = iota((SUB, LANES), 1)
    place = iota(square, 0)
    hots, facts = [], []
    for r in range(rows):
        hots.append(ones_where(place == rank[r : r + 1, :]).astype(BF16))
        fact = jnp.where(sub == 0, col_a[r : r + 1, :], col_b[r : r + 1, :])
        fact = jnp.where(sub == 2, r, fact)
        fact = jnp.where(sub == 3, lane8, fact)
        fact = jnp.where(sub == 4, 1, fact)
        facts.append(fact.astype(F32).astype(BF16))
    meta_t = dot(jnp.concatenate(facts, 1), jnp.concatenate(hots, 1), NT)
    meta = jnp.transpose(jnp.concatenate([meta_t, jnp.zeros((LANES - SUB, LANES), F32)], 0))
    first_row, first_lane, inside = column_facts(meta, sz)
    hot = ones_where(inside).astype(BF16)
    before_in = ones_where(iota(square, 0) < iota(square, 1)).astype(BF16)
    slot = (first_lane + dot(hot, before_in)).astype(I32)
    second = slot >= LANES
    slot_lane = slot & (LANES - 1)

    loads[0].wait()
    for r in range(rows):
        window_ref[r : r + 1, :] = block[0, 0:1, r * LANES : (r + 1) * LANES]
        window_ref[rows + r : rows + r + 1, :] = block[1, 0:1, r * LANES : (r + 1) * LANES]
    window = jnp.concatenate([window_ref[0:rows, :], window_ref[rows : 2 * rows, :]], 1)
    high, low = split(window)
    row_of = first_row.astype(I32)[:, 0:rows]
    which = iota((LANES, rows), 1)
    near = ones_where(which == row_of).astype(BF16)
    far = ones_where(which == row_of + 1).astype(BF16)
    near_w = dot(near, high) + dot(near, low)
    far_w = dot(far, high) + dot(far, low)
    sticks = []
    for part in range(2):
        cut = slice(part * LANES, (part + 1) * LANES)
        value = jnp.where(second, pick(far_w[:, cut], slot_lane), pick(near_w[:, cut], slot_lane))
        sticks.append(jnp.where(inside, value, 0.0))
    sticks = jnp.concatenate(sticks, 1)
    loads[1].wait()
    depth = dot3((table[0], table[1]), split(sticks), NT)

    channels, layers, devices = sz.channels, sz.layers, sz.devices
    ids = jnp.where(
        meta_t[4:5, :] > 0.5, meta_t[0:1, :] * sz.extent + meta_t[1:2, :], -1.0
    )
    ids = jnp.broadcast_to(ids, (devices, LANES))
    rows_ref[...] = depth

    def item(i):
        return ids if i == channels else rows_ref[pl.ds(i, devices, stride=channels), :]

    for r in range(sz.out_rows):
        send_ref[pl.ds(r, devices, stride=sz.rows), :] = pack_row(r, item, sz.out_pieces)
    loads[2].wait()
    for al in range(layers):
        turned[...] = jnp.transpose(pot[al])
        for p in range(layers):
            at = sz.out_rows + al * layers + p
            send_ref[pl.ds(at, devices, stride=sz.rows), :] = turned[
                pl.ds(p, devices, stride=layers), :
            ]
    length = dot(hot, all_ones).astype(I32)
    shift = iota(square, 1) - first_lane.astype(I32)
    top = lax.shift_right_arithmetic(length - 1, 1)
    for turn in range(2):
        p = shift + turn * LANES
        held = (p >= 0) & (p < length)
        depth_of = jnp.where(p <= top, p, p + sz.extent - length) & (sz.extent - 1)
        depth_ref[turn] = jnp.where(held, depth_of, -1)
    row_t = jnp.broadcast_to(meta_t[2:3, :].astype(I32), shape)
    slot_hot_ref[...] = jnp.concatenate(
        [ones_where(row == row_t), ones_where(row == row_t + 1)], 1
    ).astype(BF16)
    fa = signed(col_a & (sz.extent - 1), sz.extent)
    fb = signed(col_b, sz.extent)
    fc = signed(cells & (sz.extent - 1), sz.extent)
    kinetic = (fa * fa + fb * fb + fc * fc).astype(F32) / (RADIUS * RADIUS)
    kinetic_ref[...] = jnp.where(live, kinetic, -1.0)
    bands.wait()


def plane_kernel(sz, recv_ref, fb_ref, fa_ref, ia_ref, ib_ref, orbitals_ref,
                 out_ref, middle_ref,
                 fb, fa, ia, ib, hot_ref, planes, back, group_ref, z_ref, sems, band_sems):
    bands = BandLoads(orbitals_ref, middle_ref, band_sems, EARLY, MIDDLE)
    bands.start()
    copies = [
        pltpu.make_async_copy(src, dst, sems.at[i])
        for i, (src, dst) in enumerate([(fb_ref, fb), (fa_ref, fa), (ia_ref, ia), (ib_ref, ib)])
    ]
    for c in copies:
        c.start()
    devices, layers, channels = sz.devices, sz.layers, sz.channels

    def recv_row(r):
        return recv_ref[pl.ds(r, devices, stride=sz.rows), :]

    def recv_item(i):
        return unpack_item(i, sz.out_rows, recv_row, sz.out_pieces)

    lane = iota((devices, LANES), 1)
    ids = jnp.where(lane < sz.sticks, recv_item(channels), -1.0).astype(I32)
    if channels < SUB:
        z_ref[...] = jnp.zeros(z_ref.shape, F32)
    for i in range(channels):
        z_ref[pl.ds(i, devices, stride=SUB), :] = recv_item(i)
    col_a = lax.shift_right_arithmetic(ids, int(math.log2(sz.extent)))
    col_b = ids & (sz.extent - 1)
    sa = (col_a + HALF) & (sz.extent - 1)
    sb = (col_b + HALF) & (sz.extent - 1)
    group = jnp.where(ids >= 0, lax.shift_right_arithmetic(sa, 2), -1)
    cell = (sa & 3) * (2 * HALF) + sb
    group_ref[...] = group
    two = (2 * SUB, LANES)
    cell_rows = [(iota(two, 0) + i).astype(F32).astype(BF16) for i in range(0, CELLS, 2 * SUB)]
    group_rows = [
        (lax.shift_right_logical(iota(two, 0), 3) + g).astype(F32).astype(BF16)
        for g in range(0, GROUPS, 2)
    ]
    one, zero = jnp.ones(two, BF16), jnp.zeros(two, BF16)
    cell, group_f = cell.astype(F32), group.astype(F32)
    left_high, left_low = [], []
    for e in range(devices):
        own_cell = jnp.broadcast_to(cell[e : e + 1, :], two).astype(BF16)
        own_group = jnp.broadcast_to(group_f[e : e + 1, :], two).astype(BF16)
        values = z_ref[e * SUB : (e + 1) * SUB, :]
        high, low = split(jnp.concatenate([values, values], 0))
        here = [own_group == g for g in group_rows]
        left_high.append(jnp.concatenate([jnp.where(h, high, zero) for h in here], 0))
        left_low.append(jnp.concatenate([jnp.where(h, low, zero) for h in here], 0))
        for i, rows in enumerate(cell_rows):
            hot_ref[2 * SUB * i : 2 * SUB * (i + 1), e * LANES : (e + 1) * LANES] = jnp.where(
                own_cell == rows, one, zero
            )
    left = jnp.concatenate(
        [jnp.concatenate(left_high, 1), jnp.concatenate(left_low, 1)], 0
    )
    spread = dot(left, hot_ref[...], NT)
    size = GROUPS * SUB
    spread = spread[:size] + spread[size:]
    for half in range(2):
        planes[half * size : (half + 1) * size, :] = spread[:, half * LANES : (half + 1) * LANES]

    def plane_part(part, p):
        return planes[pl.ds(part * layers + p, KROWS, stride=SUB), :]

    grid = jnp.concatenate(
        [
            jnp.concatenate([plane_part(part, p) for p in range(layers)], 0)
            for part in range(2)
        ],
        1,
    )
    copies[0].wait()
    grid = dot3(split(grid), (fb[0], fb[1]))
    grid = jnp.concatenate(
        [
            jnp.concatenate(
                [
                    grid[p * KROWS : (p + 1) * KROWS, q * LANES : (q + 1) * LANES]
                    for q in range(4)
                ],
                0,
            )
            for p in range(layers)
        ],
        1,
    )
    copies[1].wait()
    grid = dot3((fa[0], fa[1]), split(grid))
    potential = jnp.concatenate(
        [
            jnp.concatenate(
                [
                    recv_row(sz.out_rows + al * layers + p)
                    for al in range(layers)
                ],
                0,
            )
            for p in range(layers)
        ],
        1,
    )
    half = sz.extent
    field = jnp.concatenate([grid[0:half] * potential, grid[half:] * potential], 0)
    copies[2].wait()
    grid = dot3((ia[0], ia[1]), split(field))
    grid = jnp.concatenate(
        [
            jnp.concatenate(
                [
                    grid[q * KROWS : (q + 1) * KROWS, p * LANES : (p + 1) * LANES]
                    for q in range(4)
                ],
                1,
            )
            for p in range(layers)
        ],
        0,
    )
    copies[3].wait()
    grid = dot3(split(grid), (ib[0], ib[1]))
    for part in range(2):
        for p in range(layers):
            back[pl.ds(part * layers + p, KROWS, stride=SUB), :] = grid[
                p * KROWS : (p + 1) * KROWS, part * LANES : (part + 1) * LANES
            ]

    values = jnp.concatenate([back[:size, :], back[size:, :]], 1)
    values = jnp.concatenate(split(values), 0)
    for e in range(devices):
        found = dot(values, hot_ref[:, e * LANES : (e + 1) * LANES])
        found = found[:size] + found[size:]
        own = jnp.broadcast_to(group_ref[e : e + 1, :], (SUB, LANES))
        total = jnp.zeros((SUB, LANES), F32)
        for g in range(GROUPS):
            total = total + jnp.where(own == g, found[g * SUB : (g + 1) * SUB, :], 0.0)
        z_ref[e * SUB : (e + 1) * SUB, :] = total

    def back_item(i):
        return z_ref[pl.ds(i, devices, stride=SUB), :]

    for r in range(sz.back_rows):
        out_ref[pl.ds(r, devices, stride=sz.back_rows), :] = pack_row(
            r, back_item, sz.back_pieces
        )
    bands.wait()


def final_kernel(sz, back_ref, window_ref, table_ref, depth_ref, hot_ref, kinetic_ref,
                 early_ref, middle_ref,
                 orbitals_ref,
                 applied_out, tile_ref,
                 applied_ref, factors, late_ref, acc, band_sems, out_sem):
    done = EARLY + MIDDLE
    bands = BandLoads(orbitals_ref, late_ref, band_sems, done, sz.bands_all - done)
    bands.start()
    devices, layers, rows = sz.devices, sz.layers, sz.slot_rows
    square = (LANES, LANES)

    def back_row(r):
        return back_ref[pl.ds(r, devices, stride=sz.back_rows), :]

    values = jnp.concatenate(
        [
            unpack_item(i, sz.back_rows, back_row, sz.back_pieces)
            for i in range(sz.channels)
        ],
        0,
    )
    values = jnp.transpose(values)
    sticks = dot3(split(values), (table_ref[0], table_ref[1]))
    placed = []
    for turn in range(2):
        depth = depth_ref[turn]
        held = depth >= 0
        depth = depth & (sz.extent - 1)
        placed.append(
            jnp.concatenate(
                [
                    jnp.where(held, pick(sticks[:, q * LANES : (q + 1) * LANES], depth), 0.0)
                    for q in range(2)
                ],
                1,
            )
        )
    placed = split(jnp.concatenate(placed, 0))
    hot = hot_ref[...]
    local = dot(hot, placed[0]) + dot(hot, placed[1])
    kinetic = kinetic_ref[...]
    for part in range(2):
        own = window_ref[part * rows : (part + 1) * rows, :]
        full = kinetic * own + local[:, part * LANES : (part + 1) * LANES]
        applied_ref[part * rows : (part + 1) * rows, :] = jnp.where(kinetic >= 0.0, full, 0.0)
    store = pltpu.make_async_copy(applied_ref, applied_out, out_sem)
    store.start()
    a_re = applied_ref[0:rows, :]
    a_im = applied_ref[rows : 2 * rows, :]
    factors[0] = a_im
    factors[1] = a_re - a_im
    factors[2] = a_re + a_im

    def product_of(source, first, wait=None):
        def product(i, carry):
            if wait is not None:
                wait(i)
            start = pl.multiple_of(i * CHUNK, CHUNK)
            sums = [jnp.zeros((CHUNK, LANES), F32) for _ in range(3)]
            for r in range(rows):
                x = source[0, pl.ds(start, CHUNK), r * LANES : (r + 1) * LANES]
                y = source[1, pl.ds(start, CHUNK), r * LANES : (r + 1) * LANES]
                for q, value in enumerate((x + y, x, y)):
                    sums[q] = sums[q] + value * factors[q, r : r + 1, :]
            acc[0, pl.ds(first + start, CHUNK), :] = sums[0] + sums[1]
            acc[1, pl.ds(first + start, CHUNK), :] = sums[0] - sums[2]
            return carry

        lax.fori_loop(0, source.shape[1] // CHUNK, product, 0)

    product_of(early_ref, 0)
    product_of(middle_ref, EARLY)
    product_of(late_ref, done, bands.wait_one)
    blocks = sz.bands_all // LANES
    block_row = iota((blocks, LANES), 0)
    sums = []
    for part in range(2):
        total = jnp.zeros((blocks, LANES), F32)
        for i in range(blocks):
            hot_row = ones_where(block_row == i).astype(BF16)
            high, low = split(acc[part, i * LANES : (i + 1) * LANES, :])
            total = total + (dot(hot_row, high, NT) + dot(hot_row, low, NT))
        sums.append(total * (1.0 / (sz.slots * sz.devices)))
    width = sz.band_rows
    per_row = LANES // width
    lane = iota((blocks, LANES), 1)
    for q in range(per_row):
        real = pltpu.roll(sums[0], (-q * width) % LANES, 1)
        imag = pltpu.roll(sums[1], (width - q * width) % LANES, 1)
        tile_ref[pl.ds(q, blocks, stride=per_row), :] = jnp.where(lane < width, real, imag)
    store.wait()


def sum_kernel(sz, tile_ref, out_ref):
    width = sz.band_rows
    total = jnp.sum(tile_ref[...], axis=0, keepdims=True)
    for part in range(2):
        out_ref[part, :, :] = total[:, part * width : (part + 1) * width]


def full_spec():
    return pl.BlockSpec(memory_space=pltpu.VMEM)


def any_spec():
    return pl.BlockSpec(memory_space=pl.ANY)


def vmem(mib):
    return pltpu.CompilerParams(vmem_limit_bytes=mib << 20)


def run_spread(sz, cells, orbitals, potential, table, **kw):
    return pl.pallas_call(
        lambda *refs: spread_kernel(sz, *refs),
        out_shape=(
            jax.ShapeDtypeStruct((sz.devices * sz.rows, LANES), F32),
            jax.ShapeDtypeStruct((2 * sz.slot_rows, LANES), F32),
            jax.ShapeDtypeStruct((2, LANES, LANES), I32),
            jax.ShapeDtypeStruct((sz.slot_rows, 2 * LANES), BF16),
            jax.ShapeDtypeStruct((sz.slot_rows, LANES), F32),
            pltpu.VMEM((2, EARLY, sz.slots), F32),
        ),
        in_specs=[any_spec()] * 4,
        out_specs=(full_spec(),) * 6,
        scratch_shapes=[
            pltpu.VMEM((sz.slot_rows, LANES), I32),
            pltpu.VMEM((2, SUB, sz.slots), F32),
            pltpu.VMEM((sz.layers, LANES, LANES), F32),
            pltpu.VMEM(table.shape, BF16),
            pltpu.VMEM((LANES, LANES), F32),
            pltpu.VMEM((sz.devices * sz.channels, LANES), F32),
            pltpu.SemaphoreType.DMA((4,)),
            pltpu.SemaphoreType.DMA((EARLY // CHUNK,)),
        ],
        name="spread",
        compiler_params=vmem(8),
        **kw,
    )(cells, orbitals, potential, table)


def run_planes(sz, recv, tabs, orbitals, **kw):
    mats = [tabs[n] for n in ("forward_b", "forward_a", "inverse_a", "inverse_b")]
    return pl.pallas_call(
        lambda *refs: plane_kernel(sz, *refs),
        out_shape=(
            jax.ShapeDtypeStruct((sz.devices * sz.back_rows, LANES), F32),
            pltpu.VMEM((2, MIDDLE, sz.slots), F32),
        ),
        in_specs=[full_spec()] + [any_spec()] * 5,
        out_specs=(full_spec(), full_spec()),
        scratch_shapes=[pltpu.VMEM(m.shape, BF16) for m in mats]
        + [
            pltpu.VMEM((CELLS, sz.devices * LANES), BF16),
            pltpu.VMEM((KROWS * SUB, LANES), F32),
            pltpu.VMEM((KROWS * SUB, LANES), F32),
            pltpu.VMEM((sz.devices, LANES), I32),
            pltpu.VMEM((sz.devices * SUB, LANES), F32),
            pltpu.SemaphoreType.DMA((4,)),
            pltpu.SemaphoreType.DMA((MIDDLE // CHUNK,)),
        ],
        name="planes",
        compiler_params=vmem(16),
        **kw,
    )(recv, *mats, orbitals)


def run_final(sz, back, window, table, depth, hot, kinetic, early, middle, orbitals, **kw):
    late = sz.bands_all - EARLY - MIDDLE
    return pl.pallas_call(
        lambda *refs: final_kernel(sz, *refs),
        out_shape=(
            jax.ShapeDtypeStruct((2 * sz.slot_rows, LANES), F32),
            jax.ShapeDtypeStruct((sz.devices, LANES), F32),
        ),
        in_specs=[full_spec()] * 8 + [any_spec()],
        out_specs=(any_spec(), full_spec()),
        scratch_shapes=[
            pltpu.VMEM((2 * sz.slot_rows, LANES), F32),
            pltpu.VMEM((3, sz.slot_rows, LANES), F32),
            pltpu.VMEM((2, late, sz.slots), F32),
            pltpu.VMEM((2, sz.bands_all, LANES), F32),
            pltpu.SemaphoreType.DMA((late // CHUNK,)),
            pltpu.SemaphoreType.DMA,
        ],
        name="final",
        compiler_params=vmem(20),
        **kw,
    )(back, window, table, depth, hot, kinetic, early, middle, orbitals)


def run_sum(sz, tile, **kw):
    return pl.pallas_call(
        lambda *refs: sum_kernel(sz, *refs),
        out_shape=jax.ShapeDtypeStruct((2, 1, sz.band_rows), F32),
        in_specs=[full_spec()],
        out_specs=full_spec(),
        name="add",
        compiler_params=vmem(2),
        **kw,
    )(tile)


def exchange(x):
    rows = x.reshape(x.shape[0], 1, x.shape[1])
    return lax.all_to_all(rows, "ga", split_axis=0, concat_axis=0, tiled=True).reshape(x.shape)


def local(orbitals, coeff_cells, potential):
    devices = lax.axis_size("ga")
    sz = Sizes(devices, potential.shape[1], coeff_cells.shape[0], orbitals.shape[1])
    tabs = {name: jnp.asarray(value) for name, value in tables(sz).items()}
    cells = coeff_cells.reshape(sz.slot_rows, LANES)
    stay = lambda x: pltpu.with_memory_space_constraint(x, pltpu.HBM)
    orbitals = stay(orbitals)
    send, window, depth, hot, kinetic, early = run_spread(
        sz, stay(cells), orbitals, stay(potential), stay(tabs["forward_z"])
    )
    back, middle = run_planes(sz, exchange(send), tabs, orbitals)
    applied, tile = run_final(
        sz, exchange(back), window, tabs["inverse_z"], depth, hot, kinetic, early, middle, orbitals
    )
    subspace = run_sum(sz, exchange(tile))
    return (
        applied.reshape(2, 1, sz.slots),
        jnp.transpose(subspace, (2, 0, 1)),
    )


def solution(mesh):
    in_specs = (P(None, "kpt", "ga"), P("ga"), P("ga", None, None))
    out_specs = (P(None, "kpt", "ga"), P("ga", None, "kpt"))
    return jax.shard_map(local, mesh=mesh, in_specs=in_specs, out_specs=out_specs, check_vma=False)
```

```python
import math

import jax
import jax.numpy as jnp
import numpy as np
from jax import lax
from jax.experimental import pallas as pl
from jax.experimental.pallas import tpu as pltpu
from jax.sharding import PartitionSpec as P

RADIUS = 30
LANES = 128
SUB = 8
HALF = 32
KROWS = 32
CELLS = 4 * 2 * HALF
GROUPS = KROWS // 2
CHUNK = 64
EARLY = 192
MIDDLE = 384
F32 = jnp.float32
BF16 = jnp.bfloat16
I32 = jnp.int32

NT = ((1,), (1,))
NN = ((1,), (0,))


def column_total(extent):
    indices = np.arange(extent)
    frequency = np.where(indices < extent // 2, indices, indices - extent)
    return int(np.sum(frequency[:, None] ** 2 + frequency[None, :] ** 2 <= RADIUS * RADIUS))


def packing(items, width):
    spare = LANES - width
    base = next(b for b in range(1, items + 1) if (items - b) * width <= b * spare)
    pieces = []
    row, at = 0, width
    for item in range(base, items):
        done = 0
        while done < width:
            if at == LANES:
                row, at = row + 1, width
            length = min(width - done, LANES - at)
            pieces.append((item, done, row, at, length))
            done, at = done + length, at + length
    return base, pieces


def pack_row(row, load, pieces):
    value = load(row)
    lane = lax.broadcasted_iota(I32, value.shape, 1)
    for item, source, target_row, target, length in pieces:
        if target_row == row:
            moved = pltpu.roll(load(item), (target - source) % LANES, 1)
            value = jnp.where((lane >= target) & (lane < target + length), moved, value)
    return value


def unpack_item(item, base, load, pieces):
    if item < base:
        return load(item)
    value = None
    for owner, source, row, at, length in pieces:
        if owner == item:
            moved = pltpu.roll(load(row), (source - at) % LANES, 1)
            lane = lax.broadcasted_iota(I32, moved.shape, 1)
            value = moved if value is None else jnp.where(lane >= source, moved, value)
    return value


class Sizes:
    def __init__(self, devices, extent, slots, bands_all):
        self.devices = devices
        self.extent = extent
        self.layers = extent // devices
        self.channels = 2 * self.layers
        self.slot_rows = slots // LANES
        self.slots = slots
        self.sticks = -(-column_total(extent) // devices)
        self.out_rows, self.out_pieces = packing(self.channels + 1, self.sticks)
        self.back_rows, self.back_pieces = packing(self.channels, self.sticks)
        self.rows = self.out_rows + self.layers * self.layers
        self.bands_all = bands_all
        self.band_rows = bands_all // devices
        assert extent == LANES and self.channels <= SUB


def parts_of(matrix):
    values = np.asarray(matrix, np.float32)
    high = values.astype(jnp.bfloat16)
    low = (values - high.astype(np.float32)).astype(jnp.bfloat16)
    return np.stack([high, low])


def angle(x, y, extent):
    phase = (x[:, None] * y[None, :]) % extent
    return 2.0 * math.pi * phase.astype(np.float64) / extent


def tables(sz):
    n, d, layers = sz.extent, sz.devices, sz.layers
    cells = np.arange(n)
    dev, part, lay = np.meshgrid(np.arange(d), np.arange(2), np.arange(layers), indexing="ij")
    z_rows = (dev * layers + lay).reshape(-1)
    part_rows = part.reshape(-1)
    t = angle(z_rows, cells, n)
    re, im = np.cos(t), np.sin(t)
    is_im = part_rows[:, None] == 1
    forward_z = np.concatenate([np.where(is_im, im, re), np.where(is_im, re, -im)], 1)
    freq = np.arange(2 * HALF) - HALF
    tb = angle(freq, cells, n)
    cb, sb = np.cos(tb), np.sin(tb)
    eye = np.eye(2)
    cc, ss = np.kron(eye, cb), np.kron(eye, sb)
    forward_b = np.block([[cc, ss], [-ss, cc]])
    cct, sst = cc.T, ss.T
    inverse_b = np.block([[cct, -sst], [sst, cct]])
    a_rows = (np.arange(d)[None, :] * layers + np.arange(layers)[:, None]).reshape(-1)
    lo, k = np.meshgrid(np.arange(2), np.arange(KROWS), indexing="ij")
    a_freq = (4 * (k % GROUPS) + 2 * (k // GROUPS) + lo - HALF).reshape(-1)
    ta = angle(a_rows, a_freq, n)
    ca, sa = np.cos(ta), np.sin(ta)
    forward_a = np.block([[ca, -sa], [sa, ca]])
    inverse_a = np.block([[ca.T, sa.T], [-sa.T, ca.T]])
    part2, lay2, dev2 = np.meshgrid(np.arange(2), np.arange(layers), np.arange(d), indexing="ij")
    t2 = angle((dev2 * layers + lay2).reshape(-1), cells, n)
    re2, im2 = np.cos(t2) / n**3, np.sin(t2) / n**3
    im_rows = part2.reshape(-1)[:, None] == 1
    inverse_z = np.concatenate([np.where(im_rows, im2, re2), np.where(im_rows, re2, -im2)], 1)
    return {
        "forward_z": parts_of(forward_z),
        "forward_b": parts_of(forward_b),
        "forward_a": parts_of(forward_a),
        "inverse_a": parts_of(inverse_a),
        "inverse_b": parts_of(inverse_b),
        "inverse_z": parts_of(inverse_z),
    }


def split(x):
    high = x.astype(BF16)
    return high, (x - high.astype(F32)).astype(BF16)


def dot(a, b, dims=NN):
    return lax.dot_general(a, b, (dims, ((), ())), preferred_element_type=F32)


def dot3(a, b, dims=NN):
    return dot(a[0], b[0], dims) + dot(a[0], b[1], dims) + dot(a[1], b[0], dims)


def iota(shape, dim):
    return lax.broadcasted_iota(I32, shape, dim)


def ones_where(mask):
    return jnp.where(mask, 1.0, 0.0).astype(F32)


def pick(values, lanes):
    return jnp.take_along_axis(values, lanes, axis=1, mode="promise_in_bounds")


def signed(x, extent):
    return jnp.where(x < extent // 2, x, x - extent)


def column_facts(meta, sz):
    shape = (LANES, LANES)
    col_a = jnp.broadcast_to(meta[:, 0:1], shape)
    col_b = jnp.broadcast_to(meta[:, 1:2], shape)
    row = jnp.broadcast_to(meta[:, 2:3], shape)
    lane = jnp.broadcast_to(meta[:, 3:4], shape)
    valid = jnp.broadcast_to(meta[:, 4:5], shape) > 0.5
    fa = jnp.where(col_a < sz.extent // 2, col_a, col_a - sz.extent)
    fb = jnp.where(col_b < sz.extent // 2, col_b, col_b - sz.extent)
    fc = signed(iota(shape, 1), sz.extent).astype(F32)
    inside = valid & (fc * fc <= RADIUS * RADIUS - fa * fa - fb * fb)
    return row, lane, inside


class BandLoads:
    def __init__(self, source, target, sems, first, count):
        self.refs = (source, target, sems, first)
        self.count = count // CHUNK

    def copy(self, i):
        source, target, sems, first = self.refs
        return pltpu.make_async_copy(
            source.at[:, pl.ds(first + i * CHUNK, CHUNK), :],
            target.at[:, pl.ds(i * CHUNK, CHUNK), :],
            sems.at[i],
        )

    def start(self):
        for i in range(self.count):
            self.copy(i).start()

    def wait_one(self, i):
        self.copy(i).wait()

    def wait(self):
        for i in range(self.count):
            self.copy(i).wait()


def spread_kernel(sz, cells_ref, orbitals_ref, potential_ref, table_ref,
                  send_ref, window_ref, depth_ref, slot_hot_ref, kinetic_ref, early_ref,
                  cells_in, block, pot, table, turned, rows_ref, sems, band_sems):
    loads = [
        pltpu.make_async_copy(orbitals_ref.at[:, pl.ds(0, SUB), :], block, sems.at[0]),
        pltpu.make_async_copy(table_ref, table, sems.at[1]),
        pltpu.make_async_copy(potential_ref, pot, sems.at[2]),
    ]
    cell_load = pltpu.make_async_copy(cells_ref, cells_in, sems.at[3])
    cell_load.start()
    for load in loads:
        load.start()
    bands = BandLoads(orbitals_ref, early_ref, band_sems, 0, EARLY)
    bands.start()
    cell_load.wait()
    rows = sz.slot_rows
    shape = (rows, LANES)
    cells = cells_in[...]
    live = cells >= 0
    column = lax.shift_right_arithmetic(cells, int(math.log2(sz.extent)))
    rolled = pltpu.roll(column, 1, 1)
    above = pltpu.roll(rolled, 1, 0)
    lane = iota(shape, 1)
    row = iota(shape, 0)
    before = jnp.where(lane == 0, jnp.where(row == 0, -1, above), rolled)
    starts = live & (column != before)
    flags = ones_where(starts).astype(BF16)
    square = (LANES, LANES)
    upto = ones_where(iota(square, 0) <= iota(square, 1)).astype(BF16)
    all_ones = jnp.ones(square, BF16)
    within = dot(flags, upto)
    totals = dot(flags, all_ones)
    lower = ones_where(iota((rows, rows), 1) < iota((rows, rows), 0)).astype(BF16)
    rank = (within + dot(lower, totals.astype(BF16))).astype(I32) - 1
    rank = jnp.where(starts, rank, -1)
    col_a = lax.shift_right_arithmetic(column, int(math.log2(sz.extent)))
    col_b = column & (sz.extent - 1)
    sub = iota((SUB, LANES), 0)
    lane8 = iota((SUB, LANES), 1)
    place = iota(square, 0)
    hots, facts = [], []
    for r in range(rows):
        hots.append(ones_where(place == rank[r : r + 1, :]).astype(BF16))
        fact = jnp.where(sub == 0, col_a[r : r + 1, :], col_b[r : r + 1, :])
        fact = jnp.where(sub == 2, r, fact)
        fact = jnp.where(sub == 3, lane8, fact)
        fact = jnp.where(sub == 4, 1, fact)
        facts.append(fact.astype(F32).astype(BF16))
    meta_t = dot(jnp.concatenate(facts, 1), jnp.concatenate(hots, 1), NT)
    meta = jnp.transpose(jnp.concatenate([meta_t, jnp.zeros((LANES - SUB, LANES), F32)], 0))
    first_row, first_lane, inside = column_facts(meta, sz)
    hot = ones_where(inside).astype(BF16)
    before_in = ones_where(iota(square, 0) < iota(square, 1)).astype(BF16)
    slot = (first_lane + dot(hot, before_in)).astype(I32)
    second = slot >= LANES
    slot_lane = slot & (LANES - 1)

    loads[0].wait()
    for r in range(rows):
        window_ref[r : r + 1, :] = block[0, 0:1, r * LANES : (r + 1) * LANES]
        window_ref[rows + r : rows + r + 1, :] = block[1, 0:1, r * LANES : (r + 1) * LANES]
    window = jnp.concatenate([window_ref[0:rows, :], window_ref[rows : 2 * rows, :]], 1)
    high, low = split(window)
    row_of = first_row.astype(I32)[:, 0:rows]
    which = iota((LANES, rows), 1)
    near = ones_where(which == row_of).astype(BF16)
    far = ones_where(which == row_of + 1).astype(BF16)
    near_w = dot(near, high) + dot(near, low)
    far_w = dot(far, high) + dot(far, low)
    sticks = []
    for part in range(2):
        cut = slice(part * LANES, (part + 1) * LANES)
        value = jnp.where(second, pick(far_w[:, cut], slot_lane), pick(near_w[:, cut], slot_lane))
        sticks.append(jnp.where(inside, value, 0.0))
    sticks = jnp.concatenate(sticks, 1)
    loads[1].wait()
    depth = dot3((table[0], table[1]), split(sticks), NT)

    channels, layers, devices = sz.channels, sz.layers, sz.devices
    ids = jnp.where(
        meta_t[4:5, :] > 0.5, meta_t[0:1, :] * sz.extent + meta_t[1:2, :], -1.0
    )
    ids = jnp.broadcast_to(ids, (devices, LANES))
    rows_ref[...] = depth

    def item(i):
        return ids if i == channels else rows_ref[pl.ds(i, devices, stride=channels), :]

    for r in range(sz.out_rows):
        send_ref[pl.ds(r, devices, stride=sz.rows), :] = pack_row(r, item, sz.out_pieces)
    loads[2].wait()
    for al in range(layers):
        turned[...] = jnp.transpose(pot[al])
        for p in range(layers):
            at = sz.out_rows + al * layers + p
            send_ref[pl.ds(at, devices, stride=sz.rows), :] = turned[
                pl.ds(p, devices, stride=layers), :
            ]
    length = dot(hot, all_ones).astype(I32)
    shift = iota(square, 1) - first_lane.astype(I32)
    top = lax.shift_right_arithmetic(length - 1, 1)
    for turn in range(2):
        p = shift + turn * LANES
        held = (p >= 0) & (p < length)
        depth_of = jnp.where(p <= top, p, p + sz.extent - length) & (sz.extent - 1)
        depth_ref[turn] = jnp.where(held, depth_of, -1)
    row_t = jnp.broadcast_to(meta_t[2:3, :].astype(I32), shape)
    slot_hot_ref[...] = jnp.concatenate(
        [ones_where(row == row_t), ones_where(row == row_t + 1)], 1
    ).astype(BF16)
    fa = signed(col_a & (sz.extent - 1), sz.extent)
    fb = signed(col_b, sz.extent)
    fc = signed(cells & (sz.extent - 1), sz.extent)
    kinetic = (fa * fa + fb * fb + fc * fc).astype(F32) / (RADIUS * RADIUS)
    kinetic_ref[...] = jnp.where(live, kinetic, -1.0)
    bands.wait()


def plane_kernel(sz, recv_ref, fb_ref, fa_ref, ia_ref, ib_ref, orbitals_ref,
                 out_ref, middle_ref,
                 fb, fa, ia, ib, hot_ref, planes, back, group_ref, z_ref, sems, band_sems):
    bands = BandLoads(orbitals_ref, middle_ref, band_sems, EARLY, MIDDLE)
    bands.start()
    copies = [
        pltpu.make_async_copy(src, dst, sems.at[i])
        for i, (src, dst) in enumerate([(fb_ref, fb), (fa_ref, fa), (ia_ref, ia), (ib_ref, ib)])
    ]
    for c in copies:
        c.start()
    devices, layers, channels = sz.devices, sz.layers, sz.channels

    def recv_row(r):
        return recv_ref[pl.ds(r, devices, stride=sz.rows), :]

    def recv_item(i):
        return unpack_item(i, sz.out_rows, recv_row, sz.out_pieces)

    lane = iota((devices, LANES), 1)
    ids = jnp.where(lane < sz.sticks, recv_item(channels), -1.0).astype(I32)
    if channels < SUB:
        z_ref[...] = jnp.zeros(z_ref.shape, F32)
    for i in range(channels):
        z_ref[pl.ds(i, devices, stride=SUB), :] = recv_item(i)
    col_a = lax.shift_right_arithmetic(ids, int(math.log2(sz.extent)))
    col_b = ids & (sz.extent - 1)
    sa = (col_a + HALF) & (sz.extent - 1)
    sb = (col_b + HALF) & (sz.extent - 1)
    group = jnp.where(ids >= 0, lax.shift_right_arithmetic(sa, 2), -1)
    cell = (sa & 3) * (2 * HALF) + sb
    group_ref[...] = group
    two = (2 * SUB, LANES)
    cell_rows = [(iota(two, 0) + i).astype(F32).astype(BF16) for i in range(0, CELLS, 2 * SUB)]
    group_rows = [
        (lax.shift_right_logical(iota(two, 0), 3) + g).astype(F32).astype(BF16)
        for g in range(0, GROUPS, 2)
    ]
    one, zero = jnp.ones(two, BF16), jnp.zeros(two, BF16)
    cell, group_f = cell.astype(F32), group.astype(F32)
    left_high, left_low = [], []
    for e in range(devices):
        own_cell = jnp.broadcast_to(cell[e : e + 1, :], two).astype(BF16)
        own_group = jnp.broadcast_to(group_f[e : e + 1, :], two).astype(BF16)
        values = z_ref[e * SUB : (e + 1) * SUB, :]
        high, low = split(jnp.concatenate([values, values], 0))
        here = [own_group == g for g in group_rows]
        left_high.append(jnp.concatenate([jnp.where(h, high, zero) for h in here], 0))
        left_low.append(jnp.concatenate([jnp.where(h, low, zero) for h in here], 0))
        for i, rows in enumerate(cell_rows):
            hot_ref[2 * SUB * i : 2 * SUB * (i + 1), e * LANES : (e + 1) * LANES] = jnp.where(
                own_cell == rows, one, zero
            )
    left = jnp.concatenate(
        [jnp.concatenate(left_high, 1), jnp.concatenate(left_low, 1)], 0
    )
    spread = dot(left, hot_ref[...], NT)
    size = GROUPS * SUB
    spread = spread[:size] + spread[size:]
    for half in range(2):
        planes[half * size : (half + 1) * size, :] = spread[:, half * LANES : (half + 1) * LANES]

    def plane_part(part, p):
        return planes[pl.ds(part * layers + p, KROWS, stride=SUB), :]

    grid = jnp.concatenate(
        [
            jnp.concatenate([plane_part(part, p) for p in range(layers)], 0)
            for part in range(2)
        ],
        1,
    )
    copies[0].wait()
    grid = dot3(split(grid), (fb[0], fb[1]))
    grid = jnp.concatenate(
        [
            jnp.concatenate(
                [
                    grid[p * KROWS : (p + 1) * KROWS, q * LANES : (q + 1) * LANES]
                    for q in range(4)
                ],
                0,
            )
            for p in range(layers)
        ],
        1,
    )
    copies[1].wait()
    grid = dot3((fa[0], fa[1]), split(grid))
    potential = jnp.concatenate(
        [
            jnp.concatenate(
                [
                    recv_row(sz.out_rows + al * layers + p)
                    for al in range(layers)
                ],
                0,
            )
            for p in range(layers)
        ],
        1,
    )
    half = sz.extent
    field = jnp.concatenate([grid[0:half] * potential, grid[half:] * potential], 0)
    copies[2].wait()
    grid = dot3((ia[0], ia[1]), split(field))
    grid = jnp.concatenate(
        [
            jnp.concatenate(
                [
                    grid[q * KROWS : (q + 1) * KROWS, p * LANES : (p + 1) * LANES]
                    for q in range(4)
                ],
                1,
            )
            for p in range(layers)
        ],
        0,
    )
    copies[3].wait()
    grid = dot3(split(grid), (ib[0], ib[1]))
    for part in range(2):
        for p in range(layers):
            back[pl.ds(part * layers + p, KROWS, stride=SUB), :] = grid[
                p * KROWS : (p + 1) * KROWS, part * LANES : (part + 1) * LANES
            ]

    values = jnp.concatenate([back[:size, :], back[size:, :]], 1)
    values = jnp.concatenate(split(values), 0)
    for e in range(devices):
        found = dot(values, hot_ref[:, e * LANES : (e + 1) * LANES])
        found = found[:size] + found[size:]
        own = jnp.broadcast_to(group_ref[e : e + 1, :], (SUB, LANES))
        total = jnp.zeros((SUB, LANES), F32)
        for g in range(GROUPS):
            total = total + jnp.where(own == g, found[g * SUB : (g + 1) * SUB, :], 0.0)
        z_ref[e * SUB : (e + 1) * SUB, :] = total

    def back_item(i):
        return z_ref[pl.ds(i, devices, stride=SUB), :]

    for r in range(sz.back_rows):
        out_ref[pl.ds(r, devices, stride=sz.back_rows), :] = pack_row(
            r, back_item, sz.back_pieces
        )
    bands.wait()


def final_kernel(sz, back_ref, window_ref, table_ref, depth_ref, hot_ref, kinetic_ref,
                 early_ref, middle_ref,
                 orbitals_ref,
                 applied_out, tile_ref,
                 applied_ref, factors, late_ref, acc, sums_ref, band_sems, out_sem):
    done = EARLY + MIDDLE
    bands = BandLoads(orbitals_ref, late_ref, band_sems, done, sz.bands_all - done)
    bands.start()
    devices, layers, rows = sz.devices, sz.layers, sz.slot_rows
    square = (LANES, LANES)

    def back_row(r):
        return back_ref[pl.ds(r, devices, stride=sz.back_rows), :]

    values = jnp.concatenate(
        [
            unpack_item(i, sz.back_rows, back_row, sz.back_pieces)
            for i in range(sz.channels)
        ],
        0,
    )
    values = jnp.transpose(values)
    sticks = dot3(split(values), (table_ref[0], table_ref[1]))
    placed = []
    for turn in range(2):
        depth = depth_ref[turn]
        held = depth >= 0
        depth = depth & (sz.extent - 1)
        placed.append(
            jnp.concatenate(
                [
                    jnp.where(held, pick(sticks[:, q * LANES : (q + 1) * LANES], depth), 0.0)
                    for q in range(2)
                ],
                1,
            )
        )
    placed = split(jnp.concatenate(placed, 0))
    hot = hot_ref[...]
    local = dot(hot, placed[0]) + dot(hot, placed[1])
    kinetic = kinetic_ref[...]
    for part in range(2):
        own = window_ref[part * rows : (part + 1) * rows, :]
        full = kinetic * own + local[:, part * LANES : (part + 1) * LANES]
        applied_ref[part * rows : (part + 1) * rows, :] = jnp.where(kinetic >= 0.0, full, 0.0)
    store = pltpu.make_async_copy(applied_ref, applied_out, out_sem)
    store.start()
    a_re = applied_ref[0:rows, :]
    a_im = applied_ref[rows : 2 * rows, :]
    factors[0] = a_im
    factors[1] = a_re - a_im
    factors[2] = a_re + a_im

    blocks = sz.bands_all // LANES
    block_row = iota((blocks, LANES), 0)
    sums_ref[...] = jnp.zeros(sums_ref.shape, F32)

    def product_of(source, first, wait=None):
        def product(i, carry):
            if wait is not None:
                wait(i)
            start = pl.multiple_of(i * CHUNK, CHUNK)
            sums = [jnp.zeros((CHUNK, LANES), F32) for _ in range(3)]
            for r in range(rows):
                x = source[0, pl.ds(start, CHUNK), r * LANES : (r + 1) * LANES]
                y = source[1, pl.ds(start, CHUNK), r * LANES : (r + 1) * LANES]
                for q, value in enumerate((x + y, x, y)):
                    sums[q] = sums[q] + value * factors[q, r : r + 1, :]
            end = first + (i + 1) * CHUNK
            at = pl.multiple_of((end - CHUNK) % LANES, CHUNK)
            acc[0, pl.ds(at, CHUNK), :] = sums[0] + sums[1]
            acc[1, pl.ds(at, CHUNK), :] = sums[0] - sums[2]

            @pl.when(end % LANES == 0)
            def _():
                hot_row = ones_where(block_row == end // LANES - 1).astype(BF16)
                for part in range(2):
                    high, low = split(acc[part])
                    sums_ref[part] += dot(hot_row, high, NT) + dot(hot_row, low, NT)

            return carry

        lax.fori_loop(0, source.shape[1] // CHUNK, product, 0)

    product_of(early_ref, 0)
    product_of(middle_ref, EARLY)
    product_of(late_ref, done, bands.wait_one)
    sums = [sums_ref[part] * (1.0 / (sz.slots * sz.devices)) for part in range(2)]
    width = sz.band_rows
    per_row = LANES // width
    lane = iota((blocks, LANES), 1)
    for q in range(per_row):
        real = pltpu.roll(sums[0], (-q * width) % LANES, 1)
        imag = pltpu.roll(sums[1], (width - q * width) % LANES, 1)
        tile_ref[pl.ds(q, blocks, stride=per_row), :] = jnp.where(lane < width, real, imag)
    store.wait()


def sum_kernel(sz, tile_ref, out_ref):
    width = sz.band_rows
    total = jnp.sum(tile_ref[...], axis=0, keepdims=True)
    for part in range(2):
        out_ref[part, :, :] = total[:, part * width : (part + 1) * width]


def full_spec():
    return pl.BlockSpec(memory_space=pltpu.VMEM)


def any_spec():
    return pl.BlockSpec(memory_space=pl.ANY)


def vmem(mib):
    return pltpu.CompilerParams(vmem_limit_bytes=mib << 20)


def run_spread(sz, cells, orbitals, potential, table, **kw):
    return pl.pallas_call(
        lambda *refs: spread_kernel(sz, *refs),
        out_shape=(
            jax.ShapeDtypeStruct((sz.devices * sz.rows, LANES), F32),
            jax.ShapeDtypeStruct((2 * sz.slot_rows, LANES), F32),
            jax.ShapeDtypeStruct((2, LANES, LANES), I32),
            jax.ShapeDtypeStruct((sz.slot_rows, 2 * LANES), BF16),
            jax.ShapeDtypeStruct((sz.slot_rows, LANES), F32),
            pltpu.VMEM((2, EARLY, sz.slots), F32),
        ),
        in_specs=[any_spec()] * 4,
        out_specs=(full_spec(),) * 6,
        scratch_shapes=[
            pltpu.VMEM((sz.slot_rows, LANES), I32),
            pltpu.VMEM((2, SUB, sz.slots), F32),
            pltpu.VMEM((sz.layers, LANES, LANES), F32),
            pltpu.VMEM(table.shape, BF16),
            pltpu.VMEM((LANES, LANES), F32),
            pltpu.VMEM((sz.devices * sz.channels, LANES), F32),
            pltpu.SemaphoreType.DMA((4,)),
            pltpu.SemaphoreType.DMA((EARLY // CHUNK,)),
        ],
        name="spread",
        compiler_params=vmem(8),
        **kw,
    )(cells, orbitals, potential, table)


def run_planes(sz, recv, tabs, orbitals, **kw):
    mats = [tabs[n] for n in ("forward_b", "forward_a", "inverse_a", "inverse_b")]
    return pl.pallas_call(
        lambda *refs: plane_kernel(sz, *refs),
        out_shape=(
            jax.ShapeDtypeStruct((sz.devices * sz.back_rows, LANES), F32),
            pltpu.VMEM((2, MIDDLE, sz.slots), F32),
        ),
        in_specs=[full_spec()] + [any_spec()] * 5,
        out_specs=(full_spec(), full_spec()),
        scratch_shapes=[pltpu.VMEM(m.shape, BF16) for m in mats]
        + [
            pltpu.VMEM((CELLS, sz.devices * LANES), BF16),
            pltpu.VMEM((KROWS * SUB, LANES), F32),
            pltpu.VMEM((KROWS * SUB, LANES), F32),
            pltpu.VMEM((sz.devices, LANES), I32),
            pltpu.VMEM((sz.devices * SUB, LANES), F32),
            pltpu.SemaphoreType.DMA((4,)),
            pltpu.SemaphoreType.DMA((MIDDLE // CHUNK,)),
        ],
        name="planes",
        compiler_params=vmem(16),
        **kw,
    )(recv, *mats, orbitals)


def run_final(sz, back, window, table, depth, hot, kinetic, early, middle, orbitals, **kw):
    late = sz.bands_all - EARLY - MIDDLE
    return pl.pallas_call(
        lambda *refs: final_kernel(sz, *refs),
        out_shape=(
            jax.ShapeDtypeStruct((2 * sz.slot_rows, LANES), F32),
            jax.ShapeDtypeStruct((sz.devices, LANES), F32),
        ),
        in_specs=[full_spec()] * 8 + [any_spec()],
        out_specs=(any_spec(), full_spec()),
        scratch_shapes=[
            pltpu.VMEM((2 * sz.slot_rows, LANES), F32),
            pltpu.VMEM((3, sz.slot_rows, LANES), F32),
            pltpu.VMEM((2, late, sz.slots), F32),
            pltpu.VMEM((2, LANES, LANES), F32),
            pltpu.VMEM((2, sz.bands_all // LANES, LANES), F32),
            pltpu.SemaphoreType.DMA((late // CHUNK,)),
            pltpu.SemaphoreType.DMA,
        ],
        name="final",
        compiler_params=vmem(20),
        **kw,
    )(back, window, table, depth, hot, kinetic, early, middle, orbitals)


def run_sum(sz, tile, **kw):
    return pl.pallas_call(
        lambda *refs: sum_kernel(sz, *refs),
        out_shape=jax.ShapeDtypeStruct((2, 1, sz.band_rows), F32),
        in_specs=[full_spec()],
        out_specs=full_spec(),
        name="add",
        compiler_params=vmem(2),
        **kw,
    )(tile)


def exchange(x):
    rows = x.reshape(x.shape[0], 1, x.shape[1])
    return lax.all_to_all(rows, "ga", split_axis=0, concat_axis=0, tiled=True).reshape(x.shape)


def local(orbitals, coeff_cells, potential):
    devices = lax.axis_size("ga")
    sz = Sizes(devices, potential.shape[1], coeff_cells.shape[0], orbitals.shape[1])
    tabs = {name: jnp.asarray(value) for name, value in tables(sz).items()}
    cells = coeff_cells.reshape(sz.slot_rows, LANES)
    stay = lambda x: pltpu.with_memory_space_constraint(x, pltpu.HBM)
    orbitals = stay(orbitals)
    send, window, depth, hot, kinetic, early = run_spread(
        sz, stay(cells), orbitals, stay(potential), stay(tabs["forward_z"])
    )
    back, middle = run_planes(sz, exchange(send), tabs, orbitals)
    applied, tile = run_final(
        sz, exchange(back), window, tabs["inverse_z"], depth, hot, kinetic, early, middle, orbitals
    )
    subspace = run_sum(sz, exchange(tile))
    return (
        applied.reshape(2, 1, sz.slots),
        jnp.transpose(subspace, (2, 0, 1)),
    )


def solution(mesh):
    in_specs = (P(None, "kpt", "ga"), P("ga"), P("ga", None, None))
    out_specs = (P(None, "kpt", "ga"), P("ga", None, "kpt"))
    return jax.shard_map(local, mesh=mesh, in_specs=in_specs, out_specs=out_specs, check_vma=False)
```

```python
import math

import jax
import jax.numpy as jnp
import numpy as np
from jax import lax
from jax.experimental import pallas as pl
from jax.experimental.pallas import tpu as pltpu
from jax.sharding import PartitionSpec as P

RADIUS = 30
LANES = 128
SUB = 8
HALF = 32
KROWS = 32
CELLS = 4 * 2 * HALF
GROUPS = KROWS // 2
CHUNK = 64
EARLY = 192
MIDDLE = 384
F32 = jnp.float32
BF16 = jnp.bfloat16
I32 = jnp.int32

NT = ((1,), (1,))
NN = ((1,), (0,))


def column_total(extent):
    indices = np.arange(extent)
    frequency = np.where(indices < extent // 2, indices, indices - extent)
    return int(np.sum(frequency[:, None] ** 2 + frequency[None, :] ** 2 <= RADIUS * RADIUS))


def packing(items, width):
    spare = LANES - width
    base = next(b for b in range(1, items + 1) if (items - b) * width <= b * spare)
    pieces = []
    row, at = 0, width
    for item in range(base, items):
        done = 0
        while done < width:
            if at == LANES:
                row, at = row + 1, width
            length = min(width - done, LANES - at)
            pieces.append((item, done, row, at, length))
            done, at = done + length, at + length
    return base, pieces


def pack_row(row, load, pieces):
    value = load(row)
    lane = lax.broadcasted_iota(I32, value.shape, 1)
    for item, source, target_row, target, length in pieces:
        if target_row == row:
            moved = pltpu.roll(load(item), (target - source) % LANES, 1)
            value = jnp.where((lane >= target) & (lane < target + length), moved, value)
    return value


def unpack_item(item, base, load, pieces):
    if item < base:
        return load(item)
    value = None
    for owner, source, row, at, length in pieces:
        if owner == item:
            moved = pltpu.roll(load(row), (source - at) % LANES, 1)
            lane = lax.broadcasted_iota(I32, moved.shape, 1)
            value = moved if value is None else jnp.where(lane >= source, moved, value)
    return value


class Sizes:
    def __init__(self, devices, extent, slots, bands_all):
        self.devices = devices
        self.extent = extent
        self.layers = extent // devices
        self.channels = 2 * self.layers
        self.slot_rows = slots // LANES
        self.slots = slots
        self.sticks = -(-column_total(extent) // devices)
        self.out_rows, self.out_pieces = packing(self.channels + 1, self.sticks)
        self.back_rows, self.back_pieces = packing(self.channels, self.sticks)
        self.rows = self.out_rows + self.layers * self.layers
        self.bands_all = bands_all
        self.band_rows = bands_all // devices
        assert extent == LANES and self.channels <= SUB


def parts_of(matrix):
    values = np.asarray(matrix, np.float32)
    high = values.astype(jnp.bfloat16)
    low = (values - high.astype(np.float32)).astype(jnp.bfloat16)
    return np.stack([high, low])


def angle(x, y, extent):
    phase = (x[:, None] * y[None, :]) % extent
    return 2.0 * math.pi * phase.astype(np.float64) / extent


def tables(sz):
    n, d, layers = sz.extent, sz.devices, sz.layers
    cells = np.arange(n)
    dev, part, lay = np.meshgrid(np.arange(d), np.arange(2), np.arange(layers), indexing="ij")
    z_rows = (dev * layers + lay).reshape(-1)
    part_rows = part.reshape(-1)
    t = angle(z_rows, cells, n)
    re, im = np.cos(t), np.sin(t)
    is_im = part_rows[:, None] == 1
    forward_z = np.concatenate([np.where(is_im, im, re), np.where(is_im, re, -im)], 1)
    freq = np.arange(2 * HALF) - HALF
    tb = angle(freq, cells, n)
    cb, sb = np.cos(tb), np.sin(tb)
    eye = np.eye(2)
    cc, ss = np.kron(eye, cb), np.kron(eye, sb)
    forward_b = np.block([[cc, ss], [-ss, cc]])
    cct, sst = cc.T, ss.T
    inverse_b = np.block([[cct, -sst], [sst, cct]])
    a_rows = (np.arange(d)[None, :] * layers + np.arange(layers)[:, None]).reshape(-1)
    lo, k = np.meshgrid(np.arange(2), np.arange(KROWS), indexing="ij")
    a_freq = (4 * (k % GROUPS) + 2 * (k // GROUPS) + lo - HALF).reshape(-1)
    ta = angle(a_rows, a_freq, n)
    ca, sa = np.cos(ta), np.sin(ta)
    forward_a = np.block([[ca, -sa], [sa, ca]])
    inverse_a = np.block([[ca.T, sa.T], [-sa.T, ca.T]])
    part2, lay2, dev2 = np.meshgrid(np.arange(2), np.arange(layers), np.arange(d), indexing="ij")
    t2 = angle((dev2 * layers + lay2).reshape(-1), cells, n)
    re2, im2 = np.cos(t2) / n**3, np.sin(t2) / n**3
    im_rows = part2.reshape(-1)[:, None] == 1
    inverse_z = np.concatenate([np.where(im_rows, im2, re2), np.where(im_rows, re2, -im2)], 1)
    return {
        "forward_z": parts_of(forward_z),
        "forward_b": parts_of(forward_b),
        "forward_a": parts_of(forward_a),
        "inverse_a": parts_of(inverse_a),
        "inverse_b": parts_of(inverse_b),
        "inverse_z": parts_of(inverse_z),
    }


def split(x):
    high = x.astype(BF16)
    return high, (x - high.astype(F32)).astype(BF16)


def dot(a, b, dims=NN):
    return lax.dot_general(a, b, (dims, ((), ())), preferred_element_type=F32)


def dot3(a, b, dims=NN):
    return dot(a[0], b[0], dims) + dot(a[0], b[1], dims) + dot(a[1], b[0], dims)


def iota(shape, dim):
    return lax.broadcasted_iota(I32, shape, dim)


def ones_where(mask):
    return jnp.where(mask, 1.0, 0.0).astype(F32)


def pick(values, lanes):
    return jnp.take_along_axis(values, lanes, axis=1, mode="promise_in_bounds")


def signed(x, extent):
    return jnp.where(x < extent // 2, x, x - extent)


def column_facts(meta, sz):
    shape = (LANES, LANES)
    col_a = jnp.broadcast_to(meta[:, 0:1], shape)
    col_b = jnp.broadcast_to(meta[:, 1:2], shape)
    row = jnp.broadcast_to(meta[:, 2:3], shape)
    lane = jnp.broadcast_to(meta[:, 3:4], shape)
    valid = jnp.broadcast_to(meta[:, 4:5], shape) > 0.5
    fa = jnp.where(col_a < sz.extent // 2, col_a, col_a - sz.extent)
    fb = jnp.where(col_b < sz.extent // 2, col_b, col_b - sz.extent)
    fc = signed(iota(shape, 1), sz.extent).astype(F32)
    inside = valid & (fc * fc <= RADIUS * RADIUS - fa * fa - fb * fb)
    return row, lane, inside


class BandLoads:
    def __init__(self, source, target, sems, first, count):
        self.refs = (source, target, sems, first)
        self.count = count // CHUNK

    def copy(self, i):
        source, target, sems, first = self.refs
        return pltpu.make_async_copy(
            source.at[:, pl.ds(first + i * CHUNK, CHUNK), :],
            target.at[:, pl.ds(i * CHUNK, CHUNK), :],
            sems.at[i],
        )

    def start(self):
        for i in range(self.count):
            self.copy(i).start()

    def wait_one(self, i):
        self.copy(i).wait()

    def wait(self):
        for i in range(self.count):
            self.copy(i).wait()


def spread_kernel(sz, cells_ref, orbitals_ref, potential_ref, table_ref,
                  send_ref, window_ref, depth_ref, slot_hot_ref, kinetic_ref, early_ref,
                  cells_in, block, pot, table, turned, rows_ref, sems, band_sems):
    loads = [
        pltpu.make_async_copy(orbitals_ref.at[:, pl.ds(0, SUB), :], block, sems.at[0]),
        pltpu.make_async_copy(table_ref, table, sems.at[1]),
        pltpu.make_async_copy(potential_ref, pot, sems.at[2]),
    ]
    cell_load = pltpu.make_async_copy(cells_ref, cells_in, sems.at[3])
    cell_load.start()
    for load in loads:
        load.start()
    bands = BandLoads(orbitals_ref, early_ref, band_sems, 0, EARLY)
    bands.start()
    cell_load.wait()
    rows = sz.slot_rows
    shape = (rows, LANES)
    cells = cells_in[...]
    live = cells >= 0
    column = lax.shift_right_arithmetic(cells, int(math.log2(sz.extent)))
    rolled = pltpu.roll(column, 1, 1)
    above = pltpu.roll(rolled, 1, 0)
    lane = iota(shape, 1)
    row = iota(shape, 0)
    before = jnp.where(lane == 0, jnp.where(row == 0, -1, above), rolled)
    starts = live & (column != before)
    flags = ones_where(starts).astype(BF16)
    square = (LANES, LANES)
    upto = ones_where(iota(square, 0) <= iota(square, 1)).astype(BF16)
    all_ones = jnp.ones(square, BF16)
    within = dot(flags, upto)
    totals = dot(flags, all_ones)
    lower = ones_where(iota((rows, rows), 1) < iota((rows, rows), 0)).astype(BF16)
    rank = (within + dot(lower, totals.astype(BF16))).astype(I32) - 1
    rank = jnp.where(starts, rank, -1)
    col_a = lax.shift_right_arithmetic(column, int(math.log2(sz.extent)))
    col_b = column & (sz.extent - 1)
    sub = iota((SUB, LANES), 0)
    lane8 = iota((SUB, LANES), 1)
    place = iota(square, 0)
    hots, facts = [], []
    for r in range(rows):
        hots.append(ones_where(place == rank[r : r + 1, :]).astype(BF16))
        fact = jnp.where(sub == 0, col_a[r : r + 1, :], col_b[r : r + 1, :])
        fact = jnp.where(sub == 2, r, fact)
        fact = jnp.where(sub == 3, lane8, fact)
        fact = jnp.where(sub == 4, 1, fact)
        facts.append(fact.astype(F32).astype(BF16))
    meta_t = dot(jnp.concatenate(facts, 1), jnp.concatenate(hots, 1), NT)
    meta = jnp.transpose(jnp.concatenate([meta_t, jnp.zeros((LANES - SUB, LANES), F32)], 0))
    first_row, first_lane, inside = column_facts(meta, sz)
    hot = ones_where(inside).astype(BF16)
    before_in = ones_where(iota(square, 0) < iota(square, 1)).astype(BF16)
    slot = (first_lane + dot(hot, before_in)).astype(I32)
    second = slot >= LANES
    slot_lane = slot & (LANES - 1)

    loads[0].wait()
    for r in range(rows):
        window_ref[r : r + 1, :] = block[0, 0:1, r * LANES : (r + 1) * LANES]
        window_ref[rows + r : rows + r + 1, :] = block[1, 0:1, r * LANES : (r + 1) * LANES]
    window = jnp.concatenate([window_ref[0:rows, :], window_ref[rows : 2 * rows, :]], 1)
    high, low = split(window)
    row_of = first_row.astype(I32)[:, 0:rows]
    which = iota((LANES, rows), 1)
    near = ones_where(which == row_of).astype(BF16)
    far = ones_where(which == row_of + 1).astype(BF16)
    near_w = dot(near, high) + dot(near, low)
    far_w = dot(far, high) + dot(far, low)
    sticks = []
    for part in range(2):
        cut = slice(part * LANES, (part + 1) * LANES)
        value = jnp.where(second, pick(far_w[:, cut], slot_lane), pick(near_w[:, cut], slot_lane))
        sticks.append(jnp.where(inside, value, 0.0))
    sticks = jnp.concatenate(sticks, 1)
    loads[1].wait()
    depth = dot3((table[0], table[1]), split(sticks), NT)

    channels, layers, devices = sz.channels, sz.layers, sz.devices
    ids = jnp.where(
        meta_t[4:5, :] > 0.5, meta_t[0:1, :] * sz.extent + meta_t[1:2, :], -1.0
    )
    ids = jnp.broadcast_to(ids, (devices, LANES))
    rows_ref[...] = depth

    def item(i):
        return ids if i == channels else rows_ref[pl.ds(i, devices, stride=channels), :]

    for r in range(sz.out_rows):
        send_ref[pl.ds(r, devices, stride=sz.rows), :] = pack_row(r, item, sz.out_pieces)
    loads[2].wait()
    for al in range(layers):
        turned[...] = jnp.transpose(pot[al])
        for p in range(layers):
            at = sz.out_rows + al * layers + p
            send_ref[pl.ds(at, devices, stride=sz.rows), :] = turned[
                pl.ds(p, devices, stride=layers), :
            ]
    length = dot(hot, all_ones).astype(I32)
    shift = iota(square, 1) - first_lane.astype(I32)
    top = lax.shift_right_arithmetic(length - 1, 1)
    for turn in range(2):
        p = shift + turn * LANES
        held = (p >= 0) & (p < length)
        depth_of = jnp.where(p <= top, p, p + sz.extent - length) & (sz.extent - 1)
        depth_ref[turn] = jnp.where(held, depth_of, -1)
    row_t = jnp.broadcast_to(meta_t[2:3, :].astype(I32), shape)
    slot_hot_ref[...] = jnp.concatenate(
        [ones_where(row == row_t), ones_where(row == row_t + 1)], 1
    ).astype(BF16)
    fa = signed(col_a & (sz.extent - 1), sz.extent)
    fb = signed(col_b, sz.extent)
    fc = signed(cells & (sz.extent - 1), sz.extent)
    kinetic = (fa * fa + fb * fb + fc * fc).astype(F32) / (RADIUS * RADIUS)
    kinetic_ref[...] = jnp.where(live, kinetic, -1.0)
    bands.wait()


def plane_kernel(sz, recv_ref, fb_ref, fa_ref, ia_ref, ib_ref, orbitals_ref,
                 out_ref, middle_ref,
                 fb, fa, ia, ib, hot_ref, planes, back, group_ref, z_ref, sems, band_sems):
    bands = BandLoads(orbitals_ref, middle_ref, band_sems, EARLY, MIDDLE)
    bands.start()
    copies = [
        pltpu.make_async_copy(src, dst, sems.at[i])
        for i, (src, dst) in enumerate([(fb_ref, fb), (fa_ref, fa), (ia_ref, ia), (ib_ref, ib)])
    ]
    for c in copies:
        c.start()
    devices, layers, channels = sz.devices, sz.layers, sz.channels

    def recv_row(r):
        return recv_ref[pl.ds(r, devices, stride=sz.rows), :]

    def recv_item(i):
        return unpack_item(i, sz.out_rows, recv_row, sz.out_pieces)

    lane = iota((devices, LANES), 1)
    ids = jnp.where(lane < sz.sticks, recv_item(channels), -1.0).astype(I32)
    if channels < SUB:
        z_ref[...] = jnp.zeros(z_ref.shape, F32)
    for i in range(channels):
        z_ref[pl.ds(i, devices, stride=SUB), :] = recv_item(i)
    col_a = lax.shift_right_arithmetic(ids, int(math.log2(sz.extent)))
    col_b = ids & (sz.extent - 1)
    sa = (col_a + HALF) & (sz.extent - 1)
    sb = (col_b + HALF) & (sz.extent - 1)
    group = jnp.where(ids >= 0, lax.shift_right_arithmetic(sa, 2), -1)
    cell = (sa & 3) * (2 * HALF) + sb
    group_ref[...] = group
    two = (2 * SUB, LANES)
    cell_rows = [(iota(two, 0) + i).astype(F32).astype(BF16) for i in range(0, CELLS, 2 * SUB)]
    group_rows = [
        (lax.shift_right_logical(iota(two, 0), 3) + g).astype(F32).astype(BF16)
        for g in range(0, GROUPS, 2)
    ]
    one, zero = jnp.ones(two, BF16), jnp.zeros(two, BF16)
    cell, group_f = cell.astype(F32), group.astype(F32)
    left_high, left_low = [], []
    for e in range(devices):
        own_cell = jnp.broadcast_to(cell[e : e + 1, :], two).astype(BF16)
        own_group = jnp.broadcast_to(group_f[e : e + 1, :], two).astype(BF16)
        values = z_ref[e * SUB : (e + 1) * SUB, :]
        high, low = split(jnp.concatenate([values, values], 0))
        here = [own_group == g for g in group_rows]
        left_high.append(jnp.concatenate([jnp.where(h, high, zero) for h in here], 0))
        left_low.append(jnp.concatenate([jnp.where(h, low, zero) for h in here], 0))
        for i, rows in enumerate(cell_rows):
            hot_ref[2 * SUB * i : 2 * SUB * (i + 1), e * LANES : (e + 1) * LANES] = jnp.where(
                own_cell == rows, one, zero
            )
    left = jnp.concatenate(
        [jnp.concatenate(left_high, 1), jnp.concatenate(left_low, 1)], 0
    )
    spread = dot(left, hot_ref[...], NT)
    size = GROUPS * SUB
    spread = spread[:size] + spread[size:]
    for half in range(2):
        planes[half * size : (half + 1) * size, :] = spread[:, half * LANES : (half + 1) * LANES]

    def plane_part(part, p):
        return planes[pl.ds(part * layers + p, KROWS, stride=SUB), :]

    grid = jnp.concatenate(
        [
            jnp.concatenate([plane_part(part, p) for p in range(layers)], 0)
            for part in range(2)
        ],
        1,
    )
    copies[0].wait()
    grid = dot3(split(grid), (fb[0], fb[1]))
    grid = jnp.concatenate(
        [
            jnp.concatenate(
                [
                    grid[p * KROWS : (p + 1) * KROWS, q * LANES : (q + 1) * LANES]
                    for q in range(4)
                ],
                0,
            )
            for p in range(layers)
        ],
        1,
    )
    copies[1].wait()
    grid = dot3((fa[0], fa[1]), split(grid))
    potential = jnp.concatenate(
        [
            jnp.concatenate(
                [
                    recv_row(sz.out_rows + al * layers + p)
                    for al in range(layers)
                ],
                0,
            )
            for p in range(layers)
        ],
        1,
    )
    half = sz.extent
    field = jnp.concatenate([grid[0:half] * potential, grid[half:] * potential], 0)
    copies[2].wait()
    grid = dot3((ia[0], ia[1]), split(field))
    grid = jnp.concatenate(
        [
            jnp.concatenate(
                [
                    grid[q * KROWS : (q + 1) * KROWS, p * LANES : (p + 1) * LANES]
                    for q in range(4)
                ],
                1,
            )
            for p in range(layers)
        ],
        0,
    )
    copies[3].wait()
    grid = dot3(split(grid), (ib[0], ib[1]))
    for part in range(2):
        for p in range(layers):
            back[pl.ds(part * layers + p, KROWS, stride=SUB), :] = grid[
                p * KROWS : (p + 1) * KROWS, part * LANES : (part + 1) * LANES
            ]

    values = jnp.concatenate([back[:size, :], back[size:, :]], 1)
    values = jnp.concatenate(split(values), 0)
    for pair in range(0, devices, 2):
        both = dot(values, hot_ref[:, pair * LANES : (pair + 2) * LANES])
        both = both[:size] + both[size:]
        for e in (pair, pair + 1):
            found = both[:, (e - pair) * LANES : (e - pair + 1) * LANES]
            own = jnp.broadcast_to(group_ref[e : e + 1, :], (SUB, LANES))
            total = jnp.zeros((SUB, LANES), F32)
            for g in range(GROUPS):
                total = total + jnp.where(own == g, found[g * SUB : (g + 1) * SUB, :], 0.0)
            z_ref[e * SUB : (e + 1) * SUB, :] = total

    def back_item(i):
        return z_ref[pl.ds(i, devices, stride=SUB), :]

    for r in range(sz.back_rows):
        out_ref[pl.ds(r, devices, stride=sz.back_rows), :] = pack_row(
            r, back_item, sz.back_pieces
        )
    bands.wait()


def final_kernel(sz, back_ref, window_ref, table_ref, depth_ref, hot_ref, kinetic_ref,
                 early_ref, middle_ref,
                 orbitals_ref,
                 applied_out, tile_ref,
                 applied_ref, factors, late_ref, acc, sums_ref, band_sems, out_sem):
    done = EARLY + MIDDLE
    bands = BandLoads(orbitals_ref, late_ref, band_sems, done, sz.bands_all - done)
    bands.start()
    devices, layers, rows = sz.devices, sz.layers, sz.slot_rows
    square = (LANES, LANES)

    def back_row(r):
        return back_ref[pl.ds(r, devices, stride=sz.back_rows), :]

    values = jnp.concatenate(
        [
            unpack_item(i, sz.back_rows, back_row, sz.back_pieces)
            for i in range(sz.channels)
        ],
        0,
    )
    values = jnp.transpose(values)
    sticks = dot3(split(values), (table_ref[0], table_ref[1]))
    placed = []
    for turn in range(2):
        depth = depth_ref[turn]
        held = depth >= 0
        depth = depth & (sz.extent - 1)
        placed.append(
            jnp.concatenate(
                [
                    jnp.where(held, pick(sticks[:, q * LANES : (q + 1) * LANES], depth), 0.0)
                    for q in range(2)
                ],
                1,
            )
        )
    placed = split(jnp.concatenate(placed, 0))
    hot = hot_ref[...]
    local = dot(hot, placed[0]) + dot(hot, placed[1])
    kinetic = kinetic_ref[...]
    for part in range(2):
        own = window_ref[part * rows : (part + 1) * rows, :]
        full = kinetic * own + local[:, part * LANES : (part + 1) * LANES]
        applied_ref[part * rows : (part + 1) * rows, :] = jnp.where(kinetic >= 0.0, full, 0.0)
    store = pltpu.make_async_copy(applied_ref, applied_out, out_sem)
    store.start()
    a_re = applied_ref[0:rows, :]
    a_im = applied_ref[rows : 2 * rows, :]
    factors[0] = a_im
    factors[1] = a_re - a_im
    factors[2] = a_re + a_im

    blocks = sz.bands_all // LANES
    block_row = iota((blocks, LANES), 0)
    sums_ref[...] = jnp.zeros(sums_ref.shape, F32)

    def product_of(source, first, wait=None):
        def product(i, carry):
            if wait is not None:
                wait(i)
            start = pl.multiple_of(i * CHUNK, CHUNK)
            sums = [jnp.zeros((CHUNK, LANES), F32) for _ in range(3)]
            for r in range(rows):
                x = source[0, pl.ds(start, CHUNK), r * LANES : (r + 1) * LANES]
                y = source[1, pl.ds(start, CHUNK), r * LANES : (r + 1) * LANES]
                for q, value in enumerate((x + y, x, y)):
                    sums[q] = sums[q] + value * factors[q, r : r + 1, :]
            end = first + (i + 1) * CHUNK
            at = pl.multiple_of((end - CHUNK) % LANES, CHUNK)
            acc[0, pl.ds(at, CHUNK), :] = sums[0] + sums[1]
            acc[1, pl.ds(at, CHUNK), :] = sums[0] - sums[2]

            @pl.when(end % LANES == 0)
            def _():
                hot_row = ones_where(block_row == end // LANES - 1).astype(BF16)
                for part in range(2):
                    high, low = split(acc[part])
                    sums_ref[part] += dot(hot_row, high, NT) + dot(hot_row, low, NT)

            return carry

        lax.fori_loop(0, source.shape[1] // CHUNK, product, 0)

    product_of(early_ref, 0)
    product_of(middle_ref, EARLY)
    product_of(late_ref, done, bands.wait_one)
    sums = [sums_ref[part] * (1.0 / (sz.slots * sz.devices)) for part in range(2)]
    width = sz.band_rows
    per_row = LANES // width
    lane = iota((blocks, LANES), 1)
    for q in range(per_row):
        real = pltpu.roll(sums[0], (-q * width) % LANES, 1)
        imag = pltpu.roll(sums[1], (width - q * width) % LANES, 1)
        tile_ref[pl.ds(q, blocks, stride=per_row), :] = jnp.where(lane < width, real, imag)
    store.wait()


def sum_kernel(sz, tile_ref, out_ref):
    width = sz.band_rows
    total = jnp.sum(tile_ref[...], axis=0, keepdims=True)
    for part in range(2):
        out_ref[part, :, :] = total[:, part * width : (part + 1) * width]


def full_spec():
    return pl.BlockSpec(memory_space=pltpu.VMEM)


def any_spec():
    return pl.BlockSpec(memory_space=pl.ANY)


def vmem(mib):
    return pltpu.CompilerParams(vmem_limit_bytes=mib << 20)


def run_spread(sz, cells, orbitals, potential, table, **kw):
    return pl.pallas_call(
        lambda *refs: spread_kernel(sz, *refs),
        out_shape=(
            jax.ShapeDtypeStruct((sz.devices * sz.rows, LANES), F32),
            jax.ShapeDtypeStruct((2 * sz.slot_rows, LANES), F32),
            jax.ShapeDtypeStruct((2, LANES, LANES), I32),
            jax.ShapeDtypeStruct((sz.slot_rows, 2 * LANES), BF16),
            jax.ShapeDtypeStruct((sz.slot_rows, LANES), F32),
            pltpu.VMEM((2, EARLY, sz.slots), F32),
        ),
        in_specs=[any_spec()] * 4,
        out_specs=(full_spec(),) * 6,
        scratch_shapes=[
            pltpu.VMEM((sz.slot_rows, LANES), I32),
            pltpu.VMEM((2, SUB, sz.slots), F32),
            pltpu.VMEM((sz.layers, LANES, LANES), F32),
            pltpu.VMEM(table.shape, BF16),
            pltpu.VMEM((LANES, LANES), F32),
            pltpu.VMEM((sz.devices * sz.channels, LANES), F32),
            pltpu.SemaphoreType.DMA((4,)),
            pltpu.SemaphoreType.DMA((EARLY // CHUNK,)),
        ],
        name="spread",
        compiler_params=vmem(8),
        **kw,
    )(cells, orbitals, potential, table)


def run_planes(sz, recv, tabs, orbitals, **kw):
    mats = [tabs[n] for n in ("forward_b", "forward_a", "inverse_a", "inverse_b")]
    return pl.pallas_call(
        lambda *refs: plane_kernel(sz, *refs),
        out_shape=(
            jax.ShapeDtypeStruct((sz.devices * sz.back_rows, LANES), F32),
            pltpu.VMEM((2, MIDDLE, sz.slots), F32),
        ),
        in_specs=[full_spec()] + [any_spec()] * 5,
        out_specs=(full_spec(), full_spec()),
        scratch_shapes=[pltpu.VMEM(m.shape, BF16) for m in mats]
        + [
            pltpu.VMEM((CELLS, sz.devices * LANES), BF16),
            pltpu.VMEM((KROWS * SUB, LANES), F32),
            pltpu.VMEM((KROWS * SUB, LANES), F32),
            pltpu.VMEM((sz.devices, LANES), I32),
            pltpu.VMEM((sz.devices * SUB, LANES), F32),
            pltpu.SemaphoreType.DMA((4,)),
            pltpu.SemaphoreType.DMA((MIDDLE // CHUNK,)),
        ],
        name="planes",
        compiler_params=vmem(16),
        **kw,
    )(recv, *mats, orbitals)


def run_final(sz, back, window, table, depth, hot, kinetic, early, middle, orbitals, **kw):
    late = sz.bands_all - EARLY - MIDDLE
    return pl.pallas_call(
        lambda *refs: final_kernel(sz, *refs),
        out_shape=(
            jax.ShapeDtypeStruct((2 * sz.slot_rows, LANES), F32),
            jax.ShapeDtypeStruct((sz.devices, LANES), F32),
        ),
        in_specs=[full_spec()] * 8 + [any_spec()],
        out_specs=(any_spec(), full_spec()),
        scratch_shapes=[
            pltpu.VMEM((2 * sz.slot_rows, LANES), F32),
            pltpu.VMEM((3, sz.slot_rows, LANES), F32),
            pltpu.VMEM((2, late, sz.slots), F32),
            pltpu.VMEM((2, LANES, LANES), F32),
            pltpu.VMEM((2, sz.bands_all // LANES, LANES), F32),
            pltpu.SemaphoreType.DMA((late // CHUNK,)),
            pltpu.SemaphoreType.DMA,
        ],
        name="final",
        compiler_params=vmem(20),
        **kw,
    )(back, window, table, depth, hot, kinetic, early, middle, orbitals)


def run_sum(sz, tile, **kw):
    return pl.pallas_call(
        lambda *refs: sum_kernel(sz, *refs),
        out_shape=jax.ShapeDtypeStruct((2, 1, sz.band_rows), F32),
        in_specs=[full_spec()],
        out_specs=full_spec(),
        name="add",
        compiler_params=vmem(2),
        **kw,
    )(tile)


def exchange(x):
    rows = x.reshape(x.shape[0], 1, x.shape[1])
    return lax.all_to_all(rows, "ga", split_axis=0, concat_axis=0, tiled=True).reshape(x.shape)


def local(orbitals, coeff_cells, potential):
    devices = lax.axis_size("ga")
    sz = Sizes(devices, potential.shape[1], coeff_cells.shape[0], orbitals.shape[1])
    tabs = {name: jnp.asarray(value) for name, value in tables(sz).items()}
    cells = coeff_cells.reshape(sz.slot_rows, LANES)
    stay = lambda x: pltpu.with_memory_space_constraint(x, pltpu.HBM)
    orbitals = stay(orbitals)
    send, window, depth, hot, kinetic, early = run_spread(
        sz, stay(cells), orbitals, stay(potential), stay(tabs["forward_z"])
    )
    back, middle = run_planes(sz, exchange(send), tabs, orbitals)
    applied, tile = run_final(
        sz, exchange(back), window, tabs["inverse_z"], depth, hot, kinetic, early, middle, orbitals
    )
    subspace = run_sum(sz, exchange(tile))
    return (
        applied.reshape(2, 1, sz.slots),
        jnp.transpose(subspace, (2, 0, 1)),
    )


def solution(mesh):
    in_specs = (P(None, "kpt", "ga"), P("ga"), P("ga", None, None))
    out_specs = (P(None, "kpt", "ga"), P("ga", None, "kpt"))
    return jax.shard_map(local, mesh=mesh, in_specs=in_specs, out_specs=out_specs, check_vma=False)
```

```python
import math

import jax
import jax.numpy as jnp
import numpy as np
from jax import lax
from jax.experimental import pallas as pl
from jax.experimental.pallas import tpu as pltpu
from jax.sharding import PartitionSpec as P

RADIUS = 30
LANES = 128
SUB = 8
HALF = 32
KROWS = 32
CELLS = 4 * 2 * HALF
GROUPS = KROWS // 2
CHUNK = 64
EARLY = 192
MIDDLE = 320
F32 = jnp.float32
BF16 = jnp.bfloat16
I32 = jnp.int32

NT = ((1,), (1,))
NN = ((1,), (0,))


def column_total(extent):
    indices = np.arange(extent)
    frequency = np.where(indices < extent // 2, indices, indices - extent)
    return int(np.sum(frequency[:, None] ** 2 + frequency[None, :] ** 2 <= RADIUS * RADIUS))


def packing(items, width):
    spare = LANES - width
    base = next(b for b in range(1, items + 1) if (items - b) * width <= b * spare)
    pieces = []
    row, at = 0, width
    for item in range(base, items):
        done = 0
        while done < width:
            if at == LANES:
                row, at = row + 1, width
            length = min(width - done, LANES - at)
            pieces.append((item, done, row, at, length))
            done, at = done + length, at + length
    return base, pieces


def pack_row(row, load, pieces):
    value = load(row)
    lane = lax.broadcasted_iota(I32, value.shape, 1)
    for item, source, target_row, target, length in pieces:
        if target_row == row:
            moved = pltpu.roll(load(item), (target - source) % LANES, 1)
            value = jnp.where((lane >= target) & (lane < target + length), moved, value)
    return value


def unpack_item(item, base, load, pieces):
    if item < base:
        return load(item)
    value = None
    for owner, source, row, at, length in pieces:
        if owner == item:
            moved = pltpu.roll(load(row), (source - at) % LANES, 1)
            lane = lax.broadcasted_iota(I32, moved.shape, 1)
            value = moved if value is None else jnp.where(lane >= source, moved, value)
    return value


class Sizes:
    def __init__(self, devices, extent, slots, bands_all):
        self.devices = devices
        self.extent = extent
        self.layers = extent // devices
        self.channels = 2 * self.layers
        self.slot_rows = slots // LANES
        self.slots = slots
        self.sticks = -(-column_total(extent) // devices)
        self.out_rows, self.out_pieces = packing(self.channels + 1, self.sticks)
        self.back_rows, self.back_pieces = packing(self.channels, self.sticks)
        self.rows = self.out_rows + self.layers * self.layers
        self.bands_all = bands_all
        self.band_rows = bands_all // devices
        assert extent == LANES and self.channels <= SUB


def parts_of(matrix):
    values = np.asarray(matrix, np.float32)
    high = values.astype(jnp.bfloat16)
    low = (values - high.astype(np.float32)).astype(jnp.bfloat16)
    return np.stack([high, low])


def angle(x, y, extent):
    phase = (x[:, None] * y[None, :]) % extent
    return 2.0 * math.pi * phase.astype(np.float64) / extent


def tables(sz):
    n, d, layers = sz.extent, sz.devices, sz.layers
    cells = np.arange(n)
    dev, part, lay = np.meshgrid(np.arange(d), np.arange(2), np.arange(layers), indexing="ij")
    z_rows = (dev * layers + lay).reshape(-1)
    part_rows = part.reshape(-1)
    t = angle(z_rows, cells, n)
    re, im = np.cos(t), np.sin(t)
    is_im = part_rows[:, None] == 1
    forward_z = np.concatenate([np.where(is_im, im, re), np.where(is_im, re, -im)], 1)
    freq = np.arange(2 * HALF) - HALF
    tb = angle(freq, cells, n)
    cb, sb = np.cos(tb), np.sin(tb)
    eye = np.eye(2)
    cc, ss = np.kron(eye, cb), np.kron(eye, sb)
    forward_b = np.block([[cc, ss], [-ss, cc]])
    cct, sst = cc.T, ss.T
    inverse_b = np.block([[cct, -sst], [sst, cct]])
    a_rows = (np.arange(d)[None, :] * layers + np.arange(layers)[:, None]).reshape(-1)
    lo, k = np.meshgrid(np.arange(2), np.arange(KROWS), indexing="ij")
    a_freq = (4 * (k % GROUPS) + 2 * (k // GROUPS) + lo - HALF).reshape(-1)
    ta = angle(a_rows, a_freq, n)
    ca, sa = np.cos(ta), np.sin(ta)
    forward_a = np.block([[ca, -sa], [sa, ca]])
    inverse_a = np.block([[ca.T, sa.T], [-sa.T, ca.T]])
    part2, lay2, dev2 = np.meshgrid(np.arange(2), np.arange(layers), np.arange(d), indexing="ij")
    t2 = angle((dev2 * layers + lay2).reshape(-1), cells, n)
    re2, im2 = np.cos(t2) / n**3, np.sin(t2) / n**3
    im_rows = part2.reshape(-1)[:, None] == 1
    inverse_z = np.concatenate([np.where(im_rows, im2, re2), np.where(im_rows, re2, -im2)], 1)
    return {
        "forward_z": parts_of(forward_z),
        "forward_b": parts_of(forward_b),
        "forward_a": parts_of(forward_a),
        "inverse_a": parts_of(inverse_a),
        "inverse_b": parts_of(inverse_b),
        "inverse_z": parts_of(inverse_z),
    }


def split(x):
    high = x.astype(BF16)
    return high, (x - high.astype(F32)).astype(BF16)


def dot(a, b, dims=NN):
    return lax.dot_general(a, b, (dims, ((), ())), preferred_element_type=F32)


def dot3(a, b, dims=NN):
    return dot(a[0], b[0], dims) + dot(a[0], b[1], dims) + dot(a[1], b[0], dims)


def iota(shape, dim):
    return lax.broadcasted_iota(I32, shape, dim)


def ones_where(mask):
    return jnp.where(mask, 1.0, 0.0).astype(F32)


def pick(values, lanes):
    return jnp.take_along_axis(values, lanes, axis=1, mode="promise_in_bounds")


def signed(x, extent):
    return jnp.where(x < extent // 2, x, x - extent)


def column_facts(meta, sz):
    shape = (LANES, LANES)
    col_a = jnp.broadcast_to(meta[:, 0:1], shape)
    col_b = jnp.broadcast_to(meta[:, 1:2], shape)
    row = jnp.broadcast_to(meta[:, 2:3], shape)
    lane = jnp.broadcast_to(meta[:, 3:4], shape)
    valid = jnp.broadcast_to(meta[:, 4:5], shape) > 0.5
    fa = jnp.where(col_a < sz.extent // 2, col_a, col_a - sz.extent)
    fb = jnp.where(col_b < sz.extent // 2, col_b, col_b - sz.extent)
    fc = signed(iota(shape, 1), sz.extent).astype(F32)
    inside = valid & (fc * fc <= RADIUS * RADIUS - fa * fa - fb * fb)
    return row, lane, inside


class BandLoads:
    def __init__(self, source, target, sems, first, count):
        self.refs = (source, target, sems, first)
        self.count = count // CHUNK

    def copy(self, i):
        source, target, sems, first = self.refs
        return pltpu.make_async_copy(
            source.at[:, pl.ds(first + i * CHUNK, CHUNK), :],
            target.at[:, pl.ds(i * CHUNK, CHUNK), :],
            sems.at[i],
        )

    def start(self):
        for i in range(self.count):
            self.copy(i).start()

    def wait_one(self, i):
        self.copy(i).wait()

    def wait(self):
        for i in range(self.count):
            self.copy(i).wait()


def spread_kernel(sz, cells_ref, orbitals_ref, potential_ref, table_ref,
                  send_ref, window_ref, depth_ref, slot_hot_ref, kinetic_ref, early_ref,
                  cells_in, block, pot, table, turned, rows_ref, sems, band_sems):
    loads = [
        pltpu.make_async_copy(orbitals_ref.at[:, pl.ds(0, SUB), :], block, sems.at[0]),
        pltpu.make_async_copy(table_ref, table, sems.at[1]),
        pltpu.make_async_copy(potential_ref, pot, sems.at[2]),
    ]
    cell_load = pltpu.make_async_copy(cells_ref, cells_in, sems.at[3])
    cell_load.start()
    for load in loads:
        load.start()
    bands = BandLoads(orbitals_ref, early_ref, band_sems, 0, EARLY)
    bands.start()
    cell_load.wait()
    rows = sz.slot_rows
    shape = (rows, LANES)
    cells = cells_in[...]
    live = cells >= 0
    column = lax.shift_right_arithmetic(cells, int(math.log2(sz.extent)))
    rolled = pltpu.roll(column, 1, 1)
    above = pltpu.roll(rolled, 1, 0)
    lane = iota(shape, 1)
    row = iota(shape, 0)
    before = jnp.where(lane == 0, jnp.where(row == 0, -1, above), rolled)
    starts = live & (column != before)
    flags = ones_where(starts).astype(BF16)
    square = (LANES, LANES)
    upto = ones_where(iota(square, 0) <= iota(square, 1)).astype(BF16)
    all_ones = jnp.ones(square, BF16)
    within = dot(flags, upto)
    totals = dot(flags, all_ones)
    lower = ones_where(iota((rows, rows), 1) < iota((rows, rows), 0)).astype(BF16)
    rank = (within + dot(lower, totals.astype(BF16))).astype(I32) - 1
    rank = jnp.where(starts, rank, -1)
    col_a = lax.shift_right_arithmetic(column, int(math.log2(sz.extent)))
    col_b = column & (sz.extent - 1)
    sub = iota((SUB, LANES), 0)
    lane8 = iota((SUB, LANES), 1)
    place = iota(square, 0)
    hots, facts = [], []
    for r in range(rows):
        hots.append(ones_where(place == rank[r : r + 1, :]).astype(BF16))
        fact = jnp.where(sub == 0, col_a[r : r + 1, :], col_b[r : r + 1, :])
        fact = jnp.where(sub == 2, r, fact)
        fact = jnp.where(sub == 3, lane8, fact)
        fact = jnp.where(sub == 4, 1, fact)
        facts.append(fact.astype(F32).astype(BF16))
    meta_t = dot(jnp.concatenate(facts, 1), jnp.concatenate(hots, 1), NT)
    meta = jnp.transpose(jnp.concatenate([meta_t, jnp.zeros((LANES - SUB, LANES), F32)], 0))
    first_row, first_lane, inside = column_facts(meta, sz)
    hot = ones_where(inside).astype(BF16)
    before_in = ones_where(iota(square, 0) < iota(square, 1)).astype(BF16)
    slot = (first_lane + dot(hot, before_in)).astype(I32)
    second = slot >= LANES
    slot_lane = slot & (LANES - 1)

    loads[0].wait()
    for r in range(rows):
        window_ref[r : r + 1, :] = block[0, 0:1, r * LANES : (r + 1) * LANES]
        window_ref[rows + r : rows + r + 1, :] = block[1, 0:1, r * LANES : (r + 1) * LANES]
    window = jnp.concatenate([window_ref[0:rows, :], window_ref[rows : 2 * rows, :]], 1)
    high, low = split(window)
    row_of = first_row.astype(I32)[:, 0:rows]
    which = iota((LANES, rows), 1)
    near = ones_where(which == row_of).astype(BF16)
    far = ones_where(which == row_of + 1).astype(BF16)
    near_w = dot(near, high) + dot(near, low)
    far_w = dot(far, high) + dot(far, low)
    sticks = []
    for part in range(2):
        cut = slice(part * LANES, (part + 1) * LANES)
        value = jnp.where(second, pick(far_w[:, cut], slot_lane), pick(near_w[:, cut], slot_lane))
        sticks.append(jnp.where(inside, value, 0.0))
    sticks = jnp.concatenate(sticks, 1)
    loads[1].wait()
    depth = dot3((table[0], table[1]), split(sticks), NT)

    channels, layers, devices = sz.channels, sz.layers, sz.devices
    ids = jnp.where(
        meta_t[4:5, :] > 0.5, meta_t[0:1, :] * sz.extent + meta_t[1:2, :], -1.0
    )
    ids = jnp.broadcast_to(ids, (devices, LANES))
    rows_ref[...] = depth

    def item(i):
        return ids if i == channels else rows_ref[pl.ds(i, devices, stride=channels), :]

    for r in range(sz.out_rows):
        send_ref[pl.ds(r, devices, stride=sz.rows), :] = pack_row(r, item, sz.out_pieces)
    loads[2].wait()
    for al in range(layers):
        turned[...] = jnp.transpose(pot[al])
        for p in range(layers):
            at = sz.out_rows + al * layers + p
            send_ref[pl.ds(at, devices, stride=sz.rows), :] = turned[
                pl.ds(p, devices, stride=layers), :
            ]
    length = dot(hot, all_ones).astype(I32)
    shift = iota(square, 1) - first_lane.astype(I32)
    top = lax.shift_right_arithmetic(length - 1, 1)
    for turn in range(2):
        p = shift + turn * LANES
        held = (p >= 0) & (p < length)
        depth_of = jnp.where(p <= top, p, p + sz.extent - length) & (sz.extent - 1)
        depth_ref[turn] = jnp.where(held, depth_of, -1)
    row_t = jnp.broadcast_to(meta_t[2:3, :].astype(I32), shape)
    slot_hot_ref[...] = jnp.concatenate(
        [ones_where(row == row_t), ones_where(row == row_t + 1)], 1
    ).astype(BF16)
    fa = signed(col_a & (sz.extent - 1), sz.extent)
    fb = signed(col_b, sz.extent)
    fc = signed(cells & (sz.extent - 1), sz.extent)
    kinetic = (fa * fa + fb * fb + fc * fc).astype(F32) / (RADIUS * RADIUS)
    kinetic_ref[...] = jnp.where(live, kinetic, -1.0)
    bands.wait()


def plane_kernel(sz, recv_ref, fb_ref, fa_ref, ia_ref, ib_ref, orbitals_ref,
                 out_ref, middle_ref,
                 fb, fa, ia, ib, hot_ref, planes, back, group_ref, z_ref, sems, band_sems):
    bands = BandLoads(orbitals_ref, middle_ref, band_sems, EARLY, MIDDLE)
    bands.start()
    copies = [
        pltpu.make_async_copy(src, dst, sems.at[i])
        for i, (src, dst) in enumerate([(fb_ref, fb), (fa_ref, fa), (ia_ref, ia), (ib_ref, ib)])
    ]
    for c in copies:
        c.start()
    devices, layers, channels = sz.devices, sz.layers, sz.channels

    def recv_row(r):
        return recv_ref[pl.ds(r, devices, stride=sz.rows), :]

    def recv_item(i):
        return unpack_item(i, sz.out_rows, recv_row, sz.out_pieces)

    lane = iota((devices, LANES), 1)
    ids = jnp.where(lane < sz.sticks, recv_item(channels), -1.0).astype(I32)
    if channels < SUB:
        z_ref[...] = jnp.zeros(z_ref.shape, F32)
    for i in range(channels):
        z_ref[pl.ds(i, devices, stride=SUB), :] = recv_item(i)
    col_a = lax.shift_right_arithmetic(ids, int(math.log2(sz.extent)))
    col_b = ids & (sz.extent - 1)
    sa = (col_a + HALF) & (sz.extent - 1)
    sb = (col_b + HALF) & (sz.extent - 1)
    group = jnp.where(ids >= 0, lax.shift_right_arithmetic(sa, 2), -1)
    cell = (sa & 3) * (2 * HALF) + sb
    group_ref[...] = group
    two = (2 * SUB, LANES)
    cell_rows = [(iota(two, 0) + i).astype(F32).astype(BF16) for i in range(0, CELLS, 2 * SUB)]
    group_rows = [
        (lax.shift_right_logical(iota(two, 0), 3) + g).astype(F32).astype(BF16)
        for g in range(0, GROUPS, 2)
    ]
    one, zero = jnp.ones(two, BF16), jnp.zeros(two, BF16)
    cell, group_f = cell.astype(F32), group.astype(F32)
    left_high, left_low = [], []
    for e in range(devices):
        own_cell = jnp.broadcast_to(cell[e : e + 1, :], two).astype(BF16)
        own_group = jnp.broadcast_to(group_f[e : e + 1, :], two).astype(BF16)
        values = z_ref[e * SUB : (e + 1) * SUB, :]
        high, low = split(jnp.concatenate([values, values], 0))
        here = [own_group == g for g in group_rows]
        left_high.append(jnp.concatenate([jnp.where(h, high, zero) for h in here], 0))
        left_low.append(jnp.concatenate([jnp.where(h, low, zero) for h in here], 0))
        for i, rows in enumerate(cell_rows):
            hot_ref[2 * SUB * i : 2 * SUB * (i + 1), e * LANES : (e + 1) * LANES] = jnp.where(
                own_cell == rows, one, zero
            )
    left = jnp.concatenate(
        [jnp.concatenate(left_high, 1), jnp.concatenate(left_low, 1)], 0
    )
    spread = dot(left, hot_ref[...], NT)
    size = GROUPS * SUB
    spread = spread[:size] + spread[size:]
    for half in range(2):
        planes[half * size : (half + 1) * size, :] = spread[:, half * LANES : (half + 1) * LANES]

    def plane_part(part, p):
        return planes[pl.ds(part * layers + p, KROWS, stride=SUB), :]

    grid = jnp.concatenate(
        [
            jnp.concatenate([plane_part(part, p) for p in range(layers)], 0)
            for part in range(2)
        ],
        1,
    )
    copies[0].wait()
    grid = dot3(split(grid), (fb[0], fb[1]))
    grid = jnp.concatenate(
        [
            jnp.concatenate(
                [
                    grid[p * KROWS : (p + 1) * KROWS, q * LANES : (q + 1) * LANES]
                    for q in range(4)
                ],
                0,
            )
            for p in range(layers)
        ],
        1,
    )
    copies[1].wait()
    grid = dot3((fa[0], fa[1]), split(grid))
    potential = jnp.concatenate(
        [
            jnp.concatenate(
                [
                    recv_row(sz.out_rows + al * layers + p)
                    for al in range(layers)
                ],
                0,
            )
            for p in range(layers)
        ],
        1,
    )
    half = sz.extent
    field = jnp.concatenate([grid[0:half] * potential, grid[half:] * potential], 0)
    copies[2].wait()
    grid = dot3((ia[0], ia[1]), split(field))
    grid = jnp.concatenate(
        [
            jnp.concatenate(
                [
                    grid[q * KROWS : (q + 1) * KROWS, p * LANES : (p + 1) * LANES]
                    for q in range(4)
                ],
                1,
            )
            for p in range(layers)
        ],
        0,
    )
    copies[3].wait()
    grid = dot3(split(grid), (ib[0], ib[1]))
    for part in range(2):
        for p in range(layers):
            back[pl.ds(part * layers + p, KROWS, stride=SUB), :] = grid[
                p * KROWS : (p + 1) * KROWS, part * LANES : (part + 1) * LANES
            ]

    values = jnp.concatenate([back[:size, :], back[size:, :]], 1)
    values = jnp.concatenate(split(values), 0)
    for pair in range(0, devices, 2):
        both = dot(values, hot_ref[:, pair * LANES : (pair + 2) * LANES])
        both = both[:size] + both[size:]
        for e in (pair, pair + 1):
            found = both[:, (e - pair) * LANES : (e - pair + 1) * LANES]
            own = jnp.broadcast_to(group_ref[e : e + 1, :], (SUB, LANES))
            total = jnp.zeros((SUB, LANES), F32)
            for g in range(GROUPS):
                total = total + jnp.where(own == g, found[g * SUB : (g + 1) * SUB, :], 0.0)
            z_ref[e * SUB : (e + 1) * SUB, :] = total

    def back_item(i):
        return z_ref[pl.ds(i, devices, stride=SUB), :]

    for r in range(sz.back_rows):
        out_ref[pl.ds(r, devices, stride=sz.back_rows), :] = pack_row(
            r, back_item, sz.back_pieces
        )
    bands.wait()


def final_kernel(sz, back_ref, window_ref, table_ref, depth_ref, hot_ref, kinetic_ref,
                 early_ref, middle_ref,
                 orbitals_ref,
                 applied_out, tile_ref,
                 applied_ref, factors, late_ref, acc, sums_ref, band_sems, out_sem):
    done = EARLY + MIDDLE
    bands = BandLoads(orbitals_ref, late_ref, band_sems, done, sz.bands_all - done)
    bands.start()
    devices, layers, rows = sz.devices, sz.layers, sz.slot_rows
    square = (LANES, LANES)

    def back_row(r):
        return back_ref[pl.ds(r, devices, stride=sz.back_rows), :]

    values = jnp.concatenate(
        [
            unpack_item(i, sz.back_rows, back_row, sz.back_pieces)
            for i in range(sz.channels)
        ],
        0,
    )
    values = jnp.transpose(values)
    sticks = dot3(split(values), (table_ref[0], table_ref[1]))
    placed = []
    for turn in range(2):
        depth = depth_ref[turn]
        held = depth >= 0
        depth = depth & (sz.extent - 1)
        placed.append(
            jnp.concatenate(
                [
                    jnp.where(held, pick(sticks[:, q * LANES : (q + 1) * LANES], depth), 0.0)
                    for q in range(2)
                ],
                1,
            )
        )
    placed = split(jnp.concatenate(placed, 0))
    hot = hot_ref[...]
    local = dot(hot, placed[0]) + dot(hot, placed[1])
    kinetic = kinetic_ref[...]
    for part in range(2):
        own = window_ref[part * rows : (part + 1) * rows, :]
        full = kinetic * own + local[:, part * LANES : (part + 1) * LANES]
        applied_ref[part * rows : (part + 1) * rows, :] = jnp.where(kinetic >= 0.0, full, 0.0)
    store = pltpu.make_async_copy(applied_ref, applied_out, out_sem)
    store.start()
    a_re = applied_ref[0:rows, :]
    a_im = applied_ref[rows : 2 * rows, :]
    factors[0] = a_im
    factors[1] = a_re - a_im
    factors[2] = a_re + a_im

    blocks = sz.bands_all // LANES
    block_row = iota((blocks, LANES), 0)
    sums_ref[...] = jnp.zeros(sums_ref.shape, F32)

    def product_of(source, first, wait=None):
        def product(i, carry):
            if wait is not None:
                wait(i)
            start = pl.multiple_of(i * CHUNK, CHUNK)
            sums = [jnp.zeros((CHUNK, LANES), F32) for _ in range(3)]
            for r in range(rows):
                x = source[0, pl.ds(start, CHUNK), r * LANES : (r + 1) * LANES]
                y = source[1, pl.ds(start, CHUNK), r * LANES : (r + 1) * LANES]
                for q, value in enumerate((x + y, x, y)):
                    sums[q] = sums[q] + value * factors[q, r : r + 1, :]
            end = first + (i + 1) * CHUNK
            at = pl.multiple_of((end - CHUNK) % LANES, CHUNK)
            acc[0, pl.ds(at, CHUNK), :] = sums[0] + sums[1]
            acc[1, pl.ds(at, CHUNK), :] = sums[0] - sums[2]

            @pl.when(end % LANES == 0)
            def _():
                hot_row = ones_where(block_row == end // LANES - 1).astype(BF16)
                for part in range(2):
                    high, low = split(acc[part])
                    sums_ref[part] += dot(hot_row, high, NT) + dot(hot_row, low, NT)

            return carry

        lax.fori_loop(0, source.shape[1] // CHUNK, product, 0)

    product_of(early_ref, 0)
    product_of(middle_ref, EARLY)
    product_of(late_ref, done, bands.wait_one)
    sums = [sums_ref[part] * (1.0 / (sz.slots * sz.devices)) for part in range(2)]
    width = sz.band_rows
    per_row = LANES // width
    lane = iota((blocks, LANES), 1)
    for q in range(per_row):
        real = pltpu.roll(sums[0], (-q * width) % LANES, 1)
        imag = pltpu.roll(sums[1], (width - q * width) % LANES, 1)
        tile_ref[pl.ds(q, blocks, stride=per_row), :] = jnp.where(lane < width, real, imag)
    store.wait()


def sum_kernel(sz, tile_ref, out_ref):
    width = sz.band_rows
    total = jnp.sum(tile_ref[...], axis=0, keepdims=True)
    for part in range(2):
        out_ref[part, :, :] = total[:, part * width : (part + 1) * width]


def full_spec():
    return pl.BlockSpec(memory_space=pltpu.VMEM)


def any_spec():
    return pl.BlockSpec(memory_space=pl.ANY)


def vmem(mib):
    return pltpu.CompilerParams(vmem_limit_bytes=mib << 20)


def run_spread(sz, cells, orbitals, potential, table, **kw):
    return pl.pallas_call(
        lambda *refs: spread_kernel(sz, *refs),
        out_shape=(
            jax.ShapeDtypeStruct((sz.devices * sz.rows, LANES), F32),
            jax.ShapeDtypeStruct((2 * sz.slot_rows, LANES), F32),
            jax.ShapeDtypeStruct((2, LANES, LANES), I32),
            jax.ShapeDtypeStruct((sz.slot_rows, 2 * LANES), BF16),
            jax.ShapeDtypeStruct((sz.slot_rows, LANES), F32),
            pltpu.VMEM((2, EARLY, sz.slots), F32),
        ),
        in_specs=[any_spec()] * 4,
        out_specs=(full_spec(),) * 6,
        scratch_shapes=[
            pltpu.VMEM((sz.slot_rows, LANES), I32),
            pltpu.VMEM((2, SUB, sz.slots), F32),
            pltpu.VMEM((sz.layers, LANES, LANES), F32),
            pltpu.VMEM(table.shape, BF16),
            pltpu.VMEM((LANES, LANES), F32),
            pltpu.VMEM((sz.devices * sz.channels, LANES), F32),
            pltpu.SemaphoreType.DMA((4,)),
            pltpu.SemaphoreType.DMA((EARLY // CHUNK,)),
        ],
        name="spread",
        compiler_params=vmem(8),
        **kw,
    )(cells, orbitals, potential, table)


def run_planes(sz, recv, tabs, orbitals, **kw):
    mats = [tabs[n] for n in ("forward_b", "forward_a", "inverse_a", "inverse_b")]
    return pl.pallas_call(
        lambda *refs: plane_kernel(sz, *refs),
        out_shape=(
            jax.ShapeDtypeStruct((sz.devices * sz.back_rows, LANES), F32),
            pltpu.VMEM((2, MIDDLE, sz.slots), F32),
        ),
        in_specs=[full_spec()] + [any_spec()] * 5,
        out_specs=(full_spec(), full_spec()),
        scratch_shapes=[pltpu.VMEM(m.shape, BF16) for m in mats]
        + [
            pltpu.VMEM((CELLS, sz.devices * LANES), BF16),
            pltpu.VMEM((KROWS * SUB, LANES), F32),
            pltpu.VMEM((KROWS * SUB, LANES), F32),
            pltpu.VMEM((sz.devices, LANES), I32),
            pltpu.VMEM((sz.devices * SUB, LANES), F32),
            pltpu.SemaphoreType.DMA((4,)),
            pltpu.SemaphoreType.DMA((MIDDLE // CHUNK,)),
        ],
        name="planes",
        compiler_params=vmem(16),
        **kw,
    )(recv, *mats, orbitals)


def run_final(sz, back, window, table, depth, hot, kinetic, early, middle, orbitals, **kw):
    late = sz.bands_all - EARLY - MIDDLE
    return pl.pallas_call(
        lambda *refs: final_kernel(sz, *refs),
        out_shape=(
            jax.ShapeDtypeStruct((2 * sz.slot_rows, LANES), F32),
            jax.ShapeDtypeStruct((sz.devices, LANES), F32),
        ),
        in_specs=[full_spec()] * 8 + [any_spec()],
        out_specs=(any_spec(), full_spec()),
        scratch_shapes=[
            pltpu.VMEM((2 * sz.slot_rows, LANES), F32),
            pltpu.VMEM((3, sz.slot_rows, LANES), F32),
            pltpu.VMEM((2, late, sz.slots), F32),
            pltpu.VMEM((2, LANES, LANES), F32),
            pltpu.VMEM((2, sz.bands_all // LANES, LANES), F32),
            pltpu.SemaphoreType.DMA((late // CHUNK,)),
            pltpu.SemaphoreType.DMA,
        ],
        name="final",
        compiler_params=vmem(20),
        **kw,
    )(back, window, table, depth, hot, kinetic, early, middle, orbitals)


def run_sum(sz, tile, **kw):
    return pl.pallas_call(
        lambda *refs: sum_kernel(sz, *refs),
        out_shape=jax.ShapeDtypeStruct((2, 1, sz.band_rows), F32),
        in_specs=[full_spec()],
        out_specs=full_spec(),
        name="add",
        compiler_params=vmem(2),
        **kw,
    )(tile)


def exchange(x):
    rows = x.reshape(x.shape[0], 1, x.shape[1])
    return lax.all_to_all(rows, "ga", split_axis=0, concat_axis=0, tiled=True).reshape(x.shape)


def local(orbitals, coeff_cells, potential):
    devices = lax.axis_size("ga")
    sz = Sizes(devices, potential.shape[1], coeff_cells.shape[0], orbitals.shape[1])
    tabs = {name: jnp.asarray(value) for name, value in tables(sz).items()}
    cells = coeff_cells.reshape(sz.slot_rows, LANES)
    stay = lambda x: pltpu.with_memory_space_constraint(x, pltpu.HBM)
    orbitals = stay(orbitals)
    send, window, depth, hot, kinetic, early = run_spread(
        sz, stay(cells), orbitals, stay(potential), stay(tabs["forward_z"])
    )
    back, middle = run_planes(sz, exchange(send), tabs, orbitals)
    applied, tile = run_final(
        sz, exchange(back), window, tabs["inverse_z"], depth, hot, kinetic, early, middle, orbitals
    )
    subspace = run_sum(sz, exchange(tile))
    return (
        applied.reshape(2, 1, sz.slots),
        jnp.transpose(subspace, (2, 0, 1)),
    )


def solution(mesh):
    in_specs = (P(None, "kpt", "ga"), P("ga"), P("ga", None, None))
    out_specs = (P(None, "kpt", "ga"), P("ga", None, "kpt"))
    return jax.shard_map(local, mesh=mesh, in_specs=in_specs, out_specs=out_specs, check_vma=False)
```
